32 devices in a mesh: xi: 8 (over z, core), eta: 4 (over y, x).
Axes of the slice: x: 2, y: 2, z: 4, core: 2. Of those that a mesh axis runs over, the one named last changes fastest.
Arguments:
- mantle_disp: float32 [3, 36, 2160], P(None, 'eta', 'xi'), may hold values from -6 to 6
- mantle_vel: float32 [3, 36, 2160], P(None, 'eta', 'xi'), may hold values from -6 to 6
- mantle_acc: float32 [3, 36, 2160], P(None, 'eta', 'xi'), may hold values from -12 to 12
- mantle_metric: float32 [3, 36, 2160], P(None, 'eta', 'xi'), may hold values from 0.7 to 1.4
- mantle_moduli: float32 [2, 36, 2160], P(None, 'eta', 'xi'), may hold values from 0.02 to 0.2
- mantle_rho: float32 [36, 2160], P('eta', 'xi'), may hold values from 0.5 to 2
- core_pot: float32 [36, 2160], P('eta', 'xi'), may hold values from -6 to 6
- core_rate: float32 [36, 2160], P('eta', 'xi'), may hold values from -6 to 6
- core_accel: float32 [36, 2160], P('eta', 'xi'), may hold values from -12 to 12
- core_metric: float32 [3, 36, 2160], P(None, 'eta', 'xi'), may hold values from 0.7 to 1.4
- core_kappa: float32 [36, 2160], P('eta', 'xi'), may hold values from 0.02 to 0.2
- core_rho: float32 [36, 2160], P('eta', 'xi'), may hold values from 0.5 to 2
- inner_disp: float32 [3, 36, 1200], P(None, 'eta', 'xi'), may hold values from -6 to 6
- inner_vel: float32 [3, 36, 1200], P(None, 'eta', 'xi'), may hold values from -6 to 6
- inner_acc: float32 [3, 36, 1200], P(None, 'eta', 'xi'), may hold values from -12 to 12
- inner_metric: float32 [3, 36, 1200], P(None, 'eta', 'xi'), may hold values from 0.7 to 1.4
- inner_moduli: float32 [2, 36, 1200], P(None, 'eta', 'xi'), may hold values from 0.02 to 0.2
- inner_rho: float32 [36, 1200], P('eta', 'xi'), may hold values from 0.5 to 2
Outputs:
- mantle_disp_new: float32 [3, 36, 2160], P(None, 'eta', 'xi')
- mantle_vel_new: float32 [3, 36, 2160], P(None, 'eta', 'xi')
- mantle_acc_new: float32 [3, 36, 2160], P(None, 'eta', 'xi')
- core_pot_new: float32 [36, 2160], P('eta', 'xi')
- core_rate_new: float32 [36, 2160], P('eta', 'xi')
- core_accel_new: float32 [36, 2160], P('eta', 'xi')
- inner_disp_new: float32 [3, 36, 1200], P(None, 'eta', 'xi')
- inner_vel_new: float32 [3, 36, 1200], P(None, 'eta', 'xi')
- inner_acc_new: float32 [3, 36, 1200], P(None, 'eta', 'xi')
The draws below stay inside these ranges and needn't reach their ends.
All inputs are finite; a program needn't handle non-finite values.
Results may differ from the reference program's by a relative error of at most 0.0001.
Values sent between devices are 32-bit elements; how exact they have to be, the bound alone decides.
No kernel may reach another device: no remote copies, remote signals or barrier semaphores. Data moves between devices by JAX's collectives and lax.ppermute only.
A program may use at most 64 MiB of HBM per device.

```python
import math
import jax
import jax.numpy as jnp
import numpy as np
from jax import lax

EX = 1
EY = 2
PX = 5
PY = 9
SIDE = 32
MANTLE_LAYERS = 2
CORE_LAYERS = 2
INNER_LAYERS = 1
RM = 9
RC = 9
RI = 5
YP = 36
XM = 2160
XC = 2160
XN = 1200
N_XI = 8
N_ETA = 4


def level_of(key, shape, shards, least, high):
    loudness, own = 1.0, jax.random.fold_in(key, 6)
    for axis_at, shards_of in shards:
        steps = jnp.exp(jax.random.uniform(jax.random.fold_in(own, axis_at), (shards_of,), jnp.float32, least / len(shards), high / len(shards)))
        loudness = loudness * jnp.repeat(steps, shape[axis_at] // shards_of).reshape([-1 if axis == axis_at else 1 for axis in range(len(shape))])
    return loudness


def noise(own_key, dims, scale, bound, cuts=(), kind=jnp.bfloat16):
    level = level_of(own_key, dims, cuts, -0.22, 0.18) if cuts else 1.0
    values = jax.random.normal(own_key, dims, jnp.float32) * scale * level
    return jnp.minimum(jnp.maximum(values, -bound), bound).astype(kind)


def setup_inputs(seed: int = 0) -> dict:
    key_list = jax.random.split(jax.random.key(seed), 19)
    return {
        "mantle_disp": noise(key_list[0], (3, YP, XM), 1.0, 6.0, ((1, 4), (2, 8)), jnp.float32),
        "mantle_vel": noise(key_list[1], (3, YP, XM), 1.0, 6.0, ((1, 4), (2, 8)), jnp.float32),
        "mantle_acc": noise(key_list[2], (3, YP, XM), 2.0, 12.0, ((1, 4), (2, 8)), jnp.float32),
        "mantle_metric": jnp.clip(jnp.exp(math.log(1.4) - 0.6931472 * jax.random.uniform(key_list[3], (3, YP, XM), jnp.float32) ** level_of(key_list[3], (3, YP, XM), ((1, 4), (2, 8)), -0.2, 0.2)), 0.7, 1.4),
        "mantle_moduli": jnp.clip(jnp.exp(math.log(0.2) - 2.3025851 * jax.random.uniform(key_list[4], (2, YP, XM), jnp.float32) ** level_of(key_list[4], (2, YP, XM), ((1, 4), (2, 8)), -0.2, 0.2)), 0.02, 0.2),
        "mantle_rho": jnp.clip(jnp.exp(math.log(2.0) - 1.3862944 * jax.random.uniform(key_list[5], (YP, XM), jnp.float32) ** level_of(key_list[5], (YP, XM), ((0, 4), (1, 8)), -0.2, 0.2)), 0.5, 2.0),
        "core_pot": noise(key_list[6], (YP, XC), 1.0, 6.0, ((0, 4), (1, 8)), jnp.float32),
        "core_rate": noise(key_list[7], (YP, XC), 1.0, 6.0, ((0, 4), (1, 8)), jnp.float32),
        "core_accel": noise(key_list[8], (YP, XC), 2.0, 12.0, ((0, 4), (1, 8)), jnp.float32),
        "core_metric": jnp.clip(jnp.exp(math.log(1.4) - 0.6931472 * jax.random.uniform(key_list[9], (3, YP, XC), jnp.float32) ** level_of(key_list[9], (3, YP, XC), ((1, 4), (2, 8)), -0.2, 0.2)), 0.7, 1.4),
        "core_kappa": jnp.clip(jnp.exp(math.log(0.2) - 2.3025851 * jax.random.uniform(key_list[10], (YP, XC), jnp.float32) ** level_of(key_list[10], (YP, XC), ((0, 4), (1, 8)), -0.2, 0.2)), 0.02, 0.2),
        "core_rho": jnp.clip(jnp.exp(math.log(2.0) - 1.3862944 * jax.random.uniform(key_list[11], (YP, XC), jnp.float32) ** level_of(key_list[11], (YP, XC), ((0, 4), (1, 8)), -0.2, 0.2)), 0.5, 2.0),
        "inner_disp": noise(key_list[12], (3, YP, XN), 1.0, 6.0, ((1, 4), (2, 8)), jnp.float32),
        "inner_vel": noise(key_list[13], (3, YP, XN), 1.0, 6.0, ((1, 4), (2, 8)), jnp.float32),
        "inner_acc": noise(key_list[14], (3, YP, XN), 2.0, 12.0, ((1, 4), (2, 8)), jnp.float32),
        "inner_metric": jnp.clip(jnp.exp(math.log(1.4) - 0.6931472 * jax.random.uniform(key_list[15], (3, YP, XN), jnp.float32) ** level_of(key_list[15], (3, YP, XN), ((1, 4), (2, 8)), -0.2, 0.2)), 0.7, 1.4),
        "inner_moduli": jnp.clip(jnp.exp(math.log(0.2) - 2.3025851 * jax.random.uniform(key_list[16], (2, YP, XN), jnp.float32) ** level_of(key_list[16], (2, YP, XN), ((1, 4), (2, 8)), -0.2, 0.2)), 0.02, 0.2),
        "inner_rho": jnp.clip(jnp.exp(math.log(2.0) - 1.3862944 * jax.random.uniform(key_list[17], (YP, XN), jnp.float32) ** level_of(key_list[17], (YP, XN), ((0, 4), (1, 8)), -0.2, 0.2)), 0.5, 2.0),
    }


time_step = 0.1
highest = lax.Precision.HIGHEST

def gll_tables():
    radical = math.sqrt(3.0 / 7.0)
    points = np.array([-1.0, -radical, 0.0, radical, 1.0])
    weights = np.array([0.1, 49.0 / 90.0, 32.0 / 45.0, 49.0 / 90.0, 0.1])
    products = np.array([np.prod([points[first_node] - points[other_node] for other_node in range(5) if other_node != first_node]) for first_node in range(5)])
    slopes = np.zeros((5, 5))
    for first_node in range(5):
        for second_node in range(5):
            if first_node == second_node:
                slopes[first_node, second_node] = np.sum([1.0 / (points[first_node] - points[other_node]) for other_node in range(5) if other_node != first_node])
            else:
                slopes[first_node, second_node] = products[first_node] / (products[second_node] * (points[first_node] - points[second_node]))
    return (weights, slopes)

def element_maps(element_count):
    weights, slopes = gll_tables()
    spread = np.zeros((4 * element_count + 1, 5 * element_count))
    for element in range(element_count):
        for node_index in range(5):
            spread[4 * element + node_index, 5 * element + node_index] = 1.0
    derive = np.kron(np.eye(element_count), slopes.T)
    element_weights = np.tile(weights, element_count)
    lumped = spread @ element_weights
    return (jnp.asarray(spread, jnp.float32), jnp.asarray(derive, jnp.float32), jnp.asarray(element_weights, jnp.float32), jnp.asarray(lumped, jnp.float32))

def expand(grid_values, tables):
    return jnp.einsum('...yixkr,ya,xb,rd->...aibkd', grid_values, tables[0][0], tables[1][0], tables[2][0], precision=highest)

def contract(node_values, tables):
    return jnp.einsum('...aibkd,ya,xb,rd->...yixkr', node_values, tables[0][0], tables[1][0], tables[2][0], precision=highest)

def slopes_of(node_values, tables):
    along_y = jnp.einsum('...aibkd,ae->...eibkd', node_values, tables[0][1], precision=highest)
    along_x = jnp.einsum('...aibkd,be->...aiekd', node_values, tables[1][1], precision=highest)
    along_r = jnp.einsum('...aibkd,de->...aibke', node_values, tables[2][1], precision=highest)
    return (along_y, along_x, along_r)

def adjoint_sum(flux_y, flux_x, flux_r, tables):
    summed = jnp.einsum('...eibkd,ae->...aibkd', flux_y, tables[0][1], precision=highest)
    summed = summed + jnp.einsum('...aiekd,be->...aibkd', flux_x, tables[1][1], precision=highest)
    summed = summed + jnp.einsum('...aibke,de->...aibkd', flux_r, tables[2][1], precision=highest)
    return summed

def node_volume(tables):
    return tables[0][2][:, None, None, None, None] * tables[1][2][None, None, :, None, None] * tables[2][2][None, None, None, None, :]

def lumped_volume(metric, tables):
    weight_grid = tables[0][3][:, None, None, None, None] * tables[1][3][None, None, :, None, None] * tables[2][3][None, None, None, None, :]
    return weight_grid / (metric[0] * metric[1] * metric[2])

def elastic_force(displace, metric, moduli, tables):
    node_values = expand(displace, tables)
    inverse_scale = expand(metric, tables)
    lame_nodes = expand(moduli, tables)
    slope_y, slope_x, slope_r = slopes_of(node_values, tables)
    physical = jnp.stack([slope_y * inverse_scale[0], slope_x * inverse_scale[1], slope_r * inverse_scale[2]], axis=1)
    dilation = physical[0, 0] + physical[1, 1] + physical[2, 2]
    strain = 0.5 * (physical + jnp.swapaxes(physical, 0, 1))
    identity = jnp.eye(3, dtype=node_values.dtype).reshape(3, 3, 1, 1, 1, 1, 1)
    stress = 2.0 * lame_nodes[1] * strain + lame_nodes[0] * dilation * identity
    volume = node_volume(tables) / (inverse_scale[0] * inverse_scale[1] * inverse_scale[2])
    fluxes = stress * (volume * inverse_scale)[None]
    summed = adjoint_sum(fluxes[:, 0], fluxes[:, 1], fluxes[:, 2], tables)
    return -contract(summed, tables)

def fluid_force(potential, metric, density, tables):
    node_values = expand(potential, tables)
    inverse_scale = expand(metric, tables)
    density_nodes = expand(density, tables)
    slope_y, slope_x, slope_r = slopes_of(node_values, tables)
    volume = node_volume(tables) / (inverse_scale[0] * inverse_scale[1] * inverse_scale[2] * density_nodes)
    summed = adjoint_sum(volume * inverse_scale[0] * inverse_scale[0] * slope_y, volume * inverse_scale[1] * inverse_scale[1] * slope_x, volume * inverse_scale[2] * inverse_scale[2] * slope_r, tables)
    return -contract(summed, tables)

def by_group(group_index, options):
    return jnp.where(group_index == 0, options[0], jnp.where(group_index == 1, options[1], jnp.where(group_index == 2, options[2], options[3])))

def canonical_ids():
    grid_shape = (N_ETA, PY, N_XI, PX, 6)
    surface_y = lax.broadcasted_iota(jnp.int32, grid_shape, 0) * (PY - 1) + lax.broadcasted_iota(jnp.int32, grid_shape, 1)
    surface_x = lax.broadcasted_iota(jnp.int32, grid_shape, 2) * (PX - 1) + lax.broadcasted_iota(jnp.int32, grid_shape, 3)
    group_index = lax.broadcasted_iota(jnp.int32, grid_shape, 4)
    wrapped = (group_index < 4) & (surface_x == SIDE)
    group_index = jnp.where(wrapped, (group_index + 1) % 4, group_index)
    surface_x = jnp.where(wrapped, 0, surface_x)
    equator = group_index < 4
    northern = equator & (surface_y == SIDE)
    southern = equator & (surface_y == 0)
    polar_x = by_group(group_index, (surface_x, SIDE, SIDE - surface_x, 0))
    north_y = by_group(group_index, (0, surface_x, SIDE, SIDE - surface_x))
    south_y = by_group(group_index, (SIDE, SIDE - surface_x, 0, surface_x))
    final_x = jnp.where(northern | southern, polar_x, surface_x)
    final_y = jnp.where(northern, north_y, jnp.where(southern, south_y, surface_y))
    final_group = jnp.where(northern, 4, jnp.where(southern, 5, group_index))
    return ((final_group * (SIDE + 1) + final_y) * (SIDE + 1) + final_x).astype(jnp.int32)

def assemble(stacked, point_ids):
    channels = stacked.shape[0]
    radial = stacked.shape[-1]
    flattened = jnp.moveaxis(stacked, 0, -2).reshape(-1, channels * radial)
    summed = jax.ops.segment_sum(flattened, point_ids.reshape(-1), num_segments=6 * (SIDE + 1) * (SIDE + 1))
    returned = summed[point_ids.reshape(-1)].reshape(point_ids.shape + (channels, radial))
    return jnp.moveaxis(returned, -2, 0)

def by_rows(function, arrays):
    reordered = tuple((jnp.moveaxis(member, -6, 0) for member in arrays))
    result = lax.map(lambda pieces: function(*pieces), reordered)
    return jnp.moveaxis(result, 0, -6)

def reference(mantle_disp, mantle_vel, mantle_acc, mantle_metric, mantle_moduli, mantle_rho, core_pot, core_rate, core_accel, core_metric, core_kappa, core_rho, inner_disp, inner_vel, inner_acc, inner_metric, inner_moduli, inner_rho):
    lateral = (element_maps(EY), element_maps(EX))
    mantle_maps = lateral + (element_maps(MANTLE_LAYERS),)
    core_maps = lateral + (element_maps(CORE_LAYERS),)
    inner_maps = lateral + (element_maps(INNER_LAYERS),)

    def blocked(grid_values, radial):
        return grid_values.reshape(grid_values.shape[:-2] + (N_ETA, PY, N_XI, PX, 6, radial))
    half_square = 0.5 * time_step * time_step
    mantle_next = mantle_disp + time_step * mantle_vel + half_square * mantle_acc
    core_next = core_pot + time_step * core_rate + half_square * core_accel
    inner_next = inner_disp + time_step * inner_vel + half_square * inner_acc
    mantle_shape = blocked(mantle_next, RM)
    core_shape = blocked(core_next, RC)
    inner_shape = blocked(inner_next, RI)
    mantle_geometry = blocked(mantle_metric, RM)
    core_geometry = blocked(core_metric, RC)
    inner_geometry = blocked(inner_metric, RI)
    mantle_force = by_rows(lambda displace, metric, moduli: elastic_force(displace, metric, moduli, mantle_maps), (mantle_shape, mantle_geometry, blocked(mantle_moduli, RM)))
    inner_force = by_rows(lambda displace, metric, moduli: elastic_force(displace, metric, moduli, inner_maps), (inner_shape, inner_geometry, blocked(inner_moduli, RI)))
    core_force = by_rows(lambda potential, metric, density: fluid_force(potential, metric, density, core_maps), (core_shape, core_geometry, blocked(core_rho, RC)))
    mantle_mass = blocked(mantle_rho, RM) * lumped_volume(mantle_geometry, mantle_maps)
    inner_mass = blocked(inner_rho, RI) * lumped_volume(inner_geometry, inner_maps)
    core_mass = lumped_volume(core_geometry, core_maps) / blocked(core_kappa, RC)
    face_lateral = core_maps[0][3][:, None, None, None] * core_maps[1][3][None, None, :, None]
    weight_top = face_lateral / (core_geometry[0][..., -1] * core_geometry[1][..., -1])
    weight_bottom = face_lateral / (core_geometry[0][..., 0] * core_geometry[1][..., 0])
    core_force = core_force.at[..., -1].add(weight_top * mantle_shape[2][..., 0])
    core_force = core_force.at[..., 0].add(-weight_bottom * inner_shape[2][..., -1])
    point_ids = canonical_ids()
    core_sums = assemble(jnp.stack([core_force, core_mass]), point_ids)
    core_acc_next = core_sums[0] / core_sums[1]
    mantle_force = mantle_force.at[2, ..., 0].add(weight_top * core_acc_next[..., -1])
    inner_force = inner_force.at[2, ..., -1].add(-weight_bottom * core_acc_next[..., 0])
    mantle_sums = assemble(jnp.concatenate([mantle_force, mantle_mass[None]]), point_ids)
    inner_sums = assemble(jnp.concatenate([inner_force, inner_mass[None]]), point_ids)
    mantle_acc_next = (mantle_sums[:3] / mantle_sums[3]).reshape(mantle_disp.shape)
    inner_acc_next = (inner_sums[:3] / inner_sums[3]).reshape(inner_disp.shape)
    core_acc_next = core_acc_next.reshape(core_pot.shape)
    half_step = 0.5 * time_step
    mantle_vel_next = mantle_vel + half_step * (mantle_acc + mantle_acc_next)
    core_rate_next = core_rate + half_step * (core_accel + core_acc_next)
    inner_vel_next = inner_vel + half_step * (inner_acc + inner_acc_next)
    return (mantle_next, mantle_vel_next, mantle_acc_next, core_next, core_rate_next, core_acc_next, inner_next, inner_vel_next, inner_acc_next)
```

```python
import collections
import functools
import math

import jax
import jax.numpy as jnp
import numpy as np
from jax import lax
from jax.experimental import pallas as pl
from jax.experimental.pallas import tpu as pltpu
from jax.sharding import PartitionSpec as P

EX = 1
MANTLE_LAYERS = 2
CORE_LAYERS = 2
INNER_LAYERS = 1
GROUPS = 6
ACROSS = 4 * EX + 1
RADIAL = 4 * MANTLE_LAYERS + 1
INNER_RADIAL = 4 * INNER_LAYERS + 1
LINES = ACROSS * GROUPS
WIDTH = LINES * RADIAL
INNER_WIDTH = LINES * INNER_RADIAL
COLUMN = GROUPS * RADIAL
NODES = LINES * 5 * MANTLE_LAYERS
PAD = 384
INNER_PAD = 256
STEP = 12
ENTRIES = 128
SLOTS = 16
CHUNK = 512
time_step = 0.1
highest = lax.Precision.HIGHEST

MM, CF, CM, IF, IM, CW, FIELDS = 3, 4, 5, 6, 9, 10, 11
PAIRS = 6


def gll_tables():
    radical = math.sqrt(3.0 / 7.0)
    points = np.array([-1.0, -radical, 0.0, radical, 1.0])
    weights = np.array([0.1, 49.0 / 90.0, 32.0 / 45.0, 49.0 / 90.0, 0.1])
    products = np.array(
        [np.prod([points[a] - points[c] for c in range(5) if c != a]) for a in range(5)]
    )
    slopes = np.zeros((5, 5))
    for a in range(5):
        for b in range(5):
            if a == b:
                slopes[a, b] = np.sum([1.0 / (points[a] - points[c]) for c in range(5) if c != a])
            else:
                slopes[a, b] = products[a] / (products[b] * (points[a] - points[b]))
    return weights, slopes


def spread_table(count):
    spread = np.zeros((4 * count + 1, 5 * count))
    for element in range(count):
        for node in range(5):
            spread[4 * element + node, 5 * element + node] = 1.0
    return spread


def padded(table, width):
    return np.pad(table, ((0, 0), (0, width - table.shape[1])))


def lane_tables(layers, width):
    weights, slopes = gll_tables()
    spread = spread_table(layers)
    derive = np.kron(np.eye(layers), slopes.T)
    eye_k = np.eye(GROUPS)
    along_x = np.kron(slopes.T, np.kron(eye_k, spread))
    along_r = np.kron(np.eye(ACROSS), np.kron(eye_k, spread @ derive))
    plain = np.kron(np.eye(ACROSS), np.kron(eye_k, spread))
    node = np.kron(weights, np.kron(np.ones(GROUPS), np.tile(weights, layers)))
    lumped_r = spread @ np.tile(weights, layers)
    lumped = np.kron(weights, np.kron(np.ones(GROUPS), lumped_r))
    table = np.concatenate([padded(t, width) for t in (along_x, along_r, plain)], axis=1)
    return table.astype(np.float32), node.astype(np.float32), lumped.astype(np.float32)


def constants(rows_local):
    weights, slopes = gll_tables()
    count_y = (rows_local - 1) // 4
    ypad = -(-rows_local // 8) * 8
    table, node, lumped = lane_tables(MANTLE_LAYERS, PAD)
    inner_table, inner_node, inner_lumped = lane_tables(INNER_LAYERS, INNER_PAD)
    small = np.eye(RADIAL)[:INNER_RADIAL]
    spread = np.kron(np.eye(LINES), small)
    inner_back = inner_table.T @ spread
    lumped_y = spread_table(count_y) @ np.tile(weights, count_y)
    lanes = np.zeros((8, PAD))
    lanes[0, :NODES] = node
    lanes[1, :WIDTH] = lumped
    lanes[2, :WIDTH] = np.kron(weights, np.ones(COLUMN))
    lanes[3, : INNER_WIDTH] = inner_node
    lanes[4, : INNER_WIDTH] = inner_lumped
    columns = np.zeros((ypad, 8))
    columns[:rows_local, 0] = lumped_y
    columns[:5, 1] = weights
    along_y = np.zeros((16, 8))
    along_y[:5, :5] = slopes
    along_y[8:13, :5] = slopes.T
    pick = np.zeros((RADIAL * 32, PAD))
    for r in range(RADIAL):
        for line in range(LINES):
            pick[r * 32 + line, line * RADIAL + r] = 1.0
    polar = np.zeros((PAIRS * 128, 256))
    for f in range(FIELDS):
        for k in (4, 5):
            for r in range(RADIAL):
                polar[(f // 2) * 128 + (f % 2) * 64 + k * RADIAL + r, (k - 4) * 128 + r * STEP + f] = 1.0
    as_f32 = lambda t: np.asarray(t, np.float32)
    return dict(
        table=as_f32(table),
        inner_table=as_f32(inner_table[:, : 2 * INNER_PAD]),
        inner_back=as_f32(inner_back),
        spread=as_f32(padded(spread, PAD)),
        squeeze=as_f32(np.pad(spread.T, ((0, PAD - WIDTH), (0, 0)))),
        lanes=as_f32(lanes),
        columns=as_f32(columns),
        along_y=as_f32(along_y),
        pick=as_f32(pick),
        polar=as_f32(polar),
        polar_back=as_f32(polar.T),
    )


def exchange_tables(count_x, count_y, rows):
    reach_x, reach_y = ACROSS - 1, rows - 1
    side = count_x * reach_x
    ypad = -(-rows // 8) * 8

    def canonical(j, i, y, x, k):
        gy, gx = j * reach_y + y, i * reach_x + x
        if k < 4 and gx == side:
            k, gx = (k + 1) % 4, 0
        if k < 4 and gy == side:
            gx, gy = ((gx, 0), (side, gx), (side - gx, side), (0, side - gx))[k]
            k = 4
        elif k < 4 and gy == 0:
            gx, gy = ((gx, side), (side, side - gx), (side - gx, 0), (0, gx))[k]
            k = 5
        return k, gy, gx

    def swapped(source, target):
        sj, si, sy, sx, sk = source
        j, i, y, x, k = target
        if sj == j and sy == y:
            if (x, sx) == (reach_x, 0):
                if (si, sk) == (i + 1, k):
                    return True
                if i == count_x - 1 and si == 0 and k < 4 and sk == (k + 1) % 4:
                    return True
            if (x, sx) == (0, reach_x):
                if (si, sk) == (i - 1, k):
                    return True
                if i == 0 and si == count_x - 1 and k < 4 and sk == (k - 1) % 4:
                    return True
        if si == i and sx == x:
            if sk == k and (sj, sy, y) in ((j + 1, 0, reach_y), (j - 1, reach_y, 0)):
                return True
            if (j, y, sj, sy) == (0, 0, count_y - 1, reach_y) and (k, sk) in ((4, 0), (0, 5)):
                return True
            if (j, y, sj, sy) == (count_y - 1, reach_y, 0, 0) and (k, sk) in ((0, 4), (5, 0)):
                return True
        return False

    def row_of(y, x, k):
        if y == reach_y:
            return x * GROUPS + k
        if y == 0:
            return 32 + x * GROUPS + k
        return 64 + (k - 4) * 2 * ypad + (ypad if x else 0) + y

    copies = collections.defaultdict(list)
    for j in range(count_y):
        for i in range(count_x):
            for y in range(rows):
                for x in range(ACROSS):
                    if 0 < y < reach_y and 0 < x < reach_x:
                        continue
                    for k in range(GROUPS):
                        copies[canonical(j, i, y, x, k)].append((j, i, y, x, k))
    pairs = collections.defaultdict(list)
    for members in copies.values():
        for target in members:
            for source in members:
                if source != target and not swapped(source, target):
                    key = (source[1] * count_y + source[0], target[1] * count_y + target[0])
                    pairs[key].append((row_of(*source[2:]), row_of(*target[2:])))
    table = np.full((count_x * count_y, 8, ENTRIES), -1.0, np.float32)
    sent = collections.Counter()
    taken = collections.Counter()
    for (source, target), links in sorted(pairs.items()):
        assert len(links) <= SLOTS
        for slot, (row_from, row_to) in enumerate(sorted(links)):
            table[source, 0, sent[source]] = target * SLOTS + slot
            table[source, 1, sent[source]] = row_from
            sent[source] += 1
            table[target, 2, taken[target]] = source * SLOTS + slot
            table[target, 3, taken[target]] = row_to
            taken[target] += 1
    assert max(max(sent.values()), max(taken.values())) <= ENTRIES
    return table


def exact_dot(a, b):
    return jnp.dot(a, b, precision=highest, preferred_element_type=jnp.float32)


def iota(shape, axis):
    return lax.broadcasted_iota(jnp.int32, shape, axis)


def own_table(table_ref, count_y):
    return table_ref[lax.axis_index("xi") * count_y + lax.axis_index("eta")]


def force_kernel(
    rows,
    count_x,
    count_y,
    disp,
    vel,
    acc,
    metric,
    moduli,
    rho,
    pot,
    rate,
    accel,
    core_metric,
    kappa,
    core_rho,
    inner_disp,
    inner_vel,
    inner_acc,
    inner_metric,
    inner_moduli,
    inner_rho,
    table_ref,
    forward,
    inner_forward,
    inner_back,
    spread,
    lanes,
    columns,
    along_y,
    pick,
    polar,
    disp_next,
    pot_next,
    inner_next,
    fields,
    send_xa,
    send_xb,
    send_ya,
    send_yb,
    send_all,
    wide,
    narrow,
    inner_rows,
    flux,
    inner_flux,
    wide_u,
    edges,
    rows_t,
    points,
):
    ne = (rows - 1) // 4
    ypad = edges.shape[0] // 2
    half = 0.5 * time_step * time_step
    for c in range(3):
        disp_next[c] = disp[c] + time_step * vel[c] + half * acc[c]
        inner_next[c] = inner_disp[c] + time_step * inner_vel[c] + half * inner_acc[c]
    pot_next[...] = pot[...] + time_step * rate[...] + half * accel[...]

    slope = along_y[0:5, 0:5]
    slope_back = along_y[8:13, 0:5]

    def along(matrix, block):
        total = matrix[:, 0:1] * block[0:1, :]
        for b in range(1, 5):
            total = total + matrix[:, b : b + 1] * block[b : b + 1, :]
        return total

    wide[...] = jnp.zeros(wide.shape, jnp.float32)
    narrow[...] = jnp.zeros(narrow.shape, jnp.float32)
    inner_rows[...] = jnp.zeros(inner_rows.shape, jnp.float32)
    fields[...] = jnp.zeros(fields.shape, jnp.float32)

    def slot(f, e):
        return (f * ne + e) * 8

    sources = [disp_next.at[0], disp_next.at[1], disp_next.at[2], pot_next]
    extras = [metric.at[0], metric.at[1], metric.at[2], moduli.at[0], moduli.at[1]]
    extras += [core_metric.at[0], core_metric.at[1], core_metric.at[2], core_rho]
    for e in range(ne):
        for f, ref in enumerate(sources):
            block = ref[4 * e : 4 * e + 5, :]
            wide[slot(f, e) : slot(f, e) + 5, :] = block
            narrow[slot(f, e) : slot(f, e) + 5, :] = along(slope, block)
        for f, ref in enumerate(extras):
            narrow[slot(4 + f, e) : slot(4 + f, e) + 5, :] = ref[4 * e : 4 * e + 5, :]
        for f in range(3):
            inner_rows[slot(f, e) : slot(f, e) + 5, :] = inner_next[f, 4 * e : 4 * e + 5, :]
    slopes_xr = exact_dot(wide[...], forward[:, 0 : 2 * PAD])
    copies = exact_dot(narrow[...], forward[:, 2 * PAD : 3 * PAD])
    inner_xr = exact_dot(inner_rows[...], inner_forward[...])

    def elastic(g, lam, mu, sy, sx, sr, jw):
        scaled = [[sy[i] * g[0], sx[i] * g[1], sr[i] * g[2]] for i in range(3)]
        trace = lam * (scaled[0][0] + scaled[1][1] + scaled[2][2])
        out = [[None] * 3 for _ in range(3)]
        weighted = [jw * g[m] for m in range(3)]
        for i in range(3):
            for m in range(3):
                if i == m:
                    stress = 2.0 * mu * scaled[i][i] + trace
                else:
                    stress = mu * (scaled[i][m] + scaled[m][i])
                out[i][m] = stress * weighted[m]
        return out

    row_weight = columns[0:5, 1:2]
    valid = (iota((5, PAD), 1) < NODES) & (iota((5, PAD), 0) < 5)
    for e in range(ne):
        def plain(f):
            return copies[slot(f, e) : slot(f, e) + 5, :]

        def x_of(f):
            return slopes_xr[slot(f, e) : slot(f, e) + 5, 0:PAD]

        def r_of(f):
            return slopes_xr[slot(f, e) : slot(f, e) + 5, PAD : 2 * PAD]

        node = row_weight * lanes[0:1, :]
        g = [jnp.where(valid, plain(4 + m), 1.0) for m in range(3)]
        q = elastic(
            g,
            plain(7),
            plain(8),
            [plain(f) for f in range(3)],
            [x_of(f) for f in range(3)],
            [r_of(f) for f in range(3)],
            node / (g[0] * g[1] * g[2]),
        )
        g = [jnp.where(valid, plain(9 + m), 1.0) for m in range(3)]
        volume = node / (g[0] * g[1] * g[2] * jnp.where(valid, plain(12), 1.0))
        q.append(
            [
                volume * g[0] * g[0] * plain(3),
                volume * g[1] * g[1] * x_of(3),
                volume * g[2] * g[2] * r_of(3),
            ]
        )
        for f in range(4):
            at = slot(f, e)
            flux[at : at + 5, 0:PAD] = q[f][1]
            flux[at : at + 5, PAD : 2 * PAD] = q[f][2]
            flux[at : at + 5, 2 * PAD : 3 * PAD] = along(slope_back, q[f][0])

        def inner_x(f):
            return inner_xr[slot(f, e) : slot(f, e) + 5, 0:INNER_WIDTH]

        def inner_r(f):
            return inner_xr[slot(f, e) : slot(f, e) + 5, INNER_PAD : INNER_PAD + INNER_WIDTH]

        here = slice(4 * e, 4 * e + 5)
        g = [inner_metric[m, here, :] for m in range(3)]
        node = row_weight * lanes[3:4, 0:INNER_WIDTH]
        q = elastic(
            g,
            inner_moduli[0, here, :],
            inner_moduli[1, here, :],
            [along(slope, inner_next[f, here, :]) for f in range(3)],
            [inner_x(f) for f in range(3)],
            [inner_r(f) for f in range(3)],
            node / (g[0] * g[1] * g[2]),
        )
        for f in range(3):
            at = slot(f, e)
            inner_flux[at : at + 5, 0:INNER_WIDTH] = q[f][1]
            inner_flux[at : at + 5, INNER_PAD : INNER_PAD + INNER_WIDTH] = q[f][2]
            inner_flux[at : at + 5, 2 * INNER_PAD : 2 * INNER_PAD + INNER_WIDTH] = along(slope_back, q[f][0])

    back = lax.dot_general(
        flux[...],
        forward[...],
        (((1,), (1,)), ((), ())),
        precision=highest,
        preferred_element_type=jnp.float32,
    )
    inner_forces = exact_dot(inner_flux[...], inner_back[...])
    for e in range(ne):
        here = slice(4 * e, 4 * e + 5)
        for f in range(3):
            fields[f, here, 0:WIDTH] = fields[f, here, 0:WIDTH] - back[slot(f, e) : slot(f, e) + 5, :]
            fields[IF + f, here, 0:WIDTH] = fields[IF + f, here, 0:WIDTH] - inner_forces[slot(f, e) : slot(f, e) + 5, :]
        fields[CF, here, 0:WIDTH] = fields[CF, here, 0:WIDTH] - back[slot(3, e) : slot(3, e) + 5, :]

    lumped_y = columns[0:rows, 0:1]
    lumped = lumped_y * lanes[1:2, 0:WIDTH]
    fields[MM, 0:rows, 0:WIDTH] = rho[...] * (lumped / (metric[0] * metric[1] * metric[2]))
    fields[CM, 0:rows, 0:WIDTH] = lumped / (core_metric[0] * core_metric[1] * core_metric[2]) / kappa[...]
    inner_mass = inner_rho[...] * (
        lumped_y * lanes[4:5, 0:INNER_WIDTH] / (inner_metric[0] * inner_metric[1] * inner_metric[2])
    )
    fields[IM, 0:rows, :] = exact_dot(inner_mass, spread[...])
    radial = lax.rem(iota((rows, WIDTH), 1), RADIAL)
    face = lumped_y * lanes[2:3, 0:WIDTH] / (core_metric[0] * core_metric[1])
    face = jnp.where((radial == 0) | (radial == RADIAL - 1), face, 0.0)
    fields[CW, 0:rows, 0:WIDTH] = face
    wide_u[...] = jnp.zeros(wide_u.shape, jnp.float32)
    wide_u[0:rows, 0:WIDTH] = disp_next[2]
    above = pltpu.roll(wide_u[...], RADIAL - 1, axis=1)
    wide_u[0:rows, :] = exact_dot(inner_next[2], spread[...])
    below = pltpu.roll(wide_u[...], PAD - (INNER_RADIAL - 1), axis=1)
    radial = lax.rem(iota((ypad, PAD), 1), RADIAL)
    jump = jnp.where(radial == RADIAL - 1, above, jnp.where(radial == 0, -below, 0.0))
    fields[CF] = fields[CF] + fields[CW] * jump

    low = iota((ypad, 128), 1) < 64
    for p in range(PAIRS):
        left = fields[2 * p]
        right = fields[2 * p + 1] if 2 * p + 1 < FIELDS else jnp.zeros_like(left)
        edges[0:ypad, p * 128 : p * 128 + 128] = jnp.where(low, left[:, 0:128], pltpu.roll(right[:, 0:128], 64, axis=1))
        edges[ypad : 2 * ypad, p * 128 : p * 128 + 128] = jnp.where(
            low,
            pltpu.roll(left, PAD - (WIDTH - COLUMN), axis=1)[:, 0:128],
            pltpu.roll(right, PAD + 64 - (WIDTH - COLUMN), axis=1)[:, 0:128],
        )
    even_x = lax.rem(lax.axis_index("xi"), 2) == 0
    even_y = lax.rem(lax.axis_index("eta"), 2) == 0
    for p in range(PAIRS):
        first = edges[0:rows, p * 128 : p * 128 + 128]
        last = edges[ypad : ypad + rows, p * 128 : p * 128 + 128]
        send_xa[p * rows : (p + 1) * rows, :] = jnp.where(even_x, last, first)
        send_xb[p * rows : (p + 1) * rows, :] = jnp.where(even_x, first, last)
    rows_t[...] = jnp.zeros(rows_t.shape, jnp.float32)
    for f in range(FIELDS):
        rows_t[f : f + 1, :] = fields[f, rows - 1 : rows, :]
        rows_t[64 + f : 65 + f, :] = fields[f, 0:1, :]
    top = rows_t[0:16, :]
    bottom = rows_t[64:80, :]
    send_ya[...] = jnp.where(even_y, top, bottom)
    send_yb[...] = jnp.where(even_y, bottom, top)

    by_line = lax.dot_general(
        pick[...],
        rows_t[...],
        (((1,), (1,)), ((), ())),
        precision=highest,
        preferred_element_type=jnp.float32,
    )
    lane = iota((32, 128), 1)
    top_points = jnp.zeros((32, 128), jnp.float32)
    bottom_points = jnp.zeros((32, 128), jnp.float32)
    for r in range(RADIAL):
        block = by_line[32 * r : 32 * r + 32, :]
        upper = jnp.where(lane < STEP, block, 0.0)
        lower = jnp.where((lane >= 64) & (lane < 64 + STEP), block, 0.0)
        top_points = top_points + (pltpu.roll(upper, STEP * r, axis=1) if r else upper)
        bottom_points = bottom_points + pltpu.roll(lower, (STEP * r + 64) % 128, axis=1)
    points[0:32, :] = top_points
    points[32:64, :] = bottom_points
    caps = exact_dot(edges[...], polar[...])
    points[64 : 64 + 2 * ypad, :] = caps[:, 0:128]
    points[64 + 2 * ypad : 64 + 4 * ypad, :] = caps[:, 128:256]

    own = own_table(table_ref, count_y)
    turned = jnp.transpose(own)
    count = points.shape[0]
    chosen = jnp.where(turned[:, 1:2] == iota((ENTRIES, count), 1).astype(jnp.float32), 1.0, 0.0)
    chosen = exact_dot(chosen, points[...])
    peers = CHUNK // SLOTS
    for c in range(count_x * count_y // peers):
        number = (iota((CHUNK, ENTRIES), 0) + c * CHUNK).astype(jnp.float32)
        placed = exact_dot(jnp.where(own[0:1, :] == number, 1.0, 0.0), chosen)
        send_all[c * peers : (c + 1) * peers] = placed.reshape(peers, SLOTS, 128)


def close_kernel(
    rows,
    count_x,
    count_y,
    got_xa,
    got_xb,
    got_ya,
    got_yb,
    got_all,
    fields,
    vel,
    acc,
    rate,
    accel,
    inner_vel,
    inner_acc,
    table_ref,
    pick,
    polar_back,
    squeeze,
    vel_next,
    acc_next,
    rate_next,
    accel_next,
    inner_vel_next,
    inner_acc_next,
    total,
    by_line,
    caps,
    narrow,
):
    ypad = total.shape[1]
    own = own_table(table_ref, count_y)
    turned = jnp.transpose(own)
    peers = CHUNK // SLOTS
    arrived = jnp.zeros((ENTRIES, 128), jnp.float32)
    for c in range(count_x * count_y // peers):
        number = (iota((ENTRIES, CHUNK), 1) + c * CHUNK).astype(jnp.float32)
        block = got_all[c * peers : (c + 1) * peers].reshape(CHUNK, 128)
        arrived = arrived + exact_dot(jnp.where(turned[:, 2:3] == number, 1.0, 0.0), block)
    count = 64 + 4 * ypad
    points = exact_dot(
        jnp.where(own[3:4, :] == iota((count, ENTRIES), 0).astype(jnp.float32), 1.0, 0.0), arrived
    )
    lane = iota((32, 128), 1)
    upper = points[0:32]
    lower = points[32:64]
    for r in range(RADIAL):
        first = pltpu.roll(upper, (128 - STEP * r) % 128, axis=1) if r else upper
        second = pltpu.roll(lower, (64 - STEP * r) % 128, axis=1)
        by_line[32 * r : 32 * r + 32, :] = jnp.where(lane < STEP, first, 0.0) + jnp.where(
            (lane >= 64) & (lane < 64 + STEP), second, 0.0
        )
    lines = lax.dot_general(
        by_line[...],
        pick[...],
        (((0,), (0,)), ((), ())),
        precision=highest,
        preferred_element_type=jnp.float32,
    )
    caps[:, 0:128] = points[64 : 64 + 2 * ypad]
    caps[:, 128:256] = points[64 + 2 * ypad : 64 + 4 * ypad]
    columns = exact_dot(caps[...], polar_back[...])

    xi = lax.axis_index("xi")
    eta = lax.axis_index("eta")
    even_x = lax.rem(xi, 2) == 0
    even_y = lax.rem(eta, 2) == 0
    lane = iota((16, PAD), 1)
    group = lax.rem(lane // RADIAL, GROUPS)
    used = lane < WIDTH
    ya = got_ya[...]
    yb = got_yb[...]
    from_above = jnp.where(even_y, ya, yb)
    from_below = jnp.where(even_y, yb, ya)
    four, five = 4 * RADIAL, 5 * RADIAL
    seam_top = jnp.where(
        group == 0,
        pltpu.roll(from_above, PAD - four, axis=1),
        jnp.where(group == 5, pltpu.roll(from_above, five, axis=1), 0.0),
    )
    seam_bottom = jnp.where(
        group == 4,
        pltpu.roll(from_below, four, axis=1),
        jnp.where(group == 0, pltpu.roll(from_below, PAD - five, axis=1), 0.0),
    )
    add_top = jnp.where(eta == count_y - 1, seam_top, from_above) + lines[0:16]
    add_bottom = jnp.where(eta == 0, seam_bottom, from_below) + lines[64:80]
    add_top = jnp.where(used, add_top, 0.0)
    add_bottom = jnp.where(used, add_bottom, 0.0)
    total[...] = fields[...]
    lane = iota((rows, 128), 1)
    inside = lax.rem(lane, 64)
    equator = inside < 4 * RADIAL
    keep = inside < COLUMN
    low = lane < 64
    last_x = xi == count_x - 1
    for p in range(PAIRS):
        xa = got_xa[p * rows : (p + 1) * rows, :]
        xb = got_xb[p * rows : (p + 1) * rows, :]
        from_right = jnp.where(even_x, xa, xb)
        from_left = jnp.where(even_x, xb, xa)
        up = jnp.where(
            inside < 3 * RADIAL,
            pltpu.roll(from_right, 128 - RADIAL, axis=1),
            pltpu.roll(from_right, 3 * RADIAL, axis=1),
        )
        down = jnp.where(
            inside < RADIAL,
            pltpu.roll(from_left, 128 - 3 * RADIAL, axis=1),
            pltpu.roll(from_left, RADIAL, axis=1),
        )
        from_right = jnp.where(last_x, jnp.where(equator, up, 0.0), from_right)
        from_left = jnp.where(xi == 0, jnp.where(equator, down, 0.0), from_left)
        at = slice(p * 128, p * 128 + 128)
        from_left = jnp.where(keep, from_left + columns[0:rows, at], 0.0)
        from_right = jnp.where(keep, from_right + columns[ypad : ypad + rows, at], 0.0)
        zero = jnp.zeros((rows, PAD - 128), jnp.float32)
        for h in range(2):
            f = 2 * p + h
            if f >= FIELDS:
                continue
            mine = low if h == 0 else ~low
            left = jnp.where(mine, from_left, 0.0)
            right = jnp.where(mine, from_right, 0.0)
            if h:
                left = pltpu.roll(left, 64, axis=1)
            total[f, 0:rows, 0:128] = total[f, 0:rows, 0:128] + left
            right = jnp.concatenate([right, zero], axis=1)
            right = pltpu.roll(right, WIDTH - COLUMN - 64 * h, axis=1)
            total[f, 0:rows, :] = total[f, 0:rows, :] + right
    for f in range(FIELDS):
        total[f, rows - 1 : rows, :] = total[f, rows - 1 : rows, :] + add_top[f : f + 1, :]
        total[f, 0:1, :] = total[f, 0:1, :] + add_bottom[f : f + 1, :]

    half = 0.5 * time_step
    lane = iota((ypad, PAD), 1)
    radial = lax.rem(lane, RADIAL)
    inside = (lane < WIDTH) & (iota((ypad, PAD), 0) < rows)
    core = total[CF] / jnp.where(inside, total[CM], 1.0)
    accel_next[...] = core[0:rows, 0:WIDTH]
    rate_next[...] = rate[...] + half * (accel[...] + core[0:rows, 0:WIDTH])
    push = total[CW] * core
    top = jnp.where(radial == 0, pltpu.roll(push, PAD - (RADIAL - 1), axis=1), 0.0)
    bottom = jnp.where(radial == INNER_RADIAL - 1, pltpu.roll(push, INNER_RADIAL - 1, axis=1), 0.0)
    mass = jnp.where(inside, total[MM], 1.0)
    inner_mass = jnp.where(inside & (radial < INNER_RADIAL), total[IM], 1.0)
    for f in range(3):
        force = total[f] + top if f == 2 else total[f]
        result = (force / mass)[0:rows, 0:WIDTH]
        acc_next[f] = result
        vel_next[f] = vel[f] + half * (acc[f] + result)
        force = total[IF + f] - bottom if f == 2 else total[IF + f]
        narrow[f * ypad : (f + 1) * ypad, :] = force / inner_mass
    squeezed = exact_dot(narrow[...], squeeze[...])
    for f in range(3):
        result = squeezed[f * ypad : f * ypad + rows, :]
        inner_acc_next[f] = result
        inner_vel_next[f] = inner_vel[f] + half * (inner_acc[f] + result)


def shards(
    count_x,
    count_y,
    mantle_disp,
    mantle_vel,
    mantle_acc,
    mantle_metric,
    mantle_moduli,
    mantle_rho,
    core_pot,
    core_rate,
    core_accel,
    core_metric,
    core_kappa,
    core_rho,
    inner_disp,
    inner_vel,
    inner_acc,
    inner_metric,
    inner_moduli,
    inner_rho,
):
    rows = mantle_disp.shape[1]
    ne = (rows - 1) // 4
    ypad = -(-rows // 8) * 8
    tables = {name: jnp.asarray(value) for name, value in constants(rows).items()}
    table = jnp.asarray(exchange_tables(count_x, count_y, rows))
    f32 = jnp.float32
    like = lambda a: jax.ShapeDtypeStruct(a.shape, f32)
    shape = lambda *s: jax.ShapeDtypeStruct(s, f32)
    devices = count_x * count_y
    edge = -(-PAIRS * rows // 8) * 8
    (mantle_next, core_next, inner_next, fields, xa, xb, ya, yb, everyone) = pl.pallas_call(
        functools.partial(force_kernel, rows, count_x, count_y),
        out_shape=[
            like(mantle_disp),
            like(core_pot),
            like(inner_disp),
            shape(FIELDS, ypad, PAD),
            shape(edge, 128),
            shape(edge, 128),
            shape(16, PAD),
            shape(16, PAD),
            shape(devices, SLOTS, 128),
        ],
        scratch_shapes=[
            pltpu.VMEM((4 * ne * 8, WIDTH), f32),
            pltpu.VMEM((13 * ne * 8, WIDTH), f32),
            pltpu.VMEM((3 * ne * 8, INNER_WIDTH), f32),
            pltpu.VMEM((4 * ne * 8, 3 * PAD), f32),
            pltpu.VMEM((3 * ne * 8, 3 * INNER_PAD), f32),
            pltpu.VMEM((ypad, PAD), f32),
            pltpu.VMEM((2 * ypad, PAIRS * 128), f32),
            pltpu.VMEM((128, PAD), f32),
            pltpu.VMEM((64 + 4 * ypad, 128), f32),
        ],
        name="forces",
    )(
        mantle_disp,
        mantle_vel,
        mantle_acc,
        mantle_metric,
        mantle_moduli,
        mantle_rho,
        core_pot,
        core_rate,
        core_accel,
        core_metric,
        core_kappa,
        core_rho,
        inner_disp,
        inner_vel,
        inner_acc,
        inner_metric,
        inner_moduli,
        inner_rho,
        table,
        tables["table"],
        tables["inner_table"],
        tables["inner_back"],
        tables["spread"],
        tables["lanes"],
        tables["columns"],
        tables["along_y"],
        tables["pick"],
        tables["polar"],
    )
    everyone = lax.all_to_all(everyone, ("xi", "eta"), 0, 0, tiled=True)
    near = [(i, i ^ 1) for i in range(count_x)]
    far = [(i, (i - 1 if i % 2 == 0 else i + 1) % count_x) for i in range(count_x)]
    xa = lax.ppermute(xa, "xi", near)
    xb = lax.ppermute(xb, "xi", far)
    near = [(j, j ^ 1) for j in range(count_y)]
    far = [(j, (j - 1 if j % 2 == 0 else j + 1) % count_y) for j in range(count_y)]
    ya = lax.ppermute(ya, "eta", near)
    yb = lax.ppermute(yb, "eta", far)
    (mantle_vel_next, mantle_acc_next, core_rate_next, core_acc_next, inner_vel_next, inner_acc_next) = pl.pallas_call(
        functools.partial(close_kernel, rows, count_x, count_y),
        out_shape=[
            like(mantle_vel),
            like(mantle_acc),
            like(core_rate),
            like(core_accel),
            like(inner_vel),
            like(inner_acc),
        ],
        scratch_shapes=[
            pltpu.VMEM((FIELDS, ypad, PAD), f32),
            pltpu.VMEM((RADIAL * 32, 128), f32),
            pltpu.VMEM((2 * ypad, 256), f32),
            pltpu.VMEM((3 * ypad, PAD), f32),
        ],
        name="close",
    )(
        xa,
        xb,
        ya,
        yb,
        everyone,
        fields,
        mantle_vel,
        mantle_acc,
        core_rate,
        core_accel,
        inner_vel,
        inner_acc,
        table,
        tables["pick"],
        tables["polar_back"],
        tables["squeeze"],
    )
    return (
        mantle_next,
        mantle_vel_next,
        mantle_acc_next,
        core_next,
        core_rate_next,
        core_acc_next,
        inner_next,
        inner_vel_next,
        inner_acc_next,
    )


def solution(mesh):
    count_x, count_y = mesh.shape["xi"], mesh.shape["eta"]
    assert count_x % 2 == 0 and count_y % 2 == 0
    assert (count_x * count_y * SLOTS) % CHUNK == 0
    vector, scalar = P(None, "eta", "xi"), P("eta", "xi")
    placed = (vector,) * 5 + (scalar,) * 4 + (vector,) + (scalar,) * 2 + (vector,) * 5 + (scalar,)
    return jax.shard_map(
        functools.partial(shards, count_x, count_y),
        mesh=mesh,
        in_specs=placed,
        out_specs=(vector,) * 3 + (scalar,) * 3 + (vector,) * 3,
        check_vma=False,
    )
```

```python
import collections
import functools
import math

import jax
import jax.numpy as jnp
import numpy as np
from jax import lax
from jax.experimental import pallas as pl
from jax.experimental.pallas import tpu as pltpu
from jax.sharding import PartitionSpec as P

EX = 1
MANTLE_LAYERS = 2
CORE_LAYERS = 2
INNER_LAYERS = 1
GROUPS = 6
ACROSS = 4 * EX + 1
RADIAL = 4 * MANTLE_LAYERS + 1
INNER_RADIAL = 4 * INNER_LAYERS + 1
LINES = ACROSS * GROUPS
WIDTH = LINES * RADIAL
INNER_WIDTH = LINES * INNER_RADIAL
COLUMN = GROUPS * RADIAL
NODES = LINES * 5 * MANTLE_LAYERS
PAD = 384
INNER_PAD = 256
STEP = 12
ENTRIES = 128
SLOTS = 16
CHUNK = 512
time_step = 0.1
highest = lax.Precision.HIGHEST

MM, CF, CM, IF, IM, CW, FIELDS = 3, 4, 5, 6, 9, 10, 11
PAIRS = 6


def gll_tables():
    radical = math.sqrt(3.0 / 7.0)
    points = np.array([-1.0, -radical, 0.0, radical, 1.0])
    weights = np.array([0.1, 49.0 / 90.0, 32.0 / 45.0, 49.0 / 90.0, 0.1])
    products = np.array(
        [np.prod([points[a] - points[c] for c in range(5) if c != a]) for a in range(5)]
    )
    slopes = np.zeros((5, 5))
    for a in range(5):
        for b in range(5):
            if a == b:
                slopes[a, b] = np.sum([1.0 / (points[a] - points[c]) for c in range(5) if c != a])
            else:
                slopes[a, b] = products[a] / (products[b] * (points[a] - points[b]))
    return weights, slopes


def spread_table(count):
    spread = np.zeros((4 * count + 1, 5 * count))
    for element in range(count):
        for node in range(5):
            spread[4 * element + node, 5 * element + node] = 1.0
    return spread


def padded(table, width):
    return np.pad(table, ((0, 0), (0, width - table.shape[1])))


def lane_tables(layers, width):
    weights, slopes = gll_tables()
    spread = spread_table(layers)
    derive = np.kron(np.eye(layers), slopes.T)
    eye_k = np.eye(GROUPS)
    along_x = np.kron(slopes.T, np.kron(eye_k, spread))
    along_r = np.kron(np.eye(ACROSS), np.kron(eye_k, spread @ derive))
    plain = np.kron(np.eye(ACROSS), np.kron(eye_k, spread))
    node = np.kron(weights, np.kron(np.ones(GROUPS), np.tile(weights, layers)))
    lumped_r = spread @ np.tile(weights, layers)
    lumped = np.kron(weights, np.kron(np.ones(GROUPS), lumped_r))
    table = np.concatenate([padded(t, width) for t in (along_x, along_r, plain)], axis=1)
    return table.astype(np.float32), node.astype(np.float32), lumped.astype(np.float32)


def constants(rows_local):
    weights, slopes = gll_tables()
    count_y = (rows_local - 1) // 4
    ypad = -(-rows_local // 8) * 8
    table, node, lumped = lane_tables(MANTLE_LAYERS, PAD)
    inner_table, inner_node, inner_lumped = lane_tables(INNER_LAYERS, INNER_PAD)
    small = np.eye(RADIAL)[:INNER_RADIAL]
    spread = np.kron(np.eye(LINES), small)
    inner_back = inner_table.T @ spread
    lumped_y = spread_table(count_y) @ np.tile(weights, count_y)
    lanes = np.zeros((8, PAD))
    lanes[0, :NODES] = node
    lanes[1, :WIDTH] = lumped
    lanes[2, :WIDTH] = np.kron(weights, np.ones(COLUMN))
    lanes[3, : INNER_WIDTH] = inner_node
    lanes[4, : INNER_WIDTH] = inner_lumped
    columns = np.zeros((ypad, 8))
    columns[:rows_local, 0] = lumped_y
    columns[:5, 1] = weights
    along_y = np.zeros((16, 8))
    along_y[:5, :5] = slopes
    along_y[8:13, :5] = slopes.T
    pick = np.zeros((RADIAL * 32, PAD))
    for r in range(RADIAL):
        for line in range(LINES):
            pick[r * 32 + line, line * RADIAL + r] = 1.0
    polar = np.zeros((PAIRS * 128, 256))
    for f in range(FIELDS):
        for k in (4, 5):
            for r in range(RADIAL):
                polar[(f // 2) * 128 + (f % 2) * 64 + k * RADIAL + r, (k - 4) * 128 + r * STEP + f] = 1.0
    as_f32 = lambda t: np.asarray(t, np.float32)
    return dict(
        table=as_f32(table),
        inner_table=as_f32(inner_table[:, : 2 * INNER_PAD]),
        inner_back=as_f32(inner_back),
        spread=as_f32(padded(spread, PAD)),
        squeeze=as_f32(np.pad(spread.T, ((0, PAD - WIDTH), (0, 0)))),
        lanes=as_f32(lanes),
        columns=as_f32(columns),
        along_y=as_f32(along_y),
        pick=as_f32(pick),
        polar=as_f32(polar),
        polar_back=as_f32(polar.T),
    )


def exchange_tables(count_x, count_y, rows):
    reach_x, reach_y = ACROSS - 1, rows - 1
    side = count_x * reach_x
    ypad = -(-rows // 8) * 8

    def canonical(j, i, y, x, k):
        gy, gx = j * reach_y + y, i * reach_x + x
        if k < 4 and gx == side:
            k, gx = (k + 1) % 4, 0
        if k < 4 and gy == side:
            gx, gy = ((gx, 0), (side, gx), (side - gx, side), (0, side - gx))[k]
            k = 4
        elif k < 4 and gy == 0:
            gx, gy = ((gx, side), (side, side - gx), (side - gx, 0), (0, gx))[k]
            k = 5
        return k, gy, gx

    def swapped(source, target):
        sj, si, sy, sx, sk = source
        j, i, y, x, k = target
        if sj == j and sy == y:
            if (x, sx) == (reach_x, 0):
                if (si, sk) == (i + 1, k):
                    return True
                if i == count_x - 1 and si == 0 and k < 4 and sk == (k + 1) % 4:
                    return True
            if (x, sx) == (0, reach_x):
                if (si, sk) == (i - 1, k):
                    return True
                if i == 0 and si == count_x - 1 and k < 4 and sk == (k - 1) % 4:
                    return True
        if si == i and sx == x:
            if sk == k and (sj, sy, y) in ((j + 1, 0, reach_y), (j - 1, reach_y, 0)):
                return True
            if (j, y, sj, sy) == (0, 0, count_y - 1, reach_y) and (k, sk) in ((4, 0), (0, 5)):
                return True
            if (j, y, sj, sy) == (count_y - 1, reach_y, 0, 0) and (k, sk) in ((0, 4), (5, 0)):
                return True
        return False

    def row_of(y, x, k):
        if y == reach_y:
            return x * GROUPS + k
        if y == 0:
            return 32 + x * GROUPS + k
        return 64 + (k - 4) * 2 * ypad + (ypad if x else 0) + y

    copies = collections.defaultdict(list)
    for j in range(count_y):
        for i in range(count_x):
            for y in range(rows):
                for x in range(ACROSS):
                    if 0 < y < reach_y and 0 < x < reach_x:
                        continue
                    for k in range(GROUPS):
                        copies[canonical(j, i, y, x, k)].append((j, i, y, x, k))
    pairs = collections.defaultdict(list)
    for members in copies.values():
        for target in members:
            for source in members:
                if source != target and not swapped(source, target):
                    key = (source[1] * count_y + source[0], target[1] * count_y + target[0])
                    pairs[key].append((row_of(*source[2:]), row_of(*target[2:])))
    table = np.full((count_x * count_y, 8, ENTRIES), -1.0, np.float32)
    sent = collections.Counter()
    taken = collections.Counter()
    for (source, target), links in sorted(pairs.items()):
        assert len(links) <= SLOTS
        for slot, (row_from, row_to) in enumerate(sorted(links)):
            table[source, 0, sent[source]] = target * SLOTS + slot
            table[source, 1, sent[source]] = row_from
            sent[source] += 1
            table[target, 2, taken[target]] = source * SLOTS + slot
            table[target, 3, taken[target]] = row_to
            taken[target] += 1
    assert max(max(sent.values()), max(taken.values())) <= ENTRIES
    return table


def exact_dot(a, b):
    return jnp.dot(a, b, precision=highest, preferred_element_type=jnp.float32)


def iota(shape, axis):
    return lax.broadcasted_iota(jnp.int32, shape, axis)


def put(ref, row, block):
    for t in range(ref.shape[0]):
        width = min(128, block.shape[1] - 128 * t)
        ref[t, row : row + block.shape[0], 0:width] = block[:, 128 * t : 128 * t + width]


def take(ref, c, first, count):
    tiles = [ref[t, pl.ds(4 * first + c, count, stride=4), :] for t in range(ref.shape[0])]
    return jnp.concatenate(tiles, axis=1)


def scatter(ref, c, block):
    for t in range(ref.shape[0]):
        ref[t, pl.ds(c, block.shape[0], stride=4), :] = block[:, 128 * t : 128 * t + 128]


def own_table(table_ref, count_y):
    return table_ref[lax.axis_index("xi") * count_y + lax.axis_index("eta")]


def force_kernel(
    rows,
    count_x,
    count_y,
    disp,
    vel,
    acc,
    metric,
    moduli,
    rho,
    pot,
    rate,
    accel,
    core_metric,
    kappa,
    core_rho,
    inner_disp,
    inner_vel,
    inner_acc,
    inner_metric,
    inner_moduli,
    inner_rho,
    table_ref,
    forward,
    inner_forward,
    inner_back,
    spread,
    lanes,
    columns,
    along_y,
    pick,
    polar,
    disp_next,
    pot_next,
    inner_next,
    fields,
    send_xa,
    send_xb,
    send_ya,
    send_yb,
    send_all,
    wide,
    narrow,
    inner_rows,
    flux,
    inner_flux,
    wide_u,
    edges,
    rows_t,
    points,
    moved,
    scale,
    lame,
    core_scale,
    inner_moved,
    inner_scale,
    inner_lame,
):
    ne = (rows - 1) // 4
    ypad = edges.shape[0] // 2
    half = 0.5 * time_step * time_step
    for y in range(rows):
        block = disp[y] + time_step * vel[y] + half * acc[y]
        disp_next[y] = block
        put(moved, 4 * y, block)
        put(scale, 4 * y, metric[y])
        put(lame, 4 * y, moduli[y])
        put(core_scale, 4 * y, core_metric[y])
        block = inner_disp[y] + time_step * inner_vel[y] + half * inner_acc[y]
        inner_next[y] = block
        put(inner_moved, 4 * y, block)
        put(inner_scale, 4 * y, inner_metric[y])
        put(inner_lame, 4 * y, inner_moduli[y])

    def part(ref, c, first=0, count=rows):
        width = WIDTH if ref.shape[0] * 128 == PAD else INNER_WIDTH
        return take(ref, c, first, count)[:, 0:width]

    pot_next[...] = pot[...] + time_step * rate[...] + half * accel[...]

    slope = along_y[0:5, 0:5]
    slope_back = along_y[8:13, 0:5]

    def along(matrix, block):
        total = matrix[:, 0:1] * block[0:1, :]
        for b in range(1, 5):
            total = total + matrix[:, b : b + 1] * block[b : b + 1, :]
        return total

    wide[...] = jnp.zeros(wide.shape, jnp.float32)
    narrow[...] = jnp.zeros(narrow.shape, jnp.float32)
    inner_rows[...] = jnp.zeros(inner_rows.shape, jnp.float32)
    fields[...] = jnp.zeros(fields.shape, jnp.float32)

    def slot(f, e):
        return (f * ne + e) * 8

    extras = [(scale, c) for c in range(3)] + [(lame, c) for c in range(2)] + [(core_scale, c) for c in range(3)]
    for e in range(ne):
        for f in range(4):
            block = part(moved, f, 4 * e, 5) if f < 3 else pot_next[4 * e : 4 * e + 5, :]
            wide[slot(f, e) : slot(f, e) + 5, :] = block
            narrow[slot(f, e) : slot(f, e) + 5, :] = along(slope, block)
        for f, (ref, c) in enumerate(extras):
            narrow[slot(4 + f, e) : slot(4 + f, e) + 5, :] = part(ref, c, 4 * e, 5)
        narrow[slot(12, e) : slot(12, e) + 5, :] = core_rho[4 * e : 4 * e + 5, :]
        for f in range(3):
            inner_rows[slot(f, e) : slot(f, e) + 5, :] = part(inner_moved, f, 4 * e, 5)
    slopes_xr = exact_dot(wide[...], forward[:, 0 : 2 * PAD])
    copies = exact_dot(narrow[...], forward[:, 2 * PAD : 3 * PAD])
    inner_xr = exact_dot(inner_rows[...], inner_forward[...])

    def elastic(g, lam, mu, sy, sx, sr, jw):
        scaled = [[sy[i] * g[0], sx[i] * g[1], sr[i] * g[2]] for i in range(3)]
        trace = lam * (scaled[0][0] + scaled[1][1] + scaled[2][2])
        out = [[None] * 3 for _ in range(3)]
        weighted = [jw * g[m] for m in range(3)]
        for i in range(3):
            for m in range(3):
                if i == m:
                    stress = 2.0 * mu * scaled[i][i] + trace
                else:
                    stress = mu * (scaled[i][m] + scaled[m][i])
                out[i][m] = stress * weighted[m]
        return out

    row_weight = columns[0:5, 1:2]
    valid = (iota((5, PAD), 1) < NODES) & (iota((5, PAD), 0) < 5)
    for e in range(ne):
        def plain(f):
            return copies[slot(f, e) : slot(f, e) + 5, :]

        def x_of(f):
            return slopes_xr[slot(f, e) : slot(f, e) + 5, 0:PAD]

        def r_of(f):
            return slopes_xr[slot(f, e) : slot(f, e) + 5, PAD : 2 * PAD]

        node = row_weight * lanes[0:1, :]
        g = [jnp.where(valid, plain(4 + m), 1.0) for m in range(3)]
        q = elastic(
            g,
            plain(7),
            plain(8),
            [plain(f) for f in range(3)],
            [x_of(f) for f in range(3)],
            [r_of(f) for f in range(3)],
            node / (g[0] * g[1] * g[2]),
        )
        g = [jnp.where(valid, plain(9 + m), 1.0) for m in range(3)]
        volume = node / (g[0] * g[1] * g[2] * jnp.where(valid, plain(12), 1.0))
        q.append(
            [
                volume * g[0] * g[0] * plain(3),
                volume * g[1] * g[1] * x_of(3),
                volume * g[2] * g[2] * r_of(3),
            ]
        )
        for f in range(4):
            at = slot(f, e)
            flux[at : at + 5, 0:PAD] = q[f][1]
            flux[at : at + 5, PAD : 2 * PAD] = q[f][2]
            flux[at : at + 5, 2 * PAD : 3 * PAD] = along(slope_back, q[f][0])

        def inner_x(f):
            return inner_xr[slot(f, e) : slot(f, e) + 5, 0:INNER_WIDTH]

        def inner_r(f):
            return inner_xr[slot(f, e) : slot(f, e) + 5, INNER_PAD : INNER_PAD + INNER_WIDTH]

        g = [part(inner_scale, m, 4 * e, 5) for m in range(3)]
        node = row_weight * lanes[3:4, 0:INNER_WIDTH]
        q = elastic(
            g,
            part(inner_lame, 0, 4 * e, 5),
            part(inner_lame, 1, 4 * e, 5),
            [along(slope, inner_rows[slot(f, e) : slot(f, e) + 5, :]) for f in range(3)],
            [inner_x(f) for f in range(3)],
            [inner_r(f) for f in range(3)],
            node / (g[0] * g[1] * g[2]),
        )
        for f in range(3):
            at = slot(f, e)
            inner_flux[at : at + 5, 0:INNER_WIDTH] = q[f][1]
            inner_flux[at : at + 5, INNER_PAD : INNER_PAD + INNER_WIDTH] = q[f][2]
            inner_flux[at : at + 5, 2 * INNER_PAD : 2 * INNER_PAD + INNER_WIDTH] = along(slope_back, q[f][0])

    back = lax.dot_general(
        flux[...],
        forward[...],
        (((1,), (1,)), ((), ())),
        precision=highest,
        preferred_element_type=jnp.float32,
    )
    inner_forces = exact_dot(inner_flux[...], inner_back[...])
    for e in range(ne):
        here = slice(4 * e, 4 * e + 5)
        for f in range(3):
            fields[f, here, 0:WIDTH] = fields[f, here, 0:WIDTH] - back[slot(f, e) : slot(f, e) + 5, :]
            fields[IF + f, here, 0:WIDTH] = fields[IF + f, here, 0:WIDTH] - inner_forces[slot(f, e) : slot(f, e) + 5, :]
        fields[CF, here, 0:WIDTH] = fields[CF, here, 0:WIDTH] - back[slot(3, e) : slot(3, e) + 5, :]

    lumped_y = columns[0:rows, 0:1]
    lumped = lumped_y * lanes[1:2, 0:WIDTH]
    fields[MM, 0:rows, 0:WIDTH] = rho[...] * (lumped / (part(scale, 0) * part(scale, 1) * part(scale, 2)))
    fields[CM, 0:rows, 0:WIDTH] = lumped / (part(core_scale, 0) * part(core_scale, 1) * part(core_scale, 2)) / kappa[...]
    inner_mass = inner_rho[...] * (
        lumped_y * lanes[4:5, 0:INNER_WIDTH] / (part(inner_scale, 0) * part(inner_scale, 1) * part(inner_scale, 2))
    )
    fields[IM, 0:rows, :] = exact_dot(inner_mass, spread[...])
    radial = lax.rem(iota((rows, WIDTH), 1), RADIAL)
    face = lumped_y * lanes[2:3, 0:WIDTH] / (part(core_scale, 0) * part(core_scale, 1))
    face = jnp.where((radial == 0) | (radial == RADIAL - 1), face, 0.0)
    fields[CW, 0:rows, 0:WIDTH] = face
    wide_u[...] = jnp.zeros(wide_u.shape, jnp.float32)
    wide_u[0:rows, 0:WIDTH] = part(moved, 2)
    above = pltpu.roll(wide_u[...], RADIAL - 1, axis=1)
    wide_u[0:rows, :] = exact_dot(part(inner_moved, 2), spread[...])
    below = pltpu.roll(wide_u[...], PAD - (INNER_RADIAL - 1), axis=1)
    radial = lax.rem(iota((ypad, PAD), 1), RADIAL)
    jump = jnp.where(radial == RADIAL - 1, above, jnp.where(radial == 0, -below, 0.0))
    fields[CF] = fields[CF] + fields[CW] * jump

    low = iota((ypad, 128), 1) < 64
    for p in range(PAIRS):
        left = fields[2 * p]
        right = fields[2 * p + 1] if 2 * p + 1 < FIELDS else jnp.zeros_like(left)
        edges[0:ypad, p * 128 : p * 128 + 128] = jnp.where(low, left[:, 0:128], pltpu.roll(right[:, 0:128], 64, axis=1))
        edges[ypad : 2 * ypad, p * 128 : p * 128 + 128] = jnp.where(
            low,
            pltpu.roll(left, PAD - (WIDTH - COLUMN), axis=1)[:, 0:128],
            pltpu.roll(right, PAD + 64 - (WIDTH - COLUMN), axis=1)[:, 0:128],
        )
    even_x = lax.rem(lax.axis_index("xi"), 2) == 0
    even_y = lax.rem(lax.axis_index("eta"), 2) == 0
    for p in range(PAIRS):
        first = edges[0:rows, p * 128 : p * 128 + 128]
        last = edges[ypad : ypad + rows, p * 128 : p * 128 + 128]
        send_xa[p * rows : (p + 1) * rows, :] = jnp.where(even_x, last, first)
        send_xb[p * rows : (p + 1) * rows, :] = jnp.where(even_x, first, last)
    rows_t[...] = jnp.zeros(rows_t.shape, jnp.float32)
    for f in range(FIELDS):
        rows_t[f : f + 1, :] = fields[f, rows - 1 : rows, :]
        rows_t[64 + f : 65 + f, :] = fields[f, 0:1, :]
    top = rows_t[0:16, :]
    bottom = rows_t[64:80, :]
    send_ya[...] = jnp.where(even_y, top, bottom)
    send_yb[...] = jnp.where(even_y, bottom, top)

    by_line = lax.dot_general(
        pick[...],
        rows_t[...],
        (((1,), (1,)), ((), ())),
        precision=highest,
        preferred_element_type=jnp.float32,
    )
    lane = iota((32, 128), 1)
    top_points = jnp.zeros((32, 128), jnp.float32)
    bottom_points = jnp.zeros((32, 128), jnp.float32)
    for r in range(RADIAL):
        block = by_line[32 * r : 32 * r + 32, :]
        upper = jnp.where(lane < STEP, block, 0.0)
        lower = jnp.where((lane >= 64) & (lane < 64 + STEP), block, 0.0)
        top_points = top_points + (pltpu.roll(upper, STEP * r, axis=1) if r else upper)
        bottom_points = bottom_points + pltpu.roll(lower, (STEP * r + 64) % 128, axis=1)
    points[0:32, :] = top_points
    points[32:64, :] = bottom_points
    caps = exact_dot(edges[...], polar[...])
    points[64 : 64 + 2 * ypad, :] = caps[:, 0:128]
    points[64 + 2 * ypad : 64 + 4 * ypad, :] = caps[:, 128:256]

    own = own_table(table_ref, count_y)
    turned = jnp.transpose(own)
    count = points.shape[0]
    chosen = jnp.where(turned[:, 1:2] == iota((ENTRIES, count), 1).astype(jnp.float32), 1.0, 0.0)
    chosen = exact_dot(chosen, points[...])
    peers = CHUNK // SLOTS
    for c in range(count_x * count_y // peers):
        number = (iota((CHUNK, ENTRIES), 0) + c * CHUNK).astype(jnp.float32)
        placed = exact_dot(jnp.where(own[0:1, :] == number, 1.0, 0.0), chosen)
        send_all[c * peers : (c + 1) * peers] = placed.reshape(peers, SLOTS, 128)


def close_kernel(
    rows,
    count_x,
    count_y,
    got_xa,
    got_xb,
    got_ya,
    got_yb,
    got_all,
    fields,
    vel,
    acc,
    rate,
    accel,
    inner_vel,
    inner_acc,
    table_ref,
    pick,
    polar_back,
    squeeze,
    vel_next,
    acc_next,
    rate_next,
    accel_next,
    inner_vel_next,
    inner_acc_next,
    total,
    by_line,
    caps,
    narrow,
    wide,
):
    ypad = total.shape[1]
    narrow[...] = jnp.zeros(narrow.shape, jnp.float32)
    own = own_table(table_ref, count_y)
    turned = jnp.transpose(own)
    peers = CHUNK // SLOTS
    arrived = jnp.zeros((ENTRIES, 128), jnp.float32)
    for c in range(count_x * count_y // peers):
        number = (iota((ENTRIES, CHUNK), 1) + c * CHUNK).astype(jnp.float32)
        block = got_all[c * peers : (c + 1) * peers].reshape(CHUNK, 128)
        arrived = arrived + exact_dot(jnp.where(turned[:, 2:3] == number, 1.0, 0.0), block)
    count = 64 + 4 * ypad
    points = exact_dot(
        jnp.where(own[3:4, :] == iota((count, ENTRIES), 0).astype(jnp.float32), 1.0, 0.0), arrived
    )
    lane = iota((32, 128), 1)
    upper = points[0:32]
    lower = points[32:64]
    for r in range(RADIAL):
        first = pltpu.roll(upper, (128 - STEP * r) % 128, axis=1) if r else upper
        second = pltpu.roll(lower, (64 - STEP * r) % 128, axis=1)
        by_line[32 * r : 32 * r + 32, :] = jnp.where(lane < STEP, first, 0.0) + jnp.where(
            (lane >= 64) & (lane < 64 + STEP), second, 0.0
        )
    lines = lax.dot_general(
        by_line[...],
        pick[...],
        (((0,), (0,)), ((), ())),
        precision=highest,
        preferred_element_type=jnp.float32,
    )
    caps[:, 0:128] = points[64 : 64 + 2 * ypad]
    caps[:, 128:256] = points[64 + 2 * ypad : 64 + 4 * ypad]
    columns = exact_dot(caps[...], polar_back[...])

    xi = lax.axis_index("xi")
    eta = lax.axis_index("eta")
    even_x = lax.rem(xi, 2) == 0
    even_y = lax.rem(eta, 2) == 0
    lane = iota((16, PAD), 1)
    group = lax.rem(lane // RADIAL, GROUPS)
    used = lane < WIDTH
    ya = got_ya[...]
    yb = got_yb[...]
    from_above = jnp.where(even_y, ya, yb)
    from_below = jnp.where(even_y, yb, ya)
    four, five = 4 * RADIAL, 5 * RADIAL
    seam_top = jnp.where(
        group == 0,
        pltpu.roll(from_above, PAD - four, axis=1),
        jnp.where(group == 5, pltpu.roll(from_above, five, axis=1), 0.0),
    )
    seam_bottom = jnp.where(
        group == 4,
        pltpu.roll(from_below, four, axis=1),
        jnp.where(group == 0, pltpu.roll(from_below, PAD - five, axis=1), 0.0),
    )
    add_top = jnp.where(eta == count_y - 1, seam_top, from_above) + lines[0:16]
    add_bottom = jnp.where(eta == 0, seam_bottom, from_below) + lines[64:80]
    add_top = jnp.where(used, add_top, 0.0)
    add_bottom = jnp.where(used, add_bottom, 0.0)
    total[...] = fields[...]
    lane = iota((rows, 128), 1)
    inside = lax.rem(lane, 64)
    equator = inside < 4 * RADIAL
    keep = inside < COLUMN
    low = lane < 64
    last_x = xi == count_x - 1
    for p in range(PAIRS):
        xa = got_xa[p * rows : (p + 1) * rows, :]
        xb = got_xb[p * rows : (p + 1) * rows, :]
        from_right = jnp.where(even_x, xa, xb)
        from_left = jnp.where(even_x, xb, xa)
        up = jnp.where(
            inside < 3 * RADIAL,
            pltpu.roll(from_right, 128 - RADIAL, axis=1),
            pltpu.roll(from_right, 3 * RADIAL, axis=1),
        )
        down = jnp.where(
            inside < RADIAL,
            pltpu.roll(from_left, 128 - 3 * RADIAL, axis=1),
            pltpu.roll(from_left, RADIAL, axis=1),
        )
        from_right = jnp.where(last_x, jnp.where(equator, up, 0.0), from_right)
        from_left = jnp.where(xi == 0, jnp.where(equator, down, 0.0), from_left)
        at = slice(p * 128, p * 128 + 128)
        from_left = jnp.where(keep, from_left + columns[0:rows, at], 0.0)
        from_right = jnp.where(keep, from_right + columns[ypad : ypad + rows, at], 0.0)
        zero = jnp.zeros((rows, PAD - 128), jnp.float32)
        for h in range(2):
            f = 2 * p + h
            if f >= FIELDS:
                continue
            mine = low if h == 0 else ~low
            left = jnp.where(mine, from_left, 0.0)
            right = jnp.where(mine, from_right, 0.0)
            if h:
                left = pltpu.roll(left, 64, axis=1)
            total[f, 0:rows, 0:128] = total[f, 0:rows, 0:128] + left
            right = jnp.concatenate([right, zero], axis=1)
            right = pltpu.roll(right, WIDTH - COLUMN - 64 * h, axis=1)
            total[f, 0:rows, :] = total[f, 0:rows, :] + right
    for f in range(FIELDS):
        total[f, rows - 1 : rows, :] = total[f, rows - 1 : rows, :] + add_top[f : f + 1, :]
        total[f, 0:1, :] = total[f, 0:1, :] + add_bottom[f : f + 1, :]

    half = 0.5 * time_step
    lane = iota((ypad, PAD), 1)
    radial = lax.rem(lane, RADIAL)
    inside = (lane < WIDTH) & (iota((ypad, PAD), 0) < rows)
    core = total[CF] / jnp.where(inside, total[CM], 1.0)
    accel_next[...] = core[0:rows, 0:WIDTH]
    rate_next[...] = rate[...] + half * (accel[...] + core[0:rows, 0:WIDTH])
    push = total[CW] * core
    top = jnp.where(radial == 0, pltpu.roll(push, PAD - (RADIAL - 1), axis=1), 0.0)
    bottom = jnp.where(radial == INNER_RADIAL - 1, pltpu.roll(push, INNER_RADIAL - 1, axis=1), 0.0)
    mass = jnp.where(inside, total[MM], 1.0)
    inner_mass = jnp.where(inside & (radial < INNER_RADIAL), total[IM], 1.0)
    for f in range(3):
        force = total[f] + top if f == 2 else total[f]
        result = (force / mass)[0:rows]
        scatter(wide, f, result)
        force = total[IF + f] - bottom if f == 2 else total[IF + f]
        scatter(narrow, f, (force / inner_mass)[0:rows])
    squeezed = exact_dot(jnp.concatenate([narrow[t] for t in range(PAD // 128)], axis=1), squeeze[...])
    for y in range(rows):
        result = jnp.concatenate([wide[t, 4 * y : 4 * y + 3, :] for t in range(PAD // 128)], axis=1)[:, 0:WIDTH]
        acc_next[y] = result
        vel_next[y] = vel[y] + half * (acc[y] + result)
        result = squeezed[4 * y : 4 * y + 3, :]
        inner_acc_next[y] = result
        inner_vel_next[y] = inner_vel[y] + half * (inner_acc[y] + result)


def shards(
    count_x,
    count_y,
    mantle_disp,
    mantle_vel,
    mantle_acc,
    mantle_metric,
    mantle_moduli,
    mantle_rho,
    core_pot,
    core_rate,
    core_accel,
    core_metric,
    core_kappa,
    core_rho,
    inner_disp,
    inner_vel,
    inner_acc,
    inner_metric,
    inner_moduli,
    inner_rho,
):
    rows = mantle_disp.shape[1]
    turn = lambda a: jnp.transpose(a, (1, 0, 2))
    mantle_disp, mantle_vel, mantle_acc = turn(mantle_disp), turn(mantle_vel), turn(mantle_acc)
    mantle_metric, mantle_moduli, core_metric = turn(mantle_metric), turn(mantle_moduli), turn(core_metric)
    inner_disp, inner_vel, inner_acc = turn(inner_disp), turn(inner_vel), turn(inner_acc)
    inner_metric, inner_moduli = turn(inner_metric), turn(inner_moduli)
    ne = (rows - 1) // 4
    ypad = -(-rows // 8) * 8
    tables = {name: jnp.asarray(value) for name, value in constants(rows).items()}
    table = jnp.asarray(exchange_tables(count_x, count_y, rows))
    f32 = jnp.float32
    like = lambda a: jax.ShapeDtypeStruct(a.shape, f32)
    shape = lambda *s: jax.ShapeDtypeStruct(s, f32)
    devices = count_x * count_y
    edge = -(-PAIRS * rows // 8) * 8
    (mantle_next, core_next, inner_next, fields, xa, xb, ya, yb, everyone) = pl.pallas_call(
        functools.partial(force_kernel, rows, count_x, count_y),
        out_shape=[
            like(mantle_disp),
            like(core_pot),
            like(inner_disp),
            shape(FIELDS, ypad, PAD),
            shape(edge, 128),
            shape(edge, 128),
            shape(16, PAD),
            shape(16, PAD),
            shape(devices, SLOTS, 128),
        ],
        scratch_shapes=[
            pltpu.VMEM((4 * ne * 8, WIDTH), f32),
            pltpu.VMEM((13 * ne * 8, WIDTH), f32),
            pltpu.VMEM((3 * ne * 8, INNER_WIDTH), f32),
            pltpu.VMEM((4 * ne * 8, 3 * PAD), f32),
            pltpu.VMEM((3 * ne * 8, 3 * INNER_PAD), f32),
            pltpu.VMEM((ypad, PAD), f32),
            pltpu.VMEM((2 * ypad, PAIRS * 128), f32),
            pltpu.VMEM((128, PAD), f32),
            pltpu.VMEM((64 + 4 * ypad, 128), f32),
        ]
        + [pltpu.VMEM((PAD // 128, 4 * rows, 128), f32)] * 4
        + [pltpu.VMEM((INNER_PAD // 128, 4 * rows, 128), f32)] * 3,
        name="forces",
    )(
        mantle_disp,
        mantle_vel,
        mantle_acc,
        mantle_metric,
        mantle_moduli,
        mantle_rho,
        core_pot,
        core_rate,
        core_accel,
        core_metric,
        core_kappa,
        core_rho,
        inner_disp,
        inner_vel,
        inner_acc,
        inner_metric,
        inner_moduli,
        inner_rho,
        table,
        tables["table"],
        tables["inner_table"],
        tables["inner_back"],
        tables["spread"],
        tables["lanes"],
        tables["columns"],
        tables["along_y"],
        tables["pick"],
        tables["polar"],
    )
    everyone = lax.all_to_all(everyone, ("xi", "eta"), 0, 0, tiled=True)
    near = [(i, i ^ 1) for i in range(count_x)]
    far = [(i, (i - 1 if i % 2 == 0 else i + 1) % count_x) for i in range(count_x)]
    xa = lax.ppermute(xa, "xi", near)
    xb = lax.ppermute(xb, "xi", far)
    near = [(j, j ^ 1) for j in range(count_y)]
    far = [(j, (j - 1 if j % 2 == 0 else j + 1) % count_y) for j in range(count_y)]
    ya = lax.ppermute(ya, "eta", near)
    yb = lax.ppermute(yb, "eta", far)
    (mantle_vel_next, mantle_acc_next, core_rate_next, core_acc_next, inner_vel_next, inner_acc_next) = pl.pallas_call(
        functools.partial(close_kernel, rows, count_x, count_y),
        out_shape=[
            like(mantle_vel),
            like(mantle_acc),
            like(core_rate),
            like(core_accel),
            like(inner_vel),
            like(inner_acc),
        ],
        scratch_shapes=[
            pltpu.VMEM((FIELDS, ypad, PAD), f32),
            pltpu.VMEM((RADIAL * 32, 128), f32),
            pltpu.VMEM((2 * ypad, 256), f32),
            pltpu.VMEM((PAD // 128, 4 * rows, 128), f32),
            pltpu.VMEM((PAD // 128, 4 * rows, 128), f32),
        ],
        name="close",
    )(
        xa,
        xb,
        ya,
        yb,
        everyone,
        fields,
        mantle_vel,
        mantle_acc,
        core_rate,
        core_accel,
        inner_vel,
        inner_acc,
        table,
        tables["pick"],
        tables["polar_back"],
        tables["squeeze"],
    )
    return (
        turn(mantle_next),
        turn(mantle_vel_next),
        turn(mantle_acc_next),
        core_next,
        core_rate_next,
        core_acc_next,
        turn(inner_next),
        turn(inner_vel_next),
        turn(inner_acc_next),
    )


def solution(mesh):
    count_x, count_y = mesh.shape["xi"], mesh.shape["eta"]
    assert count_x % 2 == 0 and count_y % 2 == 0
    assert (count_x * count_y * SLOTS) % CHUNK == 0
    vector, scalar = P(None, "eta", "xi"), P("eta", "xi")
    placed = (vector,) * 5 + (scalar,) * 4 + (vector,) + (scalar,) * 2 + (vector,) * 5 + (scalar,)
    return jax.shard_map(
        functools.partial(shards, count_x, count_y),
        mesh=mesh,
        in_specs=placed,
        out_specs=(vector,) * 3 + (scalar,) * 3 + (vector,) * 3,
        check_vma=False,
    )
```

```python
import collections
import functools
import math

import jax
import jax.numpy as jnp
import numpy as np
from jax import lax
from jax.experimental import pallas as pl
from jax.experimental.pallas import tpu as pltpu
from jax.sharding import PartitionSpec as P

EX = 1
MANTLE_LAYERS = 2
CORE_LAYERS = 2
INNER_LAYERS = 1
GROUPS = 6
ACROSS = 4 * EX + 1
RADIAL = 4 * MANTLE_LAYERS + 1
INNER_RADIAL = 4 * INNER_LAYERS + 1
LINES = ACROSS * GROUPS
WIDTH = LINES * RADIAL
INNER_WIDTH = LINES * INNER_RADIAL
COLUMN = GROUPS * RADIAL
NODES = LINES * 5 * MANTLE_LAYERS
PAD = 384
INNER_PAD = 256
STEP = 12
ENTRIES = 128
SLOTS = 16
CHUNK = 512
time_step = 0.1

MM, CF, CM, IF, IM, CW, FIELDS = 3, 4, 5, 6, 9, 10, 11
PAIRS = 6


def gll_tables():
    radical = math.sqrt(3.0 / 7.0)
    points = np.array([-1.0, -radical, 0.0, radical, 1.0])
    weights = np.array([0.1, 49.0 / 90.0, 32.0 / 45.0, 49.0 / 90.0, 0.1])
    products = np.array(
        [np.prod([points[a] - points[c] for c in range(5) if c != a]) for a in range(5)]
    )
    slopes = np.zeros((5, 5))
    for a in range(5):
        for b in range(5):
            if a == b:
                slopes[a, b] = np.sum([1.0 / (points[a] - points[c]) for c in range(5) if c != a])
            else:
                slopes[a, b] = products[a] / (products[b] * (points[a] - points[b]))
    return weights, slopes


def spread_table(count):
    spread = np.zeros((4 * count + 1, 5 * count))
    for element in range(count):
        for node in range(5):
            spread[4 * element + node, 5 * element + node] = 1.0
    return spread


def padded(table, width):
    return np.pad(table, ((0, 0), (0, width - table.shape[1])))


def lane_tables(layers, width):
    weights, slopes = gll_tables()
    spread = spread_table(layers)
    derive = np.kron(np.eye(layers), slopes.T)
    eye_k = np.eye(GROUPS)
    along_x = np.kron(slopes.T, np.kron(eye_k, spread))
    along_r = np.kron(np.eye(ACROSS), np.kron(eye_k, spread @ derive))
    plain = np.kron(np.eye(ACROSS), np.kron(eye_k, spread))
    node = np.kron(weights, np.kron(np.ones(GROUPS), np.tile(weights, layers)))
    lumped_r = spread @ np.tile(weights, layers)
    lumped = np.kron(weights, np.kron(np.ones(GROUPS), lumped_r))
    table = np.concatenate([padded(t, width) for t in (along_x, along_r, plain)], axis=1)
    return table.astype(np.float32), node.astype(np.float32), lumped.astype(np.float32)


def constants(rows_local):
    weights, slopes = gll_tables()
    count_y = (rows_local - 1) // 4
    ypad = -(-rows_local // 8) * 8
    table, node, lumped = lane_tables(MANTLE_LAYERS, PAD)
    inner_table, inner_node, inner_lumped = lane_tables(INNER_LAYERS, INNER_PAD)
    small = np.eye(RADIAL)[:INNER_RADIAL]
    spread = np.kron(np.eye(LINES), small)
    lumped_y = spread_table(count_y) @ np.tile(weights, count_y)
    lanes = np.zeros((8, PAD))
    lanes[0, :NODES] = node
    lanes[1, :WIDTH] = lumped
    lanes[2, :WIDTH] = np.kron(weights, np.ones(COLUMN))
    lanes[3, : INNER_WIDTH] = inner_node
    lanes[4, : INNER_WIDTH] = inner_lumped
    columns = np.zeros((ypad, 8))
    columns[:rows_local, 0] = lumped_y
    columns[:5, 1] = weights
    along_y = np.zeros((16, 8))
    along_y[:5, :5] = slopes
    along_y[8:13, :5] = slopes.T
    pick = np.zeros((RADIAL * 32, PAD))
    for r in range(RADIAL):
        for line in range(LINES):
            pick[r * 32 + line, line * RADIAL + r] = 1.0
    polar = np.zeros((PAIRS * 128, 256))
    for f in range(FIELDS):
        for k in (4, 5):
            for r in range(RADIAL):
                polar[(f // 2) * 128 + (f % 2) * 64 + k * RADIAL + r, (k - 4) * 128 + r * STEP + f] = 1.0
    as_f32 = lambda t: np.asarray(t, np.float32)
    as_bf16 = lambda t: np.asarray(t, np.float32).astype(bf16)

    def split(t):
        rest = as_f32(t)
        out = []
        for _ in range(3):
            out.append(rest.astype(bf16))
            rest = rest - out[-1].astype(np.float32)
        return np.stack(out)

    return dict(
        table=split(table[:, : 2 * PAD]),
        plain=as_bf16(table[:, 2 * PAD :]),
        inner_table=split(inner_table[:, : 2 * INNER_PAD]),
        spread=as_bf16(padded(spread, PAD)),
        squeeze=as_bf16(np.pad(spread.T, ((0, PAD - WIDTH), (0, 0)))),
        lanes=as_f32(lanes),
        columns=as_f32(columns),
        along_y=as_f32(along_y),
        pick=as_bf16(pick),
        polar=as_bf16(polar),
        polar_back=as_bf16(polar.T),
    )


def exchange_tables(count_x, count_y, rows):
    reach_x, reach_y = ACROSS - 1, rows - 1
    side = count_x * reach_x
    ypad = -(-rows // 8) * 8

    def canonical(j, i, y, x, k):
        gy, gx = j * reach_y + y, i * reach_x + x
        if k < 4 and gx == side:
            k, gx = (k + 1) % 4, 0
        if k < 4 and gy == side:
            gx, gy = ((gx, 0), (side, gx), (side - gx, side), (0, side - gx))[k]
            k = 4
        elif k < 4 and gy == 0:
            gx, gy = ((gx, side), (side, side - gx), (side - gx, 0), (0, gx))[k]
            k = 5
        return k, gy, gx

    def swapped(source, target):
        sj, si, sy, sx, sk = source
        j, i, y, x, k = target
        if sj == j and sy == y:
            if (x, sx) == (reach_x, 0):
                if (si, sk) == (i + 1, k):
                    return True
                if i == count_x - 1 and si == 0 and k < 4 and sk == (k + 1) % 4:
                    return True
            if (x, sx) == (0, reach_x):
                if (si, sk) == (i - 1, k):
                    return True
                if i == 0 and si == count_x - 1 and k < 4 and sk == (k - 1) % 4:
                    return True
        if si == i and sx == x:
            if sk == k and (sj, sy, y) in ((j + 1, 0, reach_y), (j - 1, reach_y, 0)):
                return True
            if (j, y, sj, sy) == (0, 0, count_y - 1, reach_y) and (k, sk) in ((4, 0), (0, 5)):
                return True
            if (j, y, sj, sy) == (count_y - 1, reach_y, 0, 0) and (k, sk) in ((0, 4), (5, 0)):
                return True
        return False

    def row_of(y, x, k):
        if y == reach_y:
            return x * GROUPS + k
        if y == 0:
            return 32 + x * GROUPS + k
        return 64 + (k - 4) * 2 * ypad + (ypad if x else 0) + y

    copies = collections.defaultdict(list)
    for j in range(count_y):
        for i in range(count_x):
            for y in range(rows):
                for x in range(ACROSS):
                    if 0 < y < reach_y and 0 < x < reach_x:
                        continue
                    for k in range(GROUPS):
                        copies[canonical(j, i, y, x, k)].append((j, i, y, x, k))
    pairs = collections.defaultdict(list)
    for members in copies.values():
        for target in members:
            for source in members:
                if source != target and not swapped(source, target):
                    key = (source[1] * count_y + source[0], target[1] * count_y + target[0])
                    pairs[key].append((row_of(*source[2:]), row_of(*target[2:])))
    table = np.full((count_x * count_y, 8, ENTRIES), -1.0, np.float32)
    sent = collections.Counter()
    taken = collections.Counter()
    for (source, target), links in sorted(pairs.items()):
        assert len(links) <= SLOTS
        for slot, (row_from, row_to) in enumerate(sorted(links)):
            table[source, 0, sent[source]] = target * SLOTS + slot
            table[source, 1, sent[source]] = row_from
            sent[source] += 1
            table[target, 2, taken[target]] = source * SLOTS + slot
            table[target, 3, taken[target]] = row_to
            taken[target] += 1
    assert max(max(sent.values()), max(taken.values())) <= ENTRIES
    return table


bf16 = jnp.bfloat16


def parts_of(x):
    high = x.astype(bf16)
    rest = x - high.astype(jnp.float32)
    middle = rest.astype(bf16)
    return high, middle, (rest - middle.astype(jnp.float32)).astype(bf16)


def product(a, b, back=False):
    dims = (((1,), (1 if back else 0,)), ((), ()))
    return lax.dot_general(a, b, dims, preferred_element_type=jnp.float32)


def pick_right(x, chosen):
    count = x.shape[0]
    out = product(jnp.concatenate(parts_of(x), axis=0), chosen)
    return out[0:count] + out[count : 2 * count] + out[2 * count : 3 * count]


def pick_left(chosen, x):
    width = x.shape[1]
    out = product(chosen, jnp.concatenate(parts_of(x), axis=1))
    return out[:, 0:width] + out[:, width : 2 * width] + out[:, 2 * width : 3 * width]


def times(x, table, lanes, back=False):
    count = x.shape[0]
    high, middle, low = parts_of(x)
    out = product(jnp.concatenate([high, middle, low], axis=0), table[0, :, lanes], back)
    total = out[0:count] + (out[count : 2 * count] + out[2 * count : 3 * count])
    out = product(jnp.concatenate([high, middle], axis=0), table[1, :, lanes], back)
    total = total + (out[0:count] + out[count : 2 * count])
    return total + product(high, table[2, :, lanes], back)


def chosen_by(condition):
    return jnp.where(condition, 1.0, 0.0).astype(bf16)


def iota(shape, axis):
    return lax.broadcasted_iota(jnp.int32, shape, axis)


def put(ref, row, block):
    for t in range(ref.shape[0]):
        width = min(128, block.shape[1] - 128 * t)
        ref[t, row : row + block.shape[0], 0:width] = block[:, 128 * t : 128 * t + width]


def take(ref, c, first, count):
    tiles = [ref[t, pl.ds(4 * first + c, count, stride=4), :] for t in range(ref.shape[0])]
    return jnp.concatenate(tiles, axis=1)


def scatter(ref, c, block):
    for t in range(ref.shape[0]):
        ref[t, pl.ds(c, block.shape[0], stride=4), :] = block[:, 128 * t : 128 * t + 128]


def own_table(table_ref, count_y):
    return table_ref[lax.axis_index("xi") * count_y + lax.axis_index("eta")]


def force_kernel(
    rows,
    count_x,
    count_y,
    disp,
    vel,
    acc,
    metric,
    moduli,
    rho,
    pot,
    rate,
    accel,
    core_metric,
    kappa,
    core_rho,
    inner_disp,
    inner_vel,
    inner_acc,
    inner_metric,
    inner_moduli,
    inner_rho,
    table_ref,
    forward,
    plain_lanes,
    inner_forward,
    spread,
    lanes,
    columns,
    along_y,
    pick,
    polar,
    disp_next,
    pot_next,
    inner_next,
    fields,
    send_xa,
    send_xb,
    send_ya,
    send_yb,
    send_all,
    wide,
    narrow,
    inner_rows,
    flux,
    inner_flux,
    wide_u,
    edges,
    rows_t,
    points,
    moved,
    scale,
    lame,
    core_scale,
    inner_moved,
    inner_scale,
    inner_lame,
    stack,
):
    ne = (rows - 1) // 4
    ypad = edges.shape[0] // 2
    half = 0.5 * time_step * time_step
    for y in range(rows):
        block = disp[y] + time_step * vel[y] + half * acc[y]
        disp_next[y] = block
        put(moved, 4 * y, block)
        put(scale, 4 * y, metric[y])
        put(lame, 4 * y, moduli[y])
        put(core_scale, 4 * y, core_metric[y])
        block = inner_disp[y] + time_step * inner_vel[y] + half * inner_acc[y]
        inner_next[y] = block
        put(inner_moved, 4 * y, block)
        put(inner_scale, 4 * y, inner_metric[y])
        put(inner_lame, 4 * y, inner_moduli[y])

    def part(ref, c, first=0, count=rows):
        width = WIDTH if ref.shape[0] * 128 == PAD else INNER_WIDTH
        return take(ref, c, first, count)[:, 0:width]

    pot_next[...] = pot[...] + time_step * rate[...] + half * accel[...]

    slope = along_y[0:5, 0:5]
    slope_back = along_y[8:13, 0:5]

    def along(matrix, block):
        total = matrix[:, 0:1] * block[0:1, :]
        for b in range(1, 5):
            total = total + matrix[:, b : b + 1] * block[b : b + 1, :]
        return total

    wide[...] = jnp.zeros(wide.shape, jnp.float32)
    narrow[...] = jnp.zeros(narrow.shape, jnp.float32)
    inner_rows[...] = jnp.zeros(inner_rows.shape, jnp.float32)
    flux[...] = jnp.zeros(flux.shape, jnp.float32)
    inner_flux[...] = jnp.zeros(inner_flux.shape, jnp.float32)
    stack[...] = jnp.zeros(stack.shape, jnp.float32)
    fields[...] = jnp.zeros(fields.shape, jnp.float32)

    def slot(f, e):
        return (f * ne + e) * 8

    extras = [(scale, c) for c in range(3)] + [(lame, c) for c in range(2)] + [(core_scale, c) for c in range(3)]
    for e in range(ne):
        for f in range(4):
            block = part(moved, f, 4 * e, 5) if f < 3 else pot_next[4 * e : 4 * e + 5, :]
            wide[slot(f, e) : slot(f, e) + 5, :] = block
            narrow[slot(f, e) : slot(f, e) + 5, :] = along(slope, block)
        for f, (ref, c) in enumerate(extras):
            narrow[slot(4 + f, e) : slot(4 + f, e) + 5, :] = part(ref, c, 4 * e, 5)
        narrow[slot(12, e) : slot(12, e) + 5, :] = core_rho[4 * e : 4 * e + 5, :]
        for f in range(3):
            inner_rows[slot(f, e) : slot(f, e) + 5, :] = part(inner_moved, f, 4 * e, 5)
    whole = slice(None)
    slopes_xr = times(wide[...], forward, whole)
    copies = pick_right(narrow[...], plain_lanes[...])
    inner_xr = times(inner_rows[...], inner_forward, whole)

    def elastic(g, lam, mu, sy, sx, sr, jw):
        scaled = [[sy[i] * g[0], sx[i] * g[1], sr[i] * g[2]] for i in range(3)]
        trace = lam * (scaled[0][0] + scaled[1][1] + scaled[2][2])
        out = [[None] * 3 for _ in range(3)]
        weighted = [jw * g[m] for m in range(3)]
        for i in range(3):
            for m in range(3):
                if i == m:
                    stress = 2.0 * mu * scaled[i][i] + trace
                else:
                    stress = mu * (scaled[i][m] + scaled[m][i])
                out[i][m] = stress * weighted[m]
        return out

    row_weight = columns[0:5, 1:2]
    valid = (iota((5, PAD), 1) < NODES) & (iota((5, PAD), 0) < 5)
    for e in range(ne):
        def plain(f):
            return copies[slot(f, e) : slot(f, e) + 5, :]

        def x_of(f):
            return slopes_xr[slot(f, e) : slot(f, e) + 5, 0:PAD]

        def r_of(f):
            return slopes_xr[slot(f, e) : slot(f, e) + 5, PAD : 2 * PAD]

        node = row_weight * lanes[0:1, :]
        g = [jnp.where(valid, plain(4 + m), 1.0) for m in range(3)]
        q = elastic(
            g,
            plain(7),
            plain(8),
            [plain(f) for f in range(3)],
            [x_of(f) for f in range(3)],
            [r_of(f) for f in range(3)],
            node / (g[0] * g[1] * g[2]),
        )
        g = [jnp.where(valid, plain(9 + m), 1.0) for m in range(3)]
        volume = node / (g[0] * g[1] * g[2] * jnp.where(valid, plain(12), 1.0))
        q.append(
            [
                volume * g[0] * g[0] * plain(3),
                volume * g[1] * g[1] * x_of(3),
                volume * g[2] * g[2] * r_of(3),
            ]
        )
        for f in range(4):
            at = slot(f, e)
            flux[at : at + 5, 0:PAD] = q[f][1]
            flux[at : at + 5, PAD : 2 * PAD] = q[f][2]
            flux[at : at + 5, 2 * PAD : 3 * PAD] = along(slope_back, q[f][0])

        def inner_x(f):
            return inner_xr[slot(f, e) : slot(f, e) + 5, 0:INNER_WIDTH]

        def inner_r(f):
            return inner_xr[slot(f, e) : slot(f, e) + 5, INNER_PAD : INNER_PAD + INNER_WIDTH]

        g = [part(inner_scale, m, 4 * e, 5) for m in range(3)]
        node = row_weight * lanes[3:4, 0:INNER_WIDTH]
        q = elastic(
            g,
            part(inner_lame, 0, 4 * e, 5),
            part(inner_lame, 1, 4 * e, 5),
            [along(slope, inner_rows[slot(f, e) : slot(f, e) + 5, :]) for f in range(3)],
            [inner_x(f) for f in range(3)],
            [inner_r(f) for f in range(3)],
            node / (g[0] * g[1] * g[2]),
        )
        for f in range(3):
            at = slot(f, e)
            inner_flux[at : at + 5, 0:INNER_WIDTH] = q[f][1]
            inner_flux[at : at + 5, INNER_PAD : INNER_PAD + INNER_WIDTH] = q[f][2]
            inner_flux[at : at + 5, 2 * INNER_PAD : 2 * INNER_PAD + INNER_WIDTH] = along(slope_back, q[f][0])

    back = times(flux[:, 0 : 2 * PAD], forward, whole, back=True)
    own_y = flux[:, 2 * PAD : 3 * PAD]
    count = own_y.shape[0]
    out = product(jnp.concatenate(parts_of(own_y), axis=0), plain_lanes[...], back=True)
    back = back + (out[0:count] + out[count : 2 * count] + out[2 * count : 3 * count])
    count = 3 * ne * 8
    stack[0:count, :] = (
        times(inner_flux[:, 0 : 2 * INNER_PAD], inner_forward, whole, back=True)
        + inner_flux[:, 2 * INNER_PAD : 2 * INNER_PAD + INNER_WIDTH]
    )
    lumped_y = columns[0:rows, 0:1]
    stack[count : count + rows, :] = inner_rho[...] * (
        lumped_y * lanes[4:5, 0:INNER_WIDTH] / (part(inner_scale, 0) * part(inner_scale, 1) * part(inner_scale, 2))
    )
    stack[count + ypad : count + ypad + rows, :] = part(inner_moved, 2)
    spreads = pick_right(stack[...], spread[...])
    inner_forces = spreads[0:count, 0:WIDTH]
    for e in range(ne):
        here = slice(4 * e, 4 * e + 5)
        for f in range(3):
            fields[f, here, 0:WIDTH] = fields[f, here, 0:WIDTH] - back[slot(f, e) : slot(f, e) + 5, :]
            fields[IF + f, here, 0:WIDTH] = fields[IF + f, here, 0:WIDTH] - inner_forces[slot(f, e) : slot(f, e) + 5, :]
        fields[CF, here, 0:WIDTH] = fields[CF, here, 0:WIDTH] - back[slot(3, e) : slot(3, e) + 5, :]

    lumped = lumped_y * lanes[1:2, 0:WIDTH]
    fields[MM, 0:rows, 0:WIDTH] = rho[...] * (lumped / (part(scale, 0) * part(scale, 1) * part(scale, 2)))
    fields[CM, 0:rows, 0:WIDTH] = lumped / (part(core_scale, 0) * part(core_scale, 1) * part(core_scale, 2)) / kappa[...]
    fields[IM, 0:rows, :] = spreads[count : count + rows]
    radial = lax.rem(iota((rows, WIDTH), 1), RADIAL)
    face = lumped_y * lanes[2:3, 0:WIDTH] / (part(core_scale, 0) * part(core_scale, 1))
    face = jnp.where((radial == 0) | (radial == RADIAL - 1), face, 0.0)
    fields[CW, 0:rows, 0:WIDTH] = face
    wide_u[...] = jnp.zeros(wide_u.shape, jnp.float32)
    wide_u[0:rows, 0:WIDTH] = part(moved, 2)
    above = pltpu.roll(wide_u[...], RADIAL - 1, axis=1)
    below = pltpu.roll(spreads[count + ypad : count + 2 * ypad], PAD - (INNER_RADIAL - 1), axis=1)
    radial = lax.rem(iota((ypad, PAD), 1), RADIAL)
    jump = jnp.where(radial == RADIAL - 1, above, jnp.where(radial == 0, -below, 0.0))
    fields[CF] = fields[CF] + fields[CW] * jump

    low = iota((ypad, 128), 1) < 64
    for p in range(PAIRS):
        left = fields[2 * p]
        right = fields[2 * p + 1] if 2 * p + 1 < FIELDS else jnp.zeros_like(left)
        edges[0:ypad, p * 128 : p * 128 + 128] = jnp.where(low, left[:, 0:128], pltpu.roll(right[:, 0:128], 64, axis=1))
        edges[ypad : 2 * ypad, p * 128 : p * 128 + 128] = jnp.where(
            low,
            pltpu.roll(left, PAD - (WIDTH - COLUMN), axis=1)[:, 0:128],
            pltpu.roll(right, PAD + 64 - (WIDTH - COLUMN), axis=1)[:, 0:128],
        )
    even_x = lax.rem(lax.axis_index("xi"), 2) == 0
    even_y = lax.rem(lax.axis_index("eta"), 2) == 0
    for p in range(PAIRS):
        first = edges[0:rows, p * 128 : p * 128 + 128]
        last = edges[ypad : ypad + rows, p * 128 : p * 128 + 128]
        send_xa[p * rows : (p + 1) * rows, :] = jnp.where(even_x, last, first)
        send_xb[p * rows : (p + 1) * rows, :] = jnp.where(even_x, first, last)
    rows_t[...] = jnp.zeros(rows_t.shape, jnp.float32)
    for f in range(FIELDS):
        rows_t[f : f + 1, :] = fields[f, rows - 1 : rows, :]
        rows_t[64 + f : 65 + f, :] = fields[f, 0:1, :]
    top = rows_t[0:16, :]
    bottom = rows_t[64:80, :]
    send_ya[...] = jnp.where(even_y, top, bottom)
    send_yb[...] = jnp.where(even_y, bottom, top)

    for at, block in ((0, top), (64, bottom)):
        for n, piece in enumerate(parts_of(block)):
            rows_t[at + 16 * n : at + 16 * n + 16, :] = piece.astype(jnp.float32)
    by_line = product(pick[...], rows_t[...].astype(bf16), back=True)
    by_line = by_line + (pltpu.roll(by_line, 128 - 16, axis=1) + pltpu.roll(by_line, 128 - 32, axis=1))
    lane = iota((32, 128), 1)
    top_points = jnp.zeros((32, 128), jnp.float32)
    bottom_points = jnp.zeros((32, 128), jnp.float32)
    for r in range(RADIAL):
        block = by_line[32 * r : 32 * r + 32, :]
        upper = jnp.where(lane < STEP, block, 0.0)
        lower = jnp.where((lane >= 64) & (lane < 64 + STEP), block, 0.0)
        top_points = top_points + (pltpu.roll(upper, STEP * r, axis=1) if r else upper)
        bottom_points = bottom_points + pltpu.roll(lower, (STEP * r + 64) % 128, axis=1)
    points[0:32, :] = top_points
    points[32:64, :] = bottom_points
    caps = pick_right(edges[...], polar[...])
    points[64 : 64 + 2 * ypad, :] = caps[:, 0:128]
    points[64 + 2 * ypad : 64 + 4 * ypad, :] = caps[:, 128:256]

    own = own_table(table_ref, count_y)
    turned = jnp.transpose(own)
    count = points.shape[0]
    chosen = chosen_by(turned[:, 1:2] == iota((ENTRIES, count), 1).astype(jnp.float32))
    chosen = pick_left(chosen, points[...])
    peers = CHUNK // SLOTS
    for c in range(count_x * count_y // peers):
        number = (iota((CHUNK, ENTRIES), 0) + c * CHUNK).astype(jnp.float32)
        placed = pick_left(chosen_by(own[0:1, :] == number), chosen)
        send_all[c * peers : (c + 1) * peers] = placed.reshape(peers, SLOTS, 128)


def close_kernel(
    rows,
    count_x,
    count_y,
    got_xa,
    got_xb,
    got_ya,
    got_yb,
    got_all,
    fields,
    vel,
    acc,
    rate,
    accel,
    inner_vel,
    inner_acc,
    table_ref,
    pick,
    polar_back,
    squeeze,
    vel_next,
    acc_next,
    rate_next,
    accel_next,
    inner_vel_next,
    inner_acc_next,
    total,
    by_line,
    caps,
    narrow,
    wide,
):
    ypad = total.shape[1]
    narrow[...] = jnp.zeros(narrow.shape, jnp.float32)
    own = own_table(table_ref, count_y)
    turned = jnp.transpose(own)
    peers = CHUNK // SLOTS
    arrived = jnp.zeros((ENTRIES, 128), jnp.float32)
    for c in range(count_x * count_y // peers):
        number = (iota((ENTRIES, CHUNK), 1) + c * CHUNK).astype(jnp.float32)
        block = got_all[c * peers : (c + 1) * peers].reshape(CHUNK, 128)
        arrived = arrived + pick_left(chosen_by(turned[:, 2:3] == number), block)
    count = 64 + 4 * ypad
    points = pick_left(chosen_by(own[3:4, :] == iota((count, ENTRIES), 0).astype(jnp.float32)), arrived)
    lane = iota((32, 128), 1)
    upper = points[0:32]
    lower = points[32:64]
    for r in range(RADIAL):
        first = pltpu.roll(upper, (128 - STEP * r) % 128, axis=1) if r else upper
        second = pltpu.roll(lower, (64 - STEP * r) % 128, axis=1)
        block = jnp.where(lane < STEP, first, 0.0) + jnp.where(
            (lane >= 64) & (lane < 64 + STEP), second, 0.0
        )
        high, middle, last = (piece.astype(jnp.float32) for piece in parts_of(block))
        by_line[32 * r : 32 * r + 32, :] = (
            high + pltpu.roll(middle, 16, axis=1) + pltpu.roll(last, 32, axis=1)
        )
    lines = lax.dot_general(
        by_line[...].astype(bf16), pick[...], (((0,), (0,)), ((), ())), preferred_element_type=jnp.float32
    )
    lines_top = lines[0:16] + (lines[16:32] + lines[32:48])
    lines_bottom = lines[64:80] + (lines[80:96] + lines[96:112])
    caps[:, 0:128] = points[64 : 64 + 2 * ypad]
    caps[:, 128:256] = points[64 + 2 * ypad : 64 + 4 * ypad]
    columns = pick_right(caps[...], polar_back[...])

    xi = lax.axis_index("xi")
    eta = lax.axis_index("eta")
    even_x = lax.rem(xi, 2) == 0
    even_y = lax.rem(eta, 2) == 0
    lane = iota((16, PAD), 1)
    group = lax.rem(lane // RADIAL, GROUPS)
    used = lane < WIDTH
    ya = got_ya[...]
    yb = got_yb[...]
    from_above = jnp.where(even_y, ya, yb)
    from_below = jnp.where(even_y, yb, ya)
    four, five = 4 * RADIAL, 5 * RADIAL
    seam_top = jnp.where(
        group == 0,
        pltpu.roll(from_above, PAD - four, axis=1),
        jnp.where(group == 5, pltpu.roll(from_above, five, axis=1), 0.0),
    )
    seam_bottom = jnp.where(
        group == 4,
        pltpu.roll(from_below, four, axis=1),
        jnp.where(group == 0, pltpu.roll(from_below, PAD - five, axis=1), 0.0),
    )
    add_top = jnp.where(eta == count_y - 1, seam_top, from_above) + lines_top
    add_bottom = jnp.where(eta == 0, seam_bottom, from_below) + lines_bottom
    add_top = jnp.where(used, add_top, 0.0)
    add_bottom = jnp.where(used, add_bottom, 0.0)
    total[...] = fields[...]
    lane = iota((rows, 128), 1)
    inside = lax.rem(lane, 64)
    equator = inside < 4 * RADIAL
    keep = inside < COLUMN
    low = lane < 64
    last_x = xi == count_x - 1
    for p in range(PAIRS):
        xa = got_xa[p * rows : (p + 1) * rows, :]
        xb = got_xb[p * rows : (p + 1) * rows, :]
        from_right = jnp.where(even_x, xa, xb)
        from_left = jnp.where(even_x, xb, xa)
        up = jnp.where(
            inside < 3 * RADIAL,
            pltpu.roll(from_right, 128 - RADIAL, axis=1),
            pltpu.roll(from_right, 3 * RADIAL, axis=1),
        )
        down = jnp.where(
            inside < RADIAL,
            pltpu.roll(from_left, 128 - 3 * RADIAL, axis=1),
            pltpu.roll(from_left, RADIAL, axis=1),
        )
        from_right = jnp.where(last_x, jnp.where(equator, up, 0.0), from_right)
        from_left = jnp.where(xi == 0, jnp.where(equator, down, 0.0), from_left)
        at = slice(p * 128, p * 128 + 128)
        from_left = jnp.where(keep, from_left + columns[0:rows, at], 0.0)
        from_right = jnp.where(keep, from_right + columns[ypad : ypad + rows, at], 0.0)
        zero = jnp.zeros((rows, PAD - 128), jnp.float32)
        for h in range(2):
            f = 2 * p + h
            if f >= FIELDS:
                continue
            mine = low if h == 0 else ~low
            left = jnp.where(mine, from_left, 0.0)
            right = jnp.where(mine, from_right, 0.0)
            if h:
                left = pltpu.roll(left, 64, axis=1)
            total[f, 0:rows, 0:128] = total[f, 0:rows, 0:128] + left
            right = jnp.concatenate([right, zero], axis=1)
            right = pltpu.roll(right, WIDTH - COLUMN - 64 * h, axis=1)
            total[f, 0:rows, :] = total[f, 0:rows, :] + right
    for f in range(FIELDS):
        total[f, rows - 1 : rows, :] = total[f, rows - 1 : rows, :] + add_top[f : f + 1, :]
        total[f, 0:1, :] = total[f, 0:1, :] + add_bottom[f : f + 1, :]

    half = 0.5 * time_step
    lane = iota((ypad, PAD), 1)
    radial = lax.rem(lane, RADIAL)
    inside = (lane < WIDTH) & (iota((ypad, PAD), 0) < rows)
    core = total[CF] / jnp.where(inside, total[CM], 1.0)
    accel_next[...] = core[0:rows, 0:WIDTH]
    rate_next[...] = rate[...] + half * (accel[...] + core[0:rows, 0:WIDTH])
    push = total[CW] * core
    top = jnp.where(radial == 0, pltpu.roll(push, PAD - (RADIAL - 1), axis=1), 0.0)
    bottom = jnp.where(radial == INNER_RADIAL - 1, pltpu.roll(push, INNER_RADIAL - 1, axis=1), 0.0)
    mass = jnp.where(inside, total[MM], 1.0)
    inner_mass = jnp.where(inside & (radial < INNER_RADIAL), total[IM], 1.0)
    for f in range(3):
        force = total[f] + top if f == 2 else total[f]
        result = (force / mass)[0:rows]
        scatter(wide, f, result)
        force = total[IF + f] - bottom if f == 2 else total[IF + f]
        scatter(narrow, f, (force / inner_mass)[0:rows])
    squeezed = pick_right(jnp.concatenate([narrow[t] for t in range(PAD // 128)], axis=1), squeeze[...])
    for y in range(rows):
        result = jnp.concatenate([wide[t, 4 * y : 4 * y + 3, :] for t in range(PAD // 128)], axis=1)[:, 0:WIDTH]
        acc_next[y] = result
        vel_next[y] = vel[y] + half * (acc[y] + result)
        result = squeezed[4 * y : 4 * y + 3, :]
        inner_acc_next[y] = result
        inner_vel_next[y] = inner_vel[y] + half * (inner_acc[y] + result)


def shards(
    count_x,
    count_y,
    mantle_disp,
    mantle_vel,
    mantle_acc,
    mantle_metric,
    mantle_moduli,
    mantle_rho,
    core_pot,
    core_rate,
    core_accel,
    core_metric,
    core_kappa,
    core_rho,
    inner_disp,
    inner_vel,
    inner_acc,
    inner_metric,
    inner_moduli,
    inner_rho,
):
    rows = mantle_disp.shape[1]
    turn = lambda a: jnp.transpose(a, (1, 0, 2))
    mantle_disp, mantle_vel, mantle_acc = turn(mantle_disp), turn(mantle_vel), turn(mantle_acc)
    mantle_metric, mantle_moduli, core_metric = turn(mantle_metric), turn(mantle_moduli), turn(core_metric)
    inner_disp, inner_vel, inner_acc = turn(inner_disp), turn(inner_vel), turn(inner_acc)
    inner_metric, inner_moduli = turn(inner_metric), turn(inner_moduli)
    ne = (rows - 1) // 4
    ypad = -(-rows // 8) * 8
    tables = {name: jnp.asarray(value) for name, value in constants(rows).items()}
    table = jnp.asarray(exchange_tables(count_x, count_y, rows))
    f32 = jnp.float32
    like = lambda a: jax.ShapeDtypeStruct(a.shape, f32)
    shape = lambda *s: jax.ShapeDtypeStruct(s, f32)
    devices = count_x * count_y
    edge = -(-PAIRS * rows // 8) * 8
    (mantle_next, core_next, inner_next, fields, xa, xb, ya, yb, everyone) = pl.pallas_call(
        functools.partial(force_kernel, rows, count_x, count_y),
        out_shape=[
            like(mantle_disp),
            like(core_pot),
            like(inner_disp),
            shape(FIELDS, ypad, PAD),
            shape(edge, 128),
            shape(edge, 128),
            shape(16, PAD),
            shape(16, PAD),
            shape(devices, SLOTS, 128),
        ],
        scratch_shapes=[
            pltpu.VMEM((4 * ne * 8, WIDTH), f32),
            pltpu.VMEM((13 * ne * 8, WIDTH), f32),
            pltpu.VMEM((3 * ne * 8, INNER_WIDTH), f32),
            pltpu.VMEM((4 * ne * 8, 3 * PAD), f32),
            pltpu.VMEM((3 * ne * 8, 3 * INNER_PAD), f32),
            pltpu.VMEM((ypad, PAD), f32),
            pltpu.VMEM((2 * ypad, PAIRS * 128), f32),
            pltpu.VMEM((128, PAD), f32),
            pltpu.VMEM((64 + 4 * ypad, 128), f32),
        ]
        + [pltpu.VMEM((PAD // 128, 4 * rows, 128), f32)] * 4
        + [pltpu.VMEM((INNER_PAD // 128, 4 * rows, 128), f32)] * 3
        + [pltpu.VMEM((3 * ne * 8 + 2 * ypad, INNER_WIDTH), f32)],
        name="forces",
    )(
        mantle_disp,
        mantle_vel,
        mantle_acc,
        mantle_metric,
        mantle_moduli,
        mantle_rho,
        core_pot,
        core_rate,
        core_accel,
        core_metric,
        core_kappa,
        core_rho,
        inner_disp,
        inner_vel,
        inner_acc,
        inner_metric,
        inner_moduli,
        inner_rho,
        table,
        tables["table"],
        tables["plain"],
        tables["inner_table"],
        tables["spread"],
        tables["lanes"],
        tables["columns"],
        tables["along_y"],
        tables["pick"],
        tables["polar"],
    )
    everyone = lax.all_to_all(everyone, ("xi", "eta"), 0, 0, tiled=True)
    near = [(i, i ^ 1) for i in range(count_x)]
    far = [(i, (i - 1 if i % 2 == 0 else i + 1) % count_x) for i in range(count_x)]
    xa = lax.ppermute(xa, "xi", near)
    xb = lax.ppermute(xb, "xi", far)
    near = [(j, j ^ 1) for j in range(count_y)]
    far = [(j, (j - 1 if j % 2 == 0 else j + 1) % count_y) for j in range(count_y)]
    ya = lax.ppermute(ya, "eta", near)
    yb = lax.ppermute(yb, "eta", far)
    (mantle_vel_next, mantle_acc_next, core_rate_next, core_acc_next, inner_vel_next, inner_acc_next) = pl.pallas_call(
        functools.partial(close_kernel, rows, count_x, count_y),
        out_shape=[
            like(mantle_vel),
            like(mantle_acc),
            like(core_rate),
            like(core_accel),
            like(inner_vel),
            like(inner_acc),
        ],
        scratch_shapes=[
            pltpu.VMEM((FIELDS, ypad, PAD), f32),
            pltpu.VMEM((RADIAL * 32, 128), f32),
            pltpu.VMEM((2 * ypad, 256), f32),
            pltpu.VMEM((PAD // 128, -(-4 * rows // 16) * 16, 128), f32),
            pltpu.VMEM((PAD // 128, 4 * rows, 128), f32),
        ],
        name="close",
    )(
        xa,
        xb,
        ya,
        yb,
        everyone,
        fields,
        mantle_vel,
        mantle_acc,
        core_rate,
        core_accel,
        inner_vel,
        inner_acc,
        table,
        tables["pick"],
        tables["polar_back"],
        tables["squeeze"],
    )
    return (
        turn(mantle_next),
        turn(mantle_vel_next),
        turn(mantle_acc_next),
        core_next,
        core_rate_next,
        core_acc_next,
        turn(inner_next),
        turn(inner_vel_next),
        turn(inner_acc_next),
    )


def solution(mesh):
    count_x, count_y = mesh.shape["xi"], mesh.shape["eta"]
    assert count_x % 2 == 0 and count_y % 2 == 0
    assert (count_x * count_y * SLOTS) % CHUNK == 0
    vector, scalar = P(None, "eta", "xi"), P("eta", "xi")
    placed = (vector,) * 5 + (scalar,) * 4 + (vector,) + (scalar,) * 2 + (vector,) * 5 + (scalar,)
    return jax.shard_map(
        functools.partial(shards, count_x, count_y),
        mesh=mesh,
        in_specs=placed,
        out_specs=(vector,) * 3 + (scalar,) * 3 + (vector,) * 3,
        check_vma=False,
    )
```

```python
import collections
import functools
import math

import jax
import jax.numpy as jnp
import numpy as np
from jax import lax
from jax.experimental import pallas as pl
from jax.experimental.pallas import tpu as pltpu
from jax.sharding import PartitionSpec as P


EX = 1
MANTLE_LAYERS = 2
INNER_LAYERS = 1
GROUPS = 6
ACROSS = 4 * EX + 1
RADIAL = 4 * MANTLE_LAYERS + 1
INNER_RADIAL = 4 * INNER_LAYERS + 1
LINES = ACROSS * GROUPS
WIDTH = LINES * RADIAL
INNER_WIDTH = LINES * INNER_RADIAL
COLUMN = GROUPS * RADIAL
NODES = LINES * 5 * MANTLE_LAYERS
PAD = 384
INNER_PAD = 256
ENTRIES = 128
BLOCK = 8
RUN_ROWS = 3
RUN_POINTS = 5
RUNS = 2
CLASS = 24
time_step = 0.1

MM, CF, CM, IF, IM, CW, FIELDS = 3, 4, 5, 6, 9, 10, 11
PAIRS = 6
CHANNELS = 10 * INNER_RADIAL + 6 * (RADIAL - INNER_RADIAL) + 2


def channel(r, f):
    if f == CW:
        return {0: CHANNELS - 2, RADIAL - 1: CHANNELS - 1}.get(r)
    if r < INNER_RADIAL:
        return 10 * r + f
    return 10 * INNER_RADIAL + 6 * (r - INNER_RADIAL) + f if f < IF else None


def runs_of(r):
    out = [(0, IF if r >= INNER_RADIAL else CW, channel(r, 0))]
    if channel(r, CW) is not None:
        out.append((CW, FIELDS, channel(r, CW)))
    return out


def gll_tables():
    radical = math.sqrt(3.0 / 7.0)
    points = np.array([-1.0, -radical, 0.0, radical, 1.0])
    weights = np.array([0.1, 49.0 / 90.0, 32.0 / 45.0, 49.0 / 90.0, 0.1])
    products = np.array(
        [np.prod([points[a] - points[c] for c in range(5) if c != a]) for a in range(5)]
    )
    slopes = np.zeros((5, 5))
    for a in range(5):
        for b in range(5):
            if a == b:
                slopes[a, b] = np.sum([1.0 / (points[a] - points[c]) for c in range(5) if c != a])
            else:
                slopes[a, b] = products[a] / (products[b] * (points[a] - points[b]))
    return weights, slopes


def spread_table(count):
    spread = np.zeros((4 * count + 1, 5 * count))
    for element in range(count):
        for node in range(5):
            spread[4 * element + node, 5 * element + node] = 1.0
    return spread


def padded(table, width):
    return np.pad(table, ((0, 0), (0, width - table.shape[1])))


def lane_tables(layers, width):
    weights, slopes = gll_tables()
    spread = spread_table(layers)
    derive = np.kron(np.eye(layers), slopes.T)
    eye_k = np.eye(GROUPS)
    along_x = np.kron(slopes.T, np.kron(eye_k, spread))
    along_r = np.kron(np.eye(ACROSS), np.kron(eye_k, spread @ derive))
    plain = np.kron(np.eye(ACROSS), np.kron(eye_k, spread))
    node = np.kron(weights, np.kron(np.ones(GROUPS), np.tile(weights, layers)))
    lumped_r = spread @ np.tile(weights, layers)
    lumped = np.kron(weights, np.kron(np.ones(GROUPS), lumped_r))
    table = np.concatenate([padded(t, width) for t in (along_x, along_r, plain)], axis=1)
    return table.astype(np.float32), node.astype(np.float32), lumped.astype(np.float32)


def constants(rows_local):
    weights, slopes = gll_tables()
    count_y = (rows_local - 1) // 4
    ypad = -(-rows_local // 8) * 8
    table, node, lumped = lane_tables(MANTLE_LAYERS, PAD)
    inner_table, inner_node, inner_lumped = lane_tables(INNER_LAYERS, INNER_PAD)
    small = np.eye(RADIAL)[:INNER_RADIAL]
    spread = np.kron(np.eye(LINES), small)
    lumped_y = spread_table(count_y) @ np.tile(weights, count_y)
    lanes = np.zeros((8, PAD))
    lanes[0, :NODES] = node
    lanes[1, :WIDTH] = lumped
    lanes[2, :WIDTH] = np.kron(weights, np.ones(COLUMN))
    lanes[3, : INNER_WIDTH] = inner_node
    lanes[4, : INNER_WIDTH] = inner_lumped
    columns = np.zeros((ypad, 8))
    columns[:rows_local, 0] = lumped_y
    columns[:5, 1] = weights
    along_y = np.zeros((16, 8))
    along_y[:5, :5] = slopes
    along_y[8:13, :5] = slopes.T
    pick = np.zeros((RADIAL * 32, PAD))
    for r in range(RADIAL):
        for line in range(LINES):
            pick[r * 32 + line, line * RADIAL + r] = 1.0
    polar = np.zeros((PAIRS * 128, 256))
    for f in range(FIELDS):
        for k in (4, 5):
            for r in range(RADIAL):
                if channel(r, f) is not None:
                    polar[(f // 2) * 128 + (f % 2) * 64 + k * RADIAL + r, (k - 4) * 128 + channel(r, f)] = 1.0
    as_f32 = lambda t: np.asarray(t, np.float32)
    as_bf16 = lambda t: np.asarray(t, np.float32).astype(bf16)

    def split(t):
        rest = as_f32(t)
        out = []
        for _ in range(3):
            out.append(rest.astype(bf16))
            rest = rest - out[-1].astype(np.float32)
        return np.stack(out)

    return dict(
        table=split(table[:, : 2 * PAD]),
        plain=as_bf16(table[:, 2 * PAD :]),
        inner_table=split(inner_table[:, : 2 * INNER_PAD]),
        spread=as_bf16(padded(spread, PAD)),
        squeeze=as_bf16(np.pad(spread.T, ((0, PAD - WIDTH), (0, 0)))),
        lanes=as_f32(lanes),
        columns=as_f32(columns),
        along_y=as_f32(along_y),
        pick=as_bf16(pick),
        polar=as_bf16(polar),
        polar_back=as_bf16(polar.T),
    )


def exchange_tables(count_x, count_y, rows):
    reach_x, reach_y = ACROSS - 1, rows - 1
    side = count_x * reach_x
    ypad = -(-rows // 8) * 8

    def canonical(j, i, y, x, k):
        gy, gx = j * reach_y + y, i * reach_x + x
        if k < 4 and gx == side:
            k, gx = (k + 1) % 4, 0
        if k < 4 and gy == side:
            gx, gy = ((gx, 0), (side, gx), (side - gx, side), (0, side - gx))[k]
            k = 4
        elif k < 4 and gy == 0:
            gx, gy = ((gx, side), (side, side - gx), (side - gx, 0), (0, gx))[k]
            k = 5
        return k, gy, gx

    def swapped(source, target):
        sj, si, sy, sx, sk = source
        j, i, y, x, k = target
        if sj == j and sy == y:
            if (x, sx) == (reach_x, 0):
                if (si, sk) == (i + 1, k):
                    return True
                if i == count_x - 1 and si == 0 and k < 4 and sk == (k + 1) % 4:
                    return True
            if (x, sx) == (0, reach_x):
                if (si, sk) == (i - 1, k):
                    return True
                if i == 0 and si == count_x - 1 and k < 4 and sk == (k - 1) % 4:
                    return True
        if si == i and sx == x:
            if sk == k and (sj, sy, y) in ((j + 1, 0, reach_y), (j - 1, reach_y, 0)):
                return True
            if (j, y, sj, sy) == (0, 0, count_y - 1, reach_y) and (k, sk) in ((4, 0), (0, 5)):
                return True
            if (j, y, sj, sy) == (count_y - 1, reach_y, 0, 0) and (k, sk) in ((0, 4), (5, 0)):
                return True
        return False

    def row_of(y, x, k):
        if y == reach_y:
            return x * GROUPS + k
        if y == 0:
            return 32 + x * GROUPS + k
        return 64 + (k - 4) * 2 * ypad + (ypad if x else 0) + y

    copies = collections.defaultdict(list)
    for j in range(count_y):
        for i in range(count_x):
            for y in range(rows):
                for x in range(ACROSS):
                    if 0 < y < reach_y and 0 < x < reach_x:
                        continue
                    for k in range(GROUPS):
                        copies[canonical(j, i, y, x, k)].append((j, i, y, x, k))
    pairs = collections.defaultdict(list)
    for members in copies.values():
        for target in members:
            for source in members:
                if source != target and not swapped(source, target):
                    key = (source[1] * count_y + source[0], target[1] * count_y + target[0])
                    pairs[key].append((row_of(*source[2:]), row_of(*target[2:])))
    table = np.full((count_x * count_y, 8, ENTRIES), -1.0, np.float32)
    sent = collections.Counter()
    taken = collections.Counter()
    peers = count_x * count_y
    for (source, target), links in sorted(pairs.items()):
        assert len(links) <= RUNS * RUN_POINTS
        for slot, (row_from, row_to) in enumerate(sorted(links)):
            run, place = divmod(slot, RUN_POINTS)
            for device, peer, row, counts, base in (
                (source, target, row_from, sent, 0),
                (target, source, row_to, taken, 2),
            ):
                assert counts[device, place] < CLASS
                entry = place * CLASS + counts[device, place]
                counts[device, place] += 1
                table[device, base, entry] = run * peers + peer
                table[device, base + 1, entry] = row
    return table


bf16 = jnp.bfloat16


def parts_of(x):
    high = x.astype(bf16)
    rest = x - high.astype(jnp.float32)
    middle = rest.astype(bf16)
    return high, middle, (rest - middle.astype(jnp.float32)).astype(bf16)


def product(a, b, back=False):
    dims = (((1,), (1 if back else 0,)), ((), ()))
    return lax.dot_general(a, b, dims, preferred_element_type=jnp.float32)


def pick_right(x, chosen):
    count = x.shape[0]
    out = product(jnp.concatenate(parts_of(x), axis=0), chosen)
    return out[0:count] + out[count : 2 * count] + out[2 * count : 3 * count]


def pick_left(chosen, x):
    width = x.shape[1]
    out = product(chosen, jnp.concatenate(parts_of(x), axis=1))
    return out[:, 0:width] + out[:, width : 2 * width] + out[:, 2 * width : 3 * width]


def times(x, table, lanes, back=False):
    count = x.shape[0]
    high, middle, low = parts_of(x)
    out = product(jnp.concatenate([high, middle, low], axis=0), table[0, :, lanes], back)
    total = out[0:count] + (out[count : 2 * count] + out[2 * count : 3 * count])
    out = product(jnp.concatenate([high, middle], axis=0), table[1, :, lanes], back)
    total = total + (out[0:count] + out[count : 2 * count])
    return total + product(high, table[2, :, lanes], back)


def turn_lanes(x, shift):
    shift = shift % x.shape[1]
    return pltpu.roll(x, shift, axis=1) if shift else x


def chosen_by(condition):
    return jnp.where(condition, 1.0, 0.0).astype(bf16)


def iota(shape, axis):
    return lax.broadcasted_iota(jnp.int32, shape, axis)


def put(ref, row, block):
    for t in range(ref.shape[0]):
        width = min(128, block.shape[1] - 128 * t)
        ref[t, row : row + block.shape[0], 0:width] = block[:, 128 * t : 128 * t + width]


def take(ref, c, first, count):
    tiles = [ref[t, pl.ds(4 * first + c, count, stride=4), :] for t in range(ref.shape[0])]
    return jnp.concatenate(tiles, axis=1)


def scatter(ref, c, block):
    for t in range(ref.shape[0]):
        ref[t, pl.ds(c, block.shape[0], stride=4), :] = block[:, 128 * t : 128 * t + 128]


def own_table(table_ref, count_y):
    return table_ref[lax.axis_index("xi") * count_y + lax.axis_index("eta")]


def force_kernel(
    rows,
    count_x,
    count_y,
    disp,
    vel,
    acc,
    metric,
    moduli,
    rho,
    pot,
    rate,
    accel,
    core_metric,
    kappa,
    core_rho,
    inner_disp,
    inner_vel,
    inner_acc,
    inner_metric,
    inner_moduli,
    inner_rho,
    table_ref,
    forward,
    plain_lanes,
    inner_forward,
    spread,
    lanes,
    columns,
    along_y,
    pick,
    polar,
    disp_next,
    pot_next,
    inner_next,
    fields,
    send_xa,
    send_xb,
    send_ya,
    send_yb,
    send_all,
    wide,
    narrow,
    inner_rows,
    flux,
    inner_flux,
    wide_u,
    edges,
    rows_t,
    points,
    moved,
    scale,
    lame,
    core_scale,
    inner_moved,
    inner_scale,
    inner_lame,
    stack,
    shifted,
):
    ne = (rows - 1) // 4
    ypad = edges.shape[0] // 2
    half = 0.5 * time_step * time_step
    for y in range(rows):
        block = disp[y] + time_step * vel[y] + half * acc[y]
        disp_next[y] = block
        put(moved, 4 * y, block)
        put(scale, 4 * y, metric[y])
        put(lame, 4 * y, moduli[y])
        put(core_scale, 4 * y, core_metric[y])
        block = inner_disp[y] + time_step * inner_vel[y] + half * inner_acc[y]
        inner_next[y] = block
        put(inner_moved, 4 * y, block)
        put(inner_scale, 4 * y, inner_metric[y])
        put(inner_lame, 4 * y, inner_moduli[y])

    def part(ref, c, first=0, count=rows):
        width = WIDTH if ref.shape[0] * 128 == PAD else INNER_WIDTH
        return take(ref, c, first, count)[:, 0:width]

    pot_next[...] = pot[...] + time_step * rate[...] + half * accel[...]

    slope = along_y[0:5, 0:5]
    slope_back = along_y[8:13, 0:5]

    def along(matrix, block):
        total = matrix[:, 0:1] * block[0:1, :]
        for b in range(1, 5):
            total = total + matrix[:, b : b + 1] * block[b : b + 1, :]
        return total

    wide[...] = jnp.zeros(wide.shape, jnp.float32)
    narrow[...] = jnp.zeros(narrow.shape, jnp.float32)
    inner_rows[...] = jnp.zeros(inner_rows.shape, jnp.float32)
    flux[...] = jnp.zeros(flux.shape, jnp.float32)
    inner_flux[...] = jnp.zeros(inner_flux.shape, jnp.float32)
    stack[...] = jnp.zeros(stack.shape, jnp.float32)
    fields[...] = jnp.zeros(fields.shape, jnp.float32)

    def slot(f, e):
        return (f * ne + e) * 8

    extras = [(scale, c) for c in range(3)] + [(lame, c) for c in range(2)] + [(core_scale, c) for c in range(3)]
    for e in range(ne):
        for f in range(4):
            block = part(moved, f, 4 * e, 5) if f < 3 else pot_next[4 * e : 4 * e + 5, :]
            wide[slot(f, e) : slot(f, e) + 5, :] = block
            narrow[slot(f, e) : slot(f, e) + 5, :] = along(slope, block)
        for f, (ref, c) in enumerate(extras):
            narrow[slot(4 + f, e) : slot(4 + f, e) + 5, :] = part(ref, c, 4 * e, 5)
        narrow[slot(12, e) : slot(12, e) + 5, :] = core_rho[4 * e : 4 * e + 5, :]
        for f in range(3):
            inner_rows[slot(f, e) : slot(f, e) + 5, :] = part(inner_moved, f, 4 * e, 5)
    whole = slice(None)
    slopes_xr = times(wide[...], forward, whole)
    copies = pick_right(narrow[...], plain_lanes[...])
    inner_xr = times(inner_rows[...], inner_forward, whole)

    def elastic(g, lam, mu, sy, sx, sr, jw):
        scaled = [[sy[i] * g[0], sx[i] * g[1], sr[i] * g[2]] for i in range(3)]
        trace = lam * (scaled[0][0] + scaled[1][1] + scaled[2][2])
        out = [[None] * 3 for _ in range(3)]
        weighted = [jw * g[m] for m in range(3)]
        for i in range(3):
            for m in range(3):
                if i == m:
                    stress = 2.0 * mu * scaled[i][i] + trace
                else:
                    stress = mu * (scaled[i][m] + scaled[m][i])
                out[i][m] = stress * weighted[m]
        return out

    row_weight = columns[0:5, 1:2]
    valid = (iota((5, PAD), 1) < NODES) & (iota((5, PAD), 0) < 5)
    for e in range(ne):
        def plain(f):
            return copies[slot(f, e) : slot(f, e) + 5, :]

        def x_of(f):
            return slopes_xr[slot(f, e) : slot(f, e) + 5, 0:PAD]

        def r_of(f):
            return slopes_xr[slot(f, e) : slot(f, e) + 5, PAD : 2 * PAD]

        node = row_weight * lanes[0:1, :]
        g = [jnp.where(valid, plain(4 + m), 1.0) for m in range(3)]
        q = elastic(
            g,
            plain(7),
            plain(8),
            [plain(f) for f in range(3)],
            [x_of(f) for f in range(3)],
            [r_of(f) for f in range(3)],
            node / (g[0] * g[1] * g[2]),
        )
        g = [jnp.where(valid, plain(9 + m), 1.0) for m in range(3)]
        volume = node / (g[0] * g[1] * g[2] * jnp.where(valid, plain(12), 1.0))
        q.append(
            [
                volume * g[0] * g[0] * plain(3),
                volume * g[1] * g[1] * x_of(3),
                volume * g[2] * g[2] * r_of(3),
            ]
        )
        for f in range(4):
            at = slot(f, e)
            flux[at : at + 5, 0:PAD] = q[f][1]
            flux[at : at + 5, PAD : 2 * PAD] = q[f][2]
            flux[at : at + 5, 2 * PAD : 3 * PAD] = along(slope_back, q[f][0])

        def inner_x(f):
            return inner_xr[slot(f, e) : slot(f, e) + 5, 0:INNER_WIDTH]

        def inner_r(f):
            return inner_xr[slot(f, e) : slot(f, e) + 5, INNER_PAD : INNER_PAD + INNER_WIDTH]

        g = [part(inner_scale, m, 4 * e, 5) for m in range(3)]
        node = row_weight * lanes[3:4, 0:INNER_WIDTH]
        q = elastic(
            g,
            part(inner_lame, 0, 4 * e, 5),
            part(inner_lame, 1, 4 * e, 5),
            [along(slope, inner_rows[slot(f, e) : slot(f, e) + 5, :]) for f in range(3)],
            [inner_x(f) for f in range(3)],
            [inner_r(f) for f in range(3)],
            node / (g[0] * g[1] * g[2]),
        )
        for f in range(3):
            at = slot(f, e)
            inner_flux[at : at + 5, 0:INNER_WIDTH] = q[f][1]
            inner_flux[at : at + 5, INNER_PAD : INNER_PAD + INNER_WIDTH] = q[f][2]
            inner_flux[at : at + 5, 2 * INNER_PAD : 2 * INNER_PAD + INNER_WIDTH] = along(slope_back, q[f][0])

    back = times(flux[:, 0 : 2 * PAD], forward, whole, back=True)
    own_y = flux[:, 2 * PAD : 3 * PAD]
    count = own_y.shape[0]
    out = product(jnp.concatenate(parts_of(own_y), axis=0), plain_lanes[...], back=True)
    back = back + (out[0:count] + out[count : 2 * count] + out[2 * count : 3 * count])
    count = 3 * ne * 8
    stack[0:count, :] = (
        times(inner_flux[:, 0 : 2 * INNER_PAD], inner_forward, whole, back=True)
        + inner_flux[:, 2 * INNER_PAD : 2 * INNER_PAD + INNER_WIDTH]
    )
    lumped_y = columns[0:rows, 0:1]
    stack[count : count + rows, :] = inner_rho[...] * (
        lumped_y * lanes[4:5, 0:INNER_WIDTH] / (part(inner_scale, 0) * part(inner_scale, 1) * part(inner_scale, 2))
    )
    stack[count + ypad : count + ypad + rows, :] = part(inner_moved, 2)
    spreads = pick_right(stack[...], spread[...])
    inner_forces = spreads[0:count, 0:WIDTH]
    for e in range(ne):
        here = slice(4 * e, 4 * e + 5)
        for f in range(3):
            fields[f, here, 0:WIDTH] = fields[f, here, 0:WIDTH] - back[slot(f, e) : slot(f, e) + 5, :]
            fields[IF + f, here, 0:WIDTH] = fields[IF + f, here, 0:WIDTH] - inner_forces[slot(f, e) : slot(f, e) + 5, :]
        fields[CF, here, 0:WIDTH] = fields[CF, here, 0:WIDTH] - back[slot(3, e) : slot(3, e) + 5, :]

    lumped = lumped_y * lanes[1:2, 0:WIDTH]
    fields[MM, 0:rows, 0:WIDTH] = rho[...] * (lumped / (part(scale, 0) * part(scale, 1) * part(scale, 2)))
    fields[CM, 0:rows, 0:WIDTH] = lumped / (part(core_scale, 0) * part(core_scale, 1) * part(core_scale, 2)) / kappa[...]
    fields[IM, 0:rows, :] = spreads[count : count + rows]
    radial = lax.rem(iota((rows, WIDTH), 1), RADIAL)
    face = lumped_y * lanes[2:3, 0:WIDTH] / (part(core_scale, 0) * part(core_scale, 1))
    face = jnp.where((radial == 0) | (radial == RADIAL - 1), face, 0.0)
    fields[CW, 0:rows, 0:WIDTH] = face
    wide_u[...] = jnp.zeros(wide_u.shape, jnp.float32)
    wide_u[0:rows, 0:WIDTH] = part(moved, 2)
    above = pltpu.roll(wide_u[...], RADIAL - 1, axis=1)
    below = pltpu.roll(spreads[count + ypad : count + 2 * ypad], PAD - (INNER_RADIAL - 1), axis=1)
    radial = lax.rem(iota((ypad, PAD), 1), RADIAL)
    jump = jnp.where(radial == RADIAL - 1, above, jnp.where(radial == 0, -below, 0.0))
    fields[CF] = fields[CF] + fields[CW] * jump

    low = iota((ypad, 128), 1) < 64
    for p in range(PAIRS):
        left = fields[2 * p]
        right = fields[2 * p + 1] if 2 * p + 1 < FIELDS else jnp.zeros_like(left)
        edges[0:ypad, p * 128 : p * 128 + 128] = jnp.where(low, left[:, 0:128], pltpu.roll(right[:, 0:128], 64, axis=1))
        edges[ypad : 2 * ypad, p * 128 : p * 128 + 128] = jnp.where(
            low,
            pltpu.roll(left, PAD - (WIDTH - COLUMN), axis=1)[:, 0:128],
            pltpu.roll(right, PAD + 64 - (WIDTH - COLUMN), axis=1)[:, 0:128],
        )
    even_x = lax.rem(lax.axis_index("xi"), 2) == 0
    even_y = lax.rem(lax.axis_index("eta"), 2) == 0
    for p in range(PAIRS):
        first = edges[0:rows, p * 128 : p * 128 + 128]
        last = edges[ypad : ypad + rows, p * 128 : p * 128 + 128]
        send_xa[p * rows : (p + 1) * rows, :] = jnp.where(even_x, last, first)
        send_xb[p * rows : (p + 1) * rows, :] = jnp.where(even_x, first, last)
    rows_t[...] = jnp.zeros(rows_t.shape, jnp.float32)
    for f in range(FIELDS):
        rows_t[f : f + 1, :] = fields[f, rows - 1 : rows, :]
        rows_t[64 + f : 65 + f, :] = fields[f, 0:1, :]
    top = rows_t[0:16, :]
    bottom = rows_t[64:80, :]
    send_ya[...] = jnp.where(even_y, top, bottom)
    send_yb[...] = jnp.where(even_y, bottom, top)

    for at, block in ((0, top), (64, bottom)):
        for n, piece in enumerate(parts_of(block)):
            rows_t[at + 16 * n : at + 16 * n + 16, :] = piece.astype(jnp.float32)
    by_line = product(pick[...], rows_t[...].astype(bf16), back=True)
    by_line = by_line + (pltpu.roll(by_line, 128 - 16, axis=1) + pltpu.roll(by_line, 128 - 32, axis=1))
    lane = iota((32, 128), 1)
    top_points = jnp.zeros((32, 128), jnp.float32)
    bottom_points = jnp.zeros((32, 128), jnp.float32)
    for r in range(RADIAL):
        block = by_line[32 * r : 32 * r + 32, :]
        for first, end, at in runs_of(r):
            upper = jnp.where((lane >= first) & (lane < end), block, 0.0)
            lower = jnp.where((lane >= 64 + first) & (lane < 64 + end), block, 0.0)
            top_points = top_points + turn_lanes(upper, at - first)
            bottom_points = bottom_points + turn_lanes(lower, at - first - 64)
    points[0:32, :] = top_points
    points[32:64, :] = bottom_points
    caps = pick_right(edges[...], polar[...])
    points[64 : 64 + 2 * ypad, :] = caps[:, 0:128]
    points[64 + 2 * ypad : 64 + 4 * ypad, :] = caps[:, 128:256]

    own = own_table(table_ref, count_y)
    turned = jnp.transpose(own)
    count = points.shape[0]
    chosen = chosen_by(turned[:, 1:2] == iota((ENTRIES, count), 1).astype(jnp.float32))
    chosen = pick_left(chosen, points[...])
    shifted[...] = jnp.zeros(shifted.shape, jnp.float32)
    lane = iota((CLASS, 128), 1)
    for place in range(RUN_POINTS):
        tile, shift = divmod(place * CHANNELS, 128)
        here = slice(place * CLASS, (place + 1) * CLASS)
        block = turn_lanes(chosen[here], shift)
        shifted[here, tile * 128 : tile * 128 + 128] = jnp.where(lane >= shift, block, 0.0)
        if shift + CHANNELS > 128:
            shifted[here, tile * 128 + 128 : tile * 128 + 256] = jnp.where(lane < shift, block, 0.0)
    peers = count_x * count_y
    number = iota((RUNS * peers, ENTRIES), 0).astype(jnp.float32)
    placed = pick_left(chosen_by(own[0:1, :] == number), shifted[...])
    for row in range(BLOCK):
        run, tile = divmod(row, RUN_ROWS)
        if run < RUNS:
            block = placed[run * peers : (run + 1) * peers, tile * 128 : tile * 128 + 128]
        else:
            block = jnp.zeros((peers, 128), jnp.float32)
        send_all[pl.ds(row, peers, stride=BLOCK), :] = block


def close_kernel(
    rows,
    count_x,
    count_y,
    got_xa,
    got_xb,
    got_ya,
    got_yb,
    got_all,
    fields,
    vel,
    acc,
    rate,
    accel,
    inner_vel,
    inner_acc,
    table_ref,
    pick,
    polar_back,
    squeeze,
    vel_next,
    acc_next,
    rate_next,
    accel_next,
    inner_vel_next,
    inner_acc_next,
    total,
    by_line,
    caps,
    narrow,
    wide,
    runs,
    arrived,
):
    ypad = total.shape[1]
    narrow[...] = jnp.zeros(narrow.shape, jnp.float32)
    own = own_table(table_ref, count_y)
    turned = jnp.transpose(own)
    peers = count_x * count_y
    for run in range(RUNS):
        for tile in range(RUN_ROWS):
            runs[run * peers : (run + 1) * peers, tile * 128 : tile * 128 + 128] = got_all[
                pl.ds(run * RUN_ROWS + tile, peers, stride=BLOCK), :
            ]
    number = iota((ENTRIES, RUNS * peers), 1).astype(jnp.float32)
    shifted = pick_left(chosen_by(turned[:, 2:3] == number), runs[...])
    lane = iota((CLASS, 128), 1)
    arrived[...] = jnp.zeros(arrived.shape, jnp.float32)
    for place in range(RUN_POINTS):
        tile, shift = divmod(place * CHANNELS, 128)
        here = slice(place * CLASS, (place + 1) * CLASS)
        block = shifted[here, tile * 128 : tile * 128 + 128]
        if shift + CHANNELS > 128:
            block = jnp.where(lane >= shift, block, shifted[here, tile * 128 + 128 : tile * 128 + 256])
        arrived[here, :] = jnp.where(lane < CHANNELS, turn_lanes(block, -shift), 0.0)
    count = 64 + 4 * ypad
    points = pick_left(chosen_by(own[3:4, :] == iota((count, ENTRIES), 0).astype(jnp.float32)), arrived[...])
    lane = iota((32, 128), 1)
    upper = points[0:32]
    lower = points[32:64]
    for r in range(RADIAL):
        block = jnp.zeros((32, 128), jnp.float32)
        for first, end, at in runs_of(r):
            high = turn_lanes(upper, first - at)
            low = turn_lanes(lower, 64 + first - at)
            block = jnp.where((lane >= first) & (lane < end), high, block)
            block = jnp.where((lane >= 64 + first) & (lane < 64 + end), low, block)
        high, middle, last = (piece.astype(jnp.float32) for piece in parts_of(block))
        by_line[32 * r : 32 * r + 32, :] = (
            high + pltpu.roll(middle, 16, axis=1) + pltpu.roll(last, 32, axis=1)
        )
    lines = lax.dot_general(
        by_line[...].astype(bf16), pick[...], (((0,), (0,)), ((), ())), preferred_element_type=jnp.float32
    )
    lines_top = lines[0:16] + (lines[16:32] + lines[32:48])
    lines_bottom = lines[64:80] + (lines[80:96] + lines[96:112])
    caps[:, 0:128] = points[64 : 64 + 2 * ypad]
    caps[:, 128:256] = points[64 + 2 * ypad : 64 + 4 * ypad]
    columns = pick_right(caps[...], polar_back[...])

    xi = lax.axis_index("xi")
    eta = lax.axis_index("eta")
    even_x = lax.rem(xi, 2) == 0
    even_y = lax.rem(eta, 2) == 0
    lane = iota((16, PAD), 1)
    group = lax.rem(lane // RADIAL, GROUPS)
    used = lane < WIDTH
    ya = got_ya[...]
    yb = got_yb[...]
    from_above = jnp.where(even_y, ya, yb)
    from_below = jnp.where(even_y, yb, ya)
    four, five = 4 * RADIAL, 5 * RADIAL
    seam_top = jnp.where(
        group == 0,
        pltpu.roll(from_above, PAD - four, axis=1),
        jnp.where(group == 5, pltpu.roll(from_above, five, axis=1), 0.0),
    )
    seam_bottom = jnp.where(
        group == 4,
        pltpu.roll(from_below, four, axis=1),
        jnp.where(group == 0, pltpu.roll(from_below, PAD - five, axis=1), 0.0),
    )
    add_top = jnp.where(eta == count_y - 1, seam_top, from_above) + lines_top
    add_bottom = jnp.where(eta == 0, seam_bottom, from_below) + lines_bottom
    add_top = jnp.where(used, add_top, 0.0)
    add_bottom = jnp.where(used, add_bottom, 0.0)
    total[...] = fields[...]
    lane = iota((rows, 128), 1)
    inside = lax.rem(lane, 64)
    equator = inside < 4 * RADIAL
    keep = inside < COLUMN
    low = lane < 64
    last_x = xi == count_x - 1
    for p in range(PAIRS):
        xa = got_xa[p * rows : (p + 1) * rows, :]
        xb = got_xb[p * rows : (p + 1) * rows, :]
        from_right = jnp.where(even_x, xa, xb)
        from_left = jnp.where(even_x, xb, xa)
        up = jnp.where(
            inside < 3 * RADIAL,
            pltpu.roll(from_right, 128 - RADIAL, axis=1),
            pltpu.roll(from_right, 3 * RADIAL, axis=1),
        )
        down = jnp.where(
            inside < RADIAL,
            pltpu.roll(from_left, 128 - 3 * RADIAL, axis=1),
            pltpu.roll(from_left, RADIAL, axis=1),
        )
        from_right = jnp.where(last_x, jnp.where(equator, up, 0.0), from_right)
        from_left = jnp.where(xi == 0, jnp.where(equator, down, 0.0), from_left)
        at = slice(p * 128, p * 128 + 128)
        from_left = jnp.where(keep, from_left + columns[0:rows, at], 0.0)
        from_right = jnp.where(keep, from_right + columns[ypad : ypad + rows, at], 0.0)
        zero = jnp.zeros((rows, PAD - 128), jnp.float32)
        for h in range(2):
            f = 2 * p + h
            if f >= FIELDS:
                continue
            mine = low if h == 0 else ~low
            left = jnp.where(mine, from_left, 0.0)
            right = jnp.where(mine, from_right, 0.0)
            if h:
                left = pltpu.roll(left, 64, axis=1)
            total[f, 0:rows, 0:128] = total[f, 0:rows, 0:128] + left
            right = jnp.concatenate([right, zero], axis=1)
            right = pltpu.roll(right, WIDTH - COLUMN - 64 * h, axis=1)
            total[f, 0:rows, :] = total[f, 0:rows, :] + right
    for f in range(FIELDS):
        total[f, rows - 1 : rows, :] = total[f, rows - 1 : rows, :] + add_top[f : f + 1, :]
        total[f, 0:1, :] = total[f, 0:1, :] + add_bottom[f : f + 1, :]

    half = 0.5 * time_step
    lane = iota((ypad, PAD), 1)
    radial = lax.rem(lane, RADIAL)
    inside = (lane < WIDTH) & (iota((ypad, PAD), 0) < rows)
    core = total[CF] / jnp.where(inside, total[CM], 1.0)
    accel_next[...] = core[0:rows, 0:WIDTH]
    rate_next[...] = rate[...] + half * (accel[...] + core[0:rows, 0:WIDTH])
    push = total[CW] * core
    top = jnp.where(radial == 0, pltpu.roll(push, PAD - (RADIAL - 1), axis=1), 0.0)
    bottom = jnp.where(radial == INNER_RADIAL - 1, pltpu.roll(push, INNER_RADIAL - 1, axis=1), 0.0)
    mass = jnp.where(inside, total[MM], 1.0)
    inner_mass = jnp.where(inside & (radial < INNER_RADIAL), total[IM], 1.0)
    for f in range(3):
        force = total[f] + top if f == 2 else total[f]
        result = (force / mass)[0:rows]
        scatter(wide, f, result)
        force = total[IF + f] - bottom if f == 2 else total[IF + f]
        scatter(narrow, f, (force / inner_mass)[0:rows])
    squeezed = pick_right(jnp.concatenate([narrow[t] for t in range(PAD // 128)], axis=1), squeeze[...])
    for y in range(rows):
        result = jnp.concatenate([wide[t, 4 * y : 4 * y + 3, :] for t in range(PAD // 128)], axis=1)[:, 0:WIDTH]
        acc_next[y] = result
        vel_next[y] = vel[y] + half * (acc[y] + result)
        result = squeezed[4 * y : 4 * y + 3, :]
        inner_acc_next[y] = result
        inner_vel_next[y] = inner_vel[y] + half * (inner_acc[y] + result)


def shards(
    count_x,
    count_y,
    mantle_disp,
    mantle_vel,
    mantle_acc,
    mantle_metric,
    mantle_moduli,
    mantle_rho,
    core_pot,
    core_rate,
    core_accel,
    core_metric,
    core_kappa,
    core_rho,
    inner_disp,
    inner_vel,
    inner_acc,
    inner_metric,
    inner_moduli,
    inner_rho,
):
    rows = mantle_disp.shape[1]
    turn = lambda a: jnp.transpose(a, (1, 0, 2))
    mantle_disp, mantle_vel, mantle_acc = turn(mantle_disp), turn(mantle_vel), turn(mantle_acc)
    mantle_metric, mantle_moduli, core_metric = turn(mantle_metric), turn(mantle_moduli), turn(core_metric)
    inner_disp, inner_vel, inner_acc = turn(inner_disp), turn(inner_vel), turn(inner_acc)
    inner_metric, inner_moduli = turn(inner_metric), turn(inner_moduli)
    ne = (rows - 1) // 4
    ypad = -(-rows // 8) * 8
    tables = {name: jnp.asarray(value) for name, value in constants(rows).items()}
    table = jnp.asarray(exchange_tables(count_x, count_y, rows))
    f32 = jnp.float32
    like = lambda a: jax.ShapeDtypeStruct(a.shape, f32)
    shape = lambda *s: jax.ShapeDtypeStruct(s, f32)
    devices = count_x * count_y
    edge = -(-PAIRS * rows // 8) * 8
    (mantle_next, core_next, inner_next, fields, xa, xb, ya, yb, everyone) = pl.pallas_call(
        functools.partial(force_kernel, rows, count_x, count_y),
        out_shape=[
            like(mantle_disp),
            like(core_pot),
            like(inner_disp),
            shape(FIELDS, ypad, PAD),
            shape(edge, 128),
            shape(edge, 128),
            shape(16, PAD),
            shape(16, PAD),
            shape(devices * BLOCK, 128),
        ],
        scratch_shapes=[
            pltpu.VMEM((4 * ne * 8, WIDTH), f32),
            pltpu.VMEM((13 * ne * 8, WIDTH), f32),
            pltpu.VMEM((3 * ne * 8, INNER_WIDTH), f32),
            pltpu.VMEM((4 * ne * 8, 3 * PAD), f32),
            pltpu.VMEM((3 * ne * 8, 3 * INNER_PAD), f32),
            pltpu.VMEM((ypad, PAD), f32),
            pltpu.VMEM((2 * ypad, PAIRS * 128), f32),
            pltpu.VMEM((128, PAD), f32),
            pltpu.VMEM((64 + 4 * ypad, 128), f32),
        ]
        + [pltpu.VMEM((PAD // 128, 4 * rows, 128), f32)] * 4
        + [pltpu.VMEM((INNER_PAD // 128, 4 * rows, 128), f32)] * 3
        + [pltpu.VMEM((3 * ne * 8 + 2 * ypad, INNER_WIDTH), f32)]
        + [pltpu.VMEM((ENTRIES, RUN_ROWS * 128), f32)],
        name="forces",
    )(
        mantle_disp,
        mantle_vel,
        mantle_acc,
        mantle_metric,
        mantle_moduli,
        mantle_rho,
        core_pot,
        core_rate,
        core_accel,
        core_metric,
        core_kappa,
        core_rho,
        inner_disp,
        inner_vel,
        inner_acc,
        inner_metric,
        inner_moduli,
        inner_rho,
        table,
        tables["table"],
        tables["plain"],
        tables["inner_table"],
        tables["spread"],
        tables["lanes"],
        tables["columns"],
        tables["along_y"],
        tables["pick"],
        tables["polar"],
    )
    everyone = lax.all_to_all(everyone, ("xi", "eta"), 0, 0, tiled=True)
    near = [(i, i ^ 1) for i in range(count_x)]
    far = [(i, (i - 1 if i % 2 == 0 else i + 1) % count_x) for i in range(count_x)]
    xa = lax.ppermute(xa, "xi", near)
    xb = lax.ppermute(xb, "xi", far)
    near = [(j, j ^ 1) for j in range(count_y)]
    far = [(j, (j - 1 if j % 2 == 0 else j + 1) % count_y) for j in range(count_y)]
    ya = lax.ppermute(ya, "eta", near)
    yb = lax.ppermute(yb, "eta", far)
    (mantle_vel_next, mantle_acc_next, core_rate_next, core_acc_next, inner_vel_next, inner_acc_next) = pl.pallas_call(
        functools.partial(close_kernel, rows, count_x, count_y),
        out_shape=[
            like(mantle_vel),
            like(mantle_acc),
            like(core_rate),
            like(core_accel),
            like(inner_vel),
            like(inner_acc),
        ],
        scratch_shapes=[
            pltpu.VMEM((FIELDS, ypad, PAD), f32),
            pltpu.VMEM((RADIAL * 32, 128), f32),
            pltpu.VMEM((2 * ypad, 256), f32),
            pltpu.VMEM((PAD // 128, -(-4 * rows // 16) * 16, 128), f32),
            pltpu.VMEM((PAD // 128, 4 * rows, 128), f32),
            pltpu.VMEM((RUNS * devices, RUN_ROWS * 128), f32),
            pltpu.VMEM((ENTRIES, 128), f32),
        ],
        compiler_params=pltpu.CompilerParams(vmem_limit_bytes=(8 << 20) + devices * (48 << 10)),
        name="close",
    )(
        xa,
        xb,
        ya,
        yb,
        everyone,
        fields,
        mantle_vel,
        mantle_acc,
        core_rate,
        core_accel,
        inner_vel,
        inner_acc,
        table,
        tables["pick"],
        tables["polar_back"],
        tables["squeeze"],
    )
    return (
        turn(mantle_next),
        turn(mantle_vel_next),
        turn(mantle_acc_next),
        core_next,
        core_rate_next,
        core_acc_next,
        turn(inner_next),
        turn(inner_vel_next),
        turn(inner_acc_next),
    )


def solution(mesh):
    count_x, count_y = mesh.shape["xi"], mesh.shape["eta"]
    assert count_x % 2 == 0 and count_y % 2 == 0
    assert (count_x * count_y) % 8 == 0
    vector, scalar = P(None, "eta", "xi"), P("eta", "xi")
    placed = (vector,) * 5 + (scalar,) * 4 + (vector,) + (scalar,) * 2 + (vector,) * 5 + (scalar,)
    return jax.shard_map(
        functools.partial(shards, count_x, count_y),
        mesh=mesh,
        in_specs=placed,
        out_specs=(vector,) * 3 + (scalar,) * 3 + (vector,) * 3,
        check_vma=False,
    )
```

```python
import collections
import functools
import math

import jax
import jax.numpy as jnp
import numpy as np
from jax import lax
from jax.experimental import pallas as pl
from jax.experimental.pallas import tpu as pltpu
from jax.sharding import PartitionSpec as P


EX = 1
MANTLE_LAYERS = 2
INNER_LAYERS = 1
GROUPS = 6
ACROSS = 4 * EX + 1
RADIAL = 4 * MANTLE_LAYERS + 1
INNER_RADIAL = 4 * INNER_LAYERS + 1
LINES = ACROSS * GROUPS
WIDTH = LINES * RADIAL
INNER_WIDTH = LINES * INNER_RADIAL
COLUMN = GROUPS * RADIAL
NODES = LINES * 5 * MANTLE_LAYERS
PAD = 384
INNER_PAD = 256
TILE = 256
ENTRIES = 128
BLOCK = 8
RUN_ROWS = 3
RUN_POINTS = 5
RUNS = 2
CLASS = 24
WINDOW_GRANT = 8 << 20
time_step = 0.1

MM, CF, CM, IF, IM, CW, FIELDS = 3, 4, 5, 6, 9, 10, 11
PAIRS = 6
CHANNELS = 10 * INNER_RADIAL + 6 * (RADIAL - INNER_RADIAL) + 2


def channel(r, f):
    if f == CW:
        return {0: CHANNELS - 2, RADIAL - 1: CHANNELS - 1}.get(r)
    if r < INNER_RADIAL:
        return 10 * r + f
    return 10 * INNER_RADIAL + 6 * (r - INNER_RADIAL) + f if f < IF else None


def runs_of(r):
    out = [(0, IF if r >= INNER_RADIAL else CW, channel(r, 0))]
    if channel(r, CW) is not None:
        out.append((CW, FIELDS, channel(r, CW)))
    return out


def gll_tables():
    radical = math.sqrt(3.0 / 7.0)
    points = np.array([-1.0, -radical, 0.0, radical, 1.0])
    weights = np.array([0.1, 49.0 / 90.0, 32.0 / 45.0, 49.0 / 90.0, 0.1])
    products = np.array(
        [np.prod([points[a] - points[c] for c in range(5) if c != a]) for a in range(5)]
    )
    slopes = np.zeros((5, 5))
    for a in range(5):
        for b in range(5):
            if a == b:
                slopes[a, b] = np.sum([1.0 / (points[a] - points[c]) for c in range(5) if c != a])
            else:
                slopes[a, b] = products[a] / (products[b] * (points[a] - points[b]))
    return weights, slopes


def spread_table(count):
    spread = np.zeros((4 * count + 1, 5 * count))
    for element in range(count):
        for node in range(5):
            spread[4 * element + node, 5 * element + node] = 1.0
    return spread


def padded(table, width):
    return np.pad(table, ((0, 0), (0, width - table.shape[1])))


def lane_tables(layers, width):
    weights, slopes = gll_tables()
    spread = spread_table(layers)
    derive = np.kron(np.eye(layers), slopes.T)
    eye_k = np.eye(GROUPS)
    along_x = np.kron(slopes.T, np.kron(eye_k, spread))
    along_r = np.kron(np.eye(ACROSS), np.kron(eye_k, spread @ derive))
    plain = np.kron(np.eye(ACROSS), np.kron(eye_k, spread))
    node = np.kron(weights, np.kron(np.ones(GROUPS), np.tile(weights, layers)))
    lumped_r = spread @ np.tile(weights, layers)
    lumped = np.kron(weights, np.kron(np.ones(GROUPS), lumped_r))
    order = node_order(layers)
    node = node[order]
    table = np.concatenate([padded(t[:, order], width) for t in (along_x, along_r, plain)], axis=1)
    return table.astype(np.float32), node.astype(np.float32), lumped.astype(np.float32)


def node_order(layers):
    radial = [max(0, (r - 1) // 4) for r in range(4 * layers + 1)]
    plain = [line * 5 * layers + 5 * e + r - 4 * e for line in range(LINES) for r, e in enumerate(radial)]
    return plain + [line * 5 * layers + 5 * e for e in range(1, layers) for line in range(LINES)]


def constants(rows_local):
    weights, slopes = gll_tables()
    count_y = (rows_local - 1) // 4
    ypad = -(-rows_local // 8) * 8
    table, node, lumped = lane_tables(MANTLE_LAYERS, PAD)
    inner_table, inner_node, inner_lumped = lane_tables(INNER_LAYERS, INNER_PAD)
    small = np.eye(RADIAL)[:INNER_RADIAL]
    spread = np.kron(np.eye(LINES), small)
    lumped_y = spread_table(count_y) @ np.tile(weights, count_y)
    lanes = np.zeros((8, PAD))
    lanes[0, :NODES] = node
    lanes[1, :WIDTH] = lumped
    lanes[2, :WIDTH] = np.kron(weights, np.ones(COLUMN))
    lanes[3, : INNER_WIDTH] = inner_node
    lanes[4, : INNER_WIDTH] = inner_lumped
    columns = np.zeros((ypad, 8))
    columns[:rows_local, 0] = lumped_y
    columns[:5, 1] = weights
    along_y = np.zeros((16, 8))
    along_y[:5, :5] = slopes
    along_y[8:13, :5] = slopes.T
    pick = np.zeros((RADIAL * 32, PAD))
    for r in range(RADIAL):
        for line in range(LINES):
            pick[r * 32 + line, line * RADIAL + r] = 1.0
    polar = np.zeros((PAIRS * 128, 256))
    for f in range(FIELDS):
        for k in (4, 5):
            for r in range(RADIAL):
                if channel(r, f) is not None:
                    polar[(f // 2) * 128 + (f % 2) * 64 + k * RADIAL + r, (k - 4) * 128 + channel(r, f)] = 1.0
    as_f32 = lambda t: np.asarray(t, np.float32)
    as_bf16 = lambda t: np.asarray(t, np.float32).astype(bf16)

    def split(t):
        rest = as_f32(t)
        out = []
        for _ in range(3):
            out.append(rest.astype(bf16))
            rest = rest - out[-1].astype(np.float32)
        return np.stack(out)

    return dict(
        table=split(table[:, : 2 * PAD]),
        plain=as_bf16(table[:, 2 * PAD + TILE :] * (np.arange(TILE, PAD) >= WIDTH)),
        inner_table=split(inner_table[:, : 2 * INNER_PAD]),
        spread=as_bf16(padded(spread, PAD)),
        squeeze=as_bf16(np.pad(spread.T, ((0, PAD - WIDTH), (0, 0)))),
        lanes=as_f32(lanes),
        columns=as_f32(columns),
        along_y=as_f32(along_y),
        pick=as_bf16(pick),
        polar=as_bf16(polar),
        polar_back=as_bf16(polar.T),
    )


def exchange_tables(count_x, count_y, rows):
    reach_x, reach_y = ACROSS - 1, rows - 1
    side = count_x * reach_x
    ypad = -(-rows // 8) * 8

    def canonical(j, i, y, x, k):
        gy, gx = j * reach_y + y, i * reach_x + x
        if k < 4 and gx == side:
            k, gx = (k + 1) % 4, 0
        if k < 4 and gy == side:
            gx, gy = ((gx, 0), (side, gx), (side - gx, side), (0, side - gx))[k]
            k = 4
        elif k < 4 and gy == 0:
            gx, gy = ((gx, side), (side, side - gx), (side - gx, 0), (0, gx))[k]
            k = 5
        return k, gy, gx

    def swapped(source, target):
        sj, si, sy, sx, sk = source
        j, i, y, x, k = target
        if sj == j and sy == y:
            if (x, sx) == (reach_x, 0):
                if (si, sk) == (i + 1, k):
                    return True
                if i == count_x - 1 and si == 0 and k < 4 and sk == (k + 1) % 4:
                    return True
            if (x, sx) == (0, reach_x):
                if (si, sk) == (i - 1, k):
                    return True
                if i == 0 and si == count_x - 1 and k < 4 and sk == (k - 1) % 4:
                    return True
        if si == i and sx == x:
            if sk == k and (sj, sy, y) in ((j + 1, 0, reach_y), (j - 1, reach_y, 0)):
                return True
            if (j, y, sj, sy) == (0, 0, count_y - 1, reach_y) and (k, sk) in ((4, 0), (0, 5)):
                return True
            if (j, y, sj, sy) == (count_y - 1, reach_y, 0, 0) and (k, sk) in ((0, 4), (5, 0)):
                return True
        return False

    def row_of(y, x, k):
        if y == reach_y:
            return x * GROUPS + k
        if y == 0:
            return 32 + x * GROUPS + k
        return 64 + (k - 4) * 2 * ypad + (ypad if x else 0) + y

    copies = collections.defaultdict(list)
    for j in range(count_y):
        for i in range(count_x):
            for y in range(rows):
                for x in range(ACROSS):
                    if 0 < y < reach_y and 0 < x < reach_x:
                        continue
                    for k in range(GROUPS):
                        copies[canonical(j, i, y, x, k)].append((j, i, y, x, k))
    pairs = collections.defaultdict(list)
    for members in copies.values():
        for target in members:
            for source in members:
                if source != target and not swapped(source, target):
                    key = (source[1] * count_y + source[0], target[1] * count_y + target[0])
                    pairs[key].append((row_of(*source[2:]), row_of(*target[2:])))
    table = np.full((count_x * count_y, 8, ENTRIES), -1.0, np.float32)
    sent = collections.Counter()
    taken = collections.Counter()
    peers = count_x * count_y
    for (source, target), links in sorted(pairs.items()):
        assert len(links) <= RUNS * RUN_POINTS
        for slot, (row_from, row_to) in enumerate(sorted(links)):
            run, place = divmod(slot, RUN_POINTS)
            for device, peer, row, counts, base in (
                (source, target, row_from, sent, 0),
                (target, source, row_to, taken, 2),
            ):
                assert counts[device, place] < CLASS
                entry = place * CLASS + counts[device, place]
                counts[device, place] += 1
                table[device, base, entry] = run * peers + peer
                table[device, base + 1, entry] = row
    return table


bf16 = jnp.bfloat16


def parts_of(x):
    high = x.astype(bf16)
    rest = x - high.astype(jnp.float32)
    middle = rest.astype(bf16)
    return high, middle, (rest - middle.astype(jnp.float32)).astype(bf16)


def product(a, b, back=False):
    dims = (((1,), (1 if back else 0,)), ((), ()))
    return lax.dot_general(a, b, dims, preferred_element_type=jnp.float32)


def pick_right(x, chosen):
    count = x.shape[0]
    out = product(jnp.concatenate(parts_of(x), axis=0), chosen)
    return out[0:count] + out[count : 2 * count] + out[2 * count : 3 * count]


def pick_left(chosen, x):
    width = x.shape[1]
    out = product(chosen, jnp.concatenate(parts_of(x), axis=1))
    return out[:, 0:width] + out[:, width : 2 * width] + out[:, 2 * width : 3 * width]


def times(x, table, lanes, back=False):
    count = x.shape[0]
    high, middle, low = parts_of(x)
    out = product(jnp.concatenate([high, middle, low], axis=0), table[0, :, lanes], back)
    total = out[0:count] + (out[count : 2 * count] + out[2 * count : 3 * count])
    out = product(jnp.concatenate([high, middle], axis=0), table[1, :, lanes], back)
    total = total + (out[0:count] + out[count : 2 * count])
    return total + product(high, table[2, :, lanes], back)


def turn_lanes(x, shift):
    shift = shift % x.shape[1]
    return pltpu.roll(x, shift, axis=1) if shift else x


def chosen_by(condition):
    return jnp.where(condition, 1.0, 0.0).astype(bf16)


def iota(shape, axis):
    return lax.broadcasted_iota(jnp.int32, shape, axis)


def put(ref, row, block):
    for t in range(ref.shape[0]):
        width = min(128, block.shape[1] - 128 * t)
        ref[t, row : row + block.shape[0], 0:width] = block[:, 128 * t : 128 * t + width]


def take(ref, c, first, count):
    tiles = [ref[t, pl.ds(4 * first + c, count, stride=4), :] for t in range(ref.shape[0])]
    return jnp.concatenate(tiles, axis=1)


def scatter(ref, c, block):
    for t in range(ref.shape[0]):
        ref[t, pl.ds(c, block.shape[0], stride=4), :] = block[:, 128 * t : 128 * t + 128]


def own_table(table_ref, count_y):
    return table_ref[lax.axis_index("xi") * count_y + lax.axis_index("eta")]


def force_kernel(
    rows,
    count_x,
    count_y,
    disp,
    vel,
    acc,
    metric,
    moduli,
    rho,
    pot,
    rate,
    accel,
    core_metric,
    kappa,
    core_rho,
    inner_disp,
    inner_vel,
    inner_acc,
    inner_metric,
    inner_moduli,
    inner_rho,
    table_ref,
    forward,
    plain_lanes,
    inner_forward,
    spread,
    lanes,
    columns,
    along_y,
    pick,
    polar,
    fields,
    send_xa,
    send_xb,
    send_ya,
    send_yb,
    send_all,
    wide,
    narrow,
    inner_rows,
    flux,
    inner_flux,
    wide_u,
    edges,
    rows_t,
    points,
    moved,
    scale,
    lame,
    core_scale,
    inner_moved,
    inner_scale,
    inner_lame,
    stack,
    shifted,
    copies,
    pot_next,
):
    ne = (rows - 1) // 4
    ypad = edges.shape[0] // 2
    half = 0.5 * time_step * time_step
    for y in range(rows):
        block = disp[y] + time_step * vel[y] + half * acc[y]
        put(moved, 4 * y, block)
        put(scale, 4 * y, metric[y])
        put(lame, 4 * y, moduli[y])
        put(core_scale, 4 * y, core_metric[y])
        block = inner_disp[y] + time_step * inner_vel[y] + half * inner_acc[y]
        put(inner_moved, 4 * y, block)
        put(inner_scale, 4 * y, inner_metric[y])
        put(inner_lame, 4 * y, inner_moduli[y])

    def part(ref, c, first=0, count=rows):
        width = WIDTH if ref.shape[0] * 128 == PAD else INNER_WIDTH
        return take(ref, c, first, count)[:, 0:width]

    pot_next[...] = pot[...] + time_step * rate[...] + half * accel[...]

    slope = along_y[0:5, 0:5]
    slope_back = along_y[8:13, 0:5]

    def along(matrix, block):
        total = matrix[:, 0:1] * block[0:1, :]
        for b in range(1, 5):
            total = total + matrix[:, b : b + 1] * block[b : b + 1, :]
        return total

    narrow[:, TILE:PAD] = jnp.zeros((narrow.shape[0], PAD - TILE), jnp.float32)
    for first in (0, INNER_PAD):
        inner_flux[:, first + 128 : first + 256] = jnp.zeros((inner_flux.shape[0], 128), jnp.float32)
    stack[...] = jnp.zeros(stack.shape, jnp.float32)
    fields[...] = jnp.zeros(fields.shape, jnp.float32)

    def slot(f, e):
        return (f * ne + e) * 8

    extras = [(scale, c) for c in range(3)] + [(lame, c) for c in range(2)] + [(core_scale, c) for c in range(3)]
    for e in range(ne):
        for f in range(4):
            block = part(moved, f, 4 * e, 5) if f < 3 else pot_next[4 * e : 4 * e + 5, :]
            wide[slot(f, e) : slot(f, e) + 5, :] = block
            narrow[slot(f, e) : slot(f, e) + 5, 0:WIDTH] = along(slope, block)
        for f, (ref, c) in enumerate(extras):
            narrow[slot(4 + f, e) : slot(4 + f, e) + 5, 0:WIDTH] = part(ref, c, 4 * e, 5)
        narrow[slot(12, e) : slot(12, e) + 5, 0:WIDTH] = core_rho[4 * e : 4 * e + 5, :]
        for f in range(3):
            inner_rows[slot(f, e) : slot(f, e) + 5, :] = part(inner_moved, f, 4 * e, 5)
    whole = slice(None)
    slopes_xr = times(wide[...], forward, whole)
    copies[...] = narrow[:, TILE:PAD] + pick_right(narrow[:, 0:WIDTH], plain_lanes[...])
    inner_xr = times(inner_rows[...], inner_forward, whole)

    def elastic(g, lam, mu, sy, sx, sr, jw):
        scaled = [[sy[i] * g[0], sx[i] * g[1], sr[i] * g[2]] for i in range(3)]
        trace = lam * (scaled[0][0] + scaled[1][1] + scaled[2][2])
        out = [[None] * 3 for _ in range(3)]
        weighted = [jw * g[m] for m in range(3)]
        for i in range(3):
            for m in range(3):
                if i == m:
                    stress = 2.0 * mu * scaled[i][i] + trace
                else:
                    stress = mu * (scaled[i][m] + scaled[m][i])
                out[i][m] = stress * weighted[m]
        return out

    row_weight = columns[0:5, 1:2]
    valid = (iota((5, PAD), 1) < NODES) & (iota((5, PAD), 0) < 5)
    for e in range(ne):
        def plain(f):
            at = slice(slot(f, e), slot(f, e) + 5)
            return jnp.concatenate([narrow[at, 0:TILE], copies[at, :]], axis=1)

        def x_of(f):
            return slopes_xr[slot(f, e) : slot(f, e) + 5, 0:PAD]

        def r_of(f):
            return slopes_xr[slot(f, e) : slot(f, e) + 5, PAD : 2 * PAD]

        node = row_weight * lanes[0:1, :]
        g = [jnp.where(valid, plain(4 + m), 1.0) for m in range(3)]
        q = elastic(
            g,
            plain(7),
            plain(8),
            [plain(f) for f in range(3)],
            [x_of(f) for f in range(3)],
            [r_of(f) for f in range(3)],
            node / (g[0] * g[1] * g[2]),
        )
        g = [jnp.where(valid, plain(9 + m), 1.0) for m in range(3)]
        volume = node / (g[0] * g[1] * g[2] * jnp.where(valid, plain(12), 1.0))
        q.append(
            [
                volume * g[0] * g[0] * plain(3),
                volume * g[1] * g[1] * x_of(3),
                volume * g[2] * g[2] * r_of(3),
            ]
        )
        for f in range(4):
            at = slot(f, e)
            flux[at : at + 5, 0:PAD] = q[f][1]
            flux[at : at + 5, PAD : 2 * PAD] = q[f][2]
            flux[at : at + 5, 2 * PAD : 3 * PAD] = along(slope_back, q[f][0])

        def inner_x(f):
            return inner_xr[slot(f, e) : slot(f, e) + 5, 0:INNER_WIDTH]

        def inner_r(f):
            return inner_xr[slot(f, e) : slot(f, e) + 5, INNER_PAD : INNER_PAD + INNER_WIDTH]

        g = [part(inner_scale, m, 4 * e, 5) for m in range(3)]
        node = row_weight * lanes[3:4, 0:INNER_WIDTH]
        q = elastic(
            g,
            part(inner_lame, 0, 4 * e, 5),
            part(inner_lame, 1, 4 * e, 5),
            [along(slope, inner_rows[slot(f, e) : slot(f, e) + 5, :]) for f in range(3)],
            [inner_x(f) for f in range(3)],
            [inner_r(f) for f in range(3)],
            node / (g[0] * g[1] * g[2]),
        )
        for f in range(3):
            at = slot(f, e)
            inner_flux[at : at + 5, 0:INNER_WIDTH] = q[f][1]
            inner_flux[at : at + 5, INNER_PAD : INNER_PAD + INNER_WIDTH] = q[f][2]
            inner_flux[at : at + 5, 2 * INNER_PAD : 2 * INNER_PAD + INNER_WIDTH] = along(slope_back, q[f][0])

    back = times(flux[:, 0 : 2 * PAD], forward, whole, back=True)
    count = flux.shape[0]
    out = product(
        jnp.concatenate(parts_of(flux[:, 2 * PAD + TILE : 3 * PAD]), axis=0), plain_lanes[...], back=True
    )
    back = back + flux[:, 2 * PAD : 2 * PAD + WIDTH] + (out[0:count] + out[count : 2 * count] + out[2 * count : 3 * count])
    count = 3 * ne * 8
    stack[0:count, :] = (
        times(inner_flux[:, 0 : 2 * INNER_PAD], inner_forward, whole, back=True)
        + inner_flux[:, 2 * INNER_PAD : 2 * INNER_PAD + INNER_WIDTH]
    )
    lumped_y = columns[0:rows, 0:1]
    stack[count : count + rows, :] = inner_rho[...] * (
        lumped_y * lanes[4:5, 0:INNER_WIDTH] / (part(inner_scale, 0) * part(inner_scale, 1) * part(inner_scale, 2))
    )
    stack[count + ypad : count + ypad + rows, :] = part(inner_moved, 2)
    spreads = pick_right(stack[...], spread[...])
    inner_forces = spreads[0:count, 0:WIDTH]
    for e in range(ne):
        here = slice(4 * e, 4 * e + 5)
        for f in range(3):
            fields[f, here, 0:WIDTH] = fields[f, here, 0:WIDTH] - back[slot(f, e) : slot(f, e) + 5, :]
            fields[IF + f, here, 0:WIDTH] = fields[IF + f, here, 0:WIDTH] - inner_forces[slot(f, e) : slot(f, e) + 5, :]
        fields[CF, here, 0:WIDTH] = fields[CF, here, 0:WIDTH] - back[slot(3, e) : slot(3, e) + 5, :]

    lumped = lumped_y * lanes[1:2, 0:WIDTH]
    fields[MM, 0:rows, 0:WIDTH] = rho[...] * (lumped / (part(scale, 0) * part(scale, 1) * part(scale, 2)))
    fields[CM, 0:rows, 0:WIDTH] = lumped / (part(core_scale, 0) * part(core_scale, 1) * part(core_scale, 2)) / kappa[...]
    fields[IM, 0:rows, :] = spreads[count : count + rows]
    radial = lax.rem(iota((rows, WIDTH), 1), RADIAL)
    face = lumped_y * lanes[2:3, 0:WIDTH] / (part(core_scale, 0) * part(core_scale, 1))
    face = jnp.where((radial == 0) | (radial == RADIAL - 1), face, 0.0)
    fields[CW, 0:rows, 0:WIDTH] = face
    wide_u[...] = jnp.zeros(wide_u.shape, jnp.float32)
    wide_u[0:rows, 0:WIDTH] = part(moved, 2)
    above = pltpu.roll(wide_u[...], RADIAL - 1, axis=1)
    below = pltpu.roll(spreads[count + ypad : count + 2 * ypad], PAD - (INNER_RADIAL - 1), axis=1)
    radial = lax.rem(iota((ypad, PAD), 1), RADIAL)
    jump = jnp.where(radial == RADIAL - 1, above, jnp.where(radial == 0, -below, 0.0))
    fields[CF] = fields[CF] + fields[CW] * jump

    low = iota((ypad, 128), 1) < 64
    for p in range(PAIRS):
        left = fields[2 * p]
        right = fields[2 * p + 1] if 2 * p + 1 < FIELDS else jnp.zeros_like(left)
        edges[0:ypad, p * 128 : p * 128 + 128] = jnp.where(low, left[:, 0:128], pltpu.roll(right[:, 0:128], 64, axis=1))
        edges[ypad : 2 * ypad, p * 128 : p * 128 + 128] = jnp.where(
            low,
            pltpu.roll(left, PAD - (WIDTH - COLUMN), axis=1)[:, 0:128],
            pltpu.roll(right, PAD + 64 - (WIDTH - COLUMN), axis=1)[:, 0:128],
        )
    even_x = lax.rem(lax.axis_index("xi"), 2) == 0
    even_y = lax.rem(lax.axis_index("eta"), 2) == 0
    for p in range(PAIRS):
        first = edges[0:rows, p * 128 : p * 128 + 128]
        last = edges[ypad : ypad + rows, p * 128 : p * 128 + 128]
        send_xa[p * rows : (p + 1) * rows, :] = jnp.where(even_x, last, first)
        send_xb[p * rows : (p + 1) * rows, :] = jnp.where(even_x, first, last)
    rows_t[0:16, :] = jnp.zeros((16, PAD), jnp.float32)
    rows_t[64:80, :] = jnp.zeros((16, PAD), jnp.float32)
    for f in range(FIELDS):
        rows_t[f : f + 1, :] = fields[f, rows - 1 : rows, :]
        rows_t[64 + f : 65 + f, :] = fields[f, 0:1, :]
    top = rows_t[0:16, :]
    bottom = rows_t[64:80, :]
    send_ya[...] = jnp.where(even_y, top, bottom)
    send_yb[...] = jnp.where(even_y, bottom, top)

    for at, block in ((0, top), (64, bottom)):
        for n, piece in enumerate(parts_of(block)):
            rows_t[at + 16 * n : at + 16 * n + 16, :] = piece.astype(jnp.float32)
    by_line = product(pick[...], rows_t[...].astype(bf16), back=True)
    by_line = by_line + (pltpu.roll(by_line, 128 - 16, axis=1) + pltpu.roll(by_line, 128 - 32, axis=1))
    lane = iota((32, 128), 1)
    top_points = jnp.zeros((32, 128), jnp.float32)
    bottom_points = jnp.zeros((32, 128), jnp.float32)
    for r in range(RADIAL):
        block = by_line[32 * r : 32 * r + 32, :]
        for first, end, at in runs_of(r):
            upper = jnp.where((lane >= first) & (lane < end), block, 0.0)
            lower = jnp.where((lane >= 64 + first) & (lane < 64 + end), block, 0.0)
            top_points = top_points + turn_lanes(upper, at - first)
            bottom_points = bottom_points + turn_lanes(lower, at - first - 64)
    points[0:32, :] = top_points
    points[32:64, :] = bottom_points
    caps = pick_right(edges[...], polar[...])
    points[64 : 64 + 2 * ypad, :] = caps[:, 0:128]
    points[64 + 2 * ypad : 64 + 4 * ypad, :] = caps[:, 128:256]

    own = own_table(table_ref, count_y)
    turned = jnp.transpose(own)
    count = points.shape[0]
    chosen = chosen_by(turned[:, 1:2] == iota((ENTRIES, count), 1).astype(jnp.float32))
    chosen = pick_left(chosen, points[...])
    shifted[...] = jnp.zeros(shifted.shape, jnp.float32)
    lane = iota((CLASS, 128), 1)
    for place in range(RUN_POINTS):
        tile, shift = divmod(place * CHANNELS, 128)
        here = slice(place * CLASS, (place + 1) * CLASS)
        block = turn_lanes(chosen[here], shift)
        shifted[here, tile * 128 : tile * 128 + 128] = jnp.where(lane >= shift, block, 0.0)
        if shift + CHANNELS > 128:
            shifted[here, tile * 128 + 128 : tile * 128 + 256] = jnp.where(lane < shift, block, 0.0)
    peers = count_x * count_y
    number = iota((RUNS * peers, ENTRIES), 0).astype(jnp.float32)
    placed = pick_left(chosen_by(own[0:1, :] == number), shifted[...])
    for row in range(BLOCK):
        run, tile = divmod(row, RUN_ROWS)
        if run < RUNS:
            block = placed[run * peers : (run + 1) * peers, tile * 128 : tile * 128 + 128]
        else:
            block = jnp.zeros((peers, 128), jnp.float32)
        send_all[pl.ds(row, peers, stride=BLOCK), :] = block


def window_kernel(
    disp,
    vel,
    acc,
    pot,
    rate,
    accel,
    inner_disp,
    inner_vel,
    inner_acc,
    fields,
    disp_next,
    pot_next,
    inner_next,
    vel_half,
    rate_half,
    inner_half,
    fields_out,
):
    half = 0.5 * time_step
    for new, between, place, speed, change in (
        (disp_next, vel_half, disp, vel, acc),
        (pot_next, rate_half, pot, rate, accel),
        (inner_next, inner_half, inner_disp, inner_vel, inner_acc),
    ):
        new[...] = place[...] + time_step * speed[...] + half * time_step * change[...]
        between[...] = speed[...] + half * change[...]
    fields_out[...] = fields[...]


def close_kernel(
    rows,
    count_x,
    count_y,
    got_xa,
    got_xb,
    got_ya,
    got_yb,
    got_all,
    fields,
    vel_half,
    rate_half,
    inner_half,
    table_ref,
    pick,
    polar_back,
    squeeze,
    vel_next,
    acc_next,
    rate_next,
    accel_next,
    inner_vel_next,
    inner_acc_next,
    total,
    by_line,
    caps,
    narrow,
    wide,
    runs,
    arrived,
):
    ypad = total.shape[1]
    narrow[...] = jnp.zeros(narrow.shape, jnp.float32)
    own = own_table(table_ref, count_y)
    turned = jnp.transpose(own)
    peers = count_x * count_y
    for run in range(RUNS):
        for tile in range(RUN_ROWS):
            runs[run * peers : (run + 1) * peers, tile * 128 : tile * 128 + 128] = got_all[
                pl.ds(run * RUN_ROWS + tile, peers, stride=BLOCK), :
            ]
    number = iota((ENTRIES, RUNS * peers), 1).astype(jnp.float32)
    shifted = pick_left(chosen_by(turned[:, 2:3] == number), runs[...])
    lane = iota((CLASS, 128), 1)
    arrived[...] = jnp.zeros(arrived.shape, jnp.float32)
    for place in range(RUN_POINTS):
        tile, shift = divmod(place * CHANNELS, 128)
        here = slice(place * CLASS, (place + 1) * CLASS)
        block = shifted[here, tile * 128 : tile * 128 + 128]
        if shift + CHANNELS > 128:
            block = jnp.where(lane >= shift, block, shifted[here, tile * 128 + 128 : tile * 128 + 256])
        arrived[here, :] = jnp.where(lane < CHANNELS, turn_lanes(block, -shift), 0.0)
    count = 64 + 4 * ypad
    points = pick_left(chosen_by(own[3:4, :] == iota((count, ENTRIES), 0).astype(jnp.float32)), arrived[...])
    lane = iota((32, 128), 1)
    upper = points[0:32]
    lower = points[32:64]
    for r in range(RADIAL):
        block = jnp.zeros((32, 128), jnp.float32)
        for first, end, at in runs_of(r):
            high = turn_lanes(upper, first - at)
            low = turn_lanes(lower, 64 + first - at)
            block = jnp.where((lane >= first) & (lane < end), high, block)
            block = jnp.where((lane >= 64 + first) & (lane < 64 + end), low, block)
        high, middle, last = (piece.astype(jnp.float32) for piece in parts_of(block))
        by_line[32 * r : 32 * r + 32, :] = (
            high + pltpu.roll(middle, 16, axis=1) + pltpu.roll(last, 32, axis=1)
        )
    lines = lax.dot_general(
        by_line[...].astype(bf16), pick[...], (((0,), (0,)), ((), ())), preferred_element_type=jnp.float32
    )
    lines_top = lines[0:16] + (lines[16:32] + lines[32:48])
    lines_bottom = lines[64:80] + (lines[80:96] + lines[96:112])
    caps[:, 0:128] = points[64 : 64 + 2 * ypad]
    caps[:, 128:256] = points[64 + 2 * ypad : 64 + 4 * ypad]
    columns = pick_right(caps[...], polar_back[...])

    xi = lax.axis_index("xi")
    eta = lax.axis_index("eta")
    even_x = lax.rem(xi, 2) == 0
    even_y = lax.rem(eta, 2) == 0
    lane = iota((16, PAD), 1)
    group = lax.rem(lane // RADIAL, GROUPS)
    used = lane < WIDTH
    ya = got_ya[...]
    yb = got_yb[...]
    from_above = jnp.where(even_y, ya, yb)
    from_below = jnp.where(even_y, yb, ya)
    four, five = 4 * RADIAL, 5 * RADIAL
    seam_top = jnp.where(
        group == 0,
        pltpu.roll(from_above, PAD - four, axis=1),
        jnp.where(group == 5, pltpu.roll(from_above, five, axis=1), 0.0),
    )
    seam_bottom = jnp.where(
        group == 4,
        pltpu.roll(from_below, four, axis=1),
        jnp.where(group == 0, pltpu.roll(from_below, PAD - five, axis=1), 0.0),
    )
    add_top = jnp.where(eta == count_y - 1, seam_top, from_above) + lines_top
    add_bottom = jnp.where(eta == 0, seam_bottom, from_below) + lines_bottom
    add_top = jnp.where(used, add_top, 0.0)
    add_bottom = jnp.where(used, add_bottom, 0.0)
    total[...] = fields[...]
    lane = iota((rows, 128), 1)
    inside = lax.rem(lane, 64)
    equator = inside < 4 * RADIAL
    keep = inside < COLUMN
    low = lane < 64
    last_x = xi == count_x - 1
    for p in range(PAIRS):
        xa = got_xa[p * rows : (p + 1) * rows, :]
        xb = got_xb[p * rows : (p + 1) * rows, :]
        from_right = jnp.where(even_x, xa, xb)
        from_left = jnp.where(even_x, xb, xa)
        up = jnp.where(
            inside < 3 * RADIAL,
            pltpu.roll(from_right, 128 - RADIAL, axis=1),
            pltpu.roll(from_right, 3 * RADIAL, axis=1),
        )
        down = jnp.where(
            inside < RADIAL,
            pltpu.roll(from_left, 128 - 3 * RADIAL, axis=1),
            pltpu.roll(from_left, RADIAL, axis=1),
        )
        from_right = jnp.where(last_x, jnp.where(equator, up, 0.0), from_right)
        from_left = jnp.where(xi == 0, jnp.where(equator, down, 0.0), from_left)
        at = slice(p * 128, p * 128 + 128)
        from_left = jnp.where(keep, from_left + columns[0:rows, at], 0.0)
        from_right = jnp.where(keep, from_right + columns[ypad : ypad + rows, at], 0.0)
        zero = jnp.zeros((rows, PAD - 128), jnp.float32)
        for h in range(2):
            f = 2 * p + h
            if f >= FIELDS:
                continue
            mine = low if h == 0 else ~low
            left = jnp.where(mine, from_left, 0.0)
            right = jnp.where(mine, from_right, 0.0)
            if h:
                left = pltpu.roll(left, 64, axis=1)
            total[f, 0:rows, 0:128] = total[f, 0:rows, 0:128] + left
            right = jnp.concatenate([right, zero], axis=1)
            right = pltpu.roll(right, WIDTH - COLUMN - 64 * h, axis=1)
            total[f, 0:rows, :] = total[f, 0:rows, :] + right
    for f in range(FIELDS):
        total[f, rows - 1 : rows, :] = total[f, rows - 1 : rows, :] + add_top[f : f + 1, :]
        total[f, 0:1, :] = total[f, 0:1, :] + add_bottom[f : f + 1, :]

    half = 0.5 * time_step
    lane = iota((ypad, PAD), 1)
    radial = lax.rem(lane, RADIAL)
    inside = (lane < WIDTH) & (iota((ypad, PAD), 0) < rows)
    core = total[CF] / jnp.where(inside, total[CM], 1.0)
    accel_next[...] = core[0:rows, 0:WIDTH]
    rate_next[...] = rate_half[...] + half * core[0:rows, 0:WIDTH]
    push = total[CW] * core
    top = jnp.where(radial == 0, pltpu.roll(push, PAD - (RADIAL - 1), axis=1), 0.0)
    bottom = jnp.where(radial == INNER_RADIAL - 1, pltpu.roll(push, INNER_RADIAL - 1, axis=1), 0.0)
    mass = jnp.where(inside, total[MM], 1.0)
    inner_mass = jnp.where(inside & (radial < INNER_RADIAL), total[IM], 1.0)
    for f in range(3):
        force = total[f] + top if f == 2 else total[f]
        result = (force / mass)[0:rows]
        scatter(wide, f, result)
        force = total[IF + f] - bottom if f == 2 else total[IF + f]
        scatter(narrow, f, (force / inner_mass)[0:rows])
    squeezed = pick_right(jnp.concatenate([narrow[t] for t in range(PAD // 128)], axis=1), squeeze[...])
    for y in range(rows):
        result = jnp.concatenate([wide[t, 4 * y : 4 * y + 3, :] for t in range(PAD // 128)], axis=1)[:, 0:WIDTH]
        acc_next[y] = result
        vel_next[y] = vel_half[y] + half * result
        result = squeezed[4 * y : 4 * y + 3, :]
        inner_acc_next[y] = result
        inner_vel_next[y] = inner_half[y] + half * result


def shards(
    count_x,
    count_y,
    mantle_disp,
    mantle_vel,
    mantle_acc,
    mantle_metric,
    mantle_moduli,
    mantle_rho,
    core_pot,
    core_rate,
    core_accel,
    core_metric,
    core_kappa,
    core_rho,
    inner_disp,
    inner_vel,
    inner_acc,
    inner_metric,
    inner_moduli,
    inner_rho,
):
    rows = mantle_disp.shape[1]
    turn = lambda a: jnp.transpose(a, (1, 0, 2))
    mantle_disp, mantle_vel, mantle_acc = turn(mantle_disp), turn(mantle_vel), turn(mantle_acc)
    mantle_metric, mantle_moduli, core_metric = turn(mantle_metric), turn(mantle_moduli), turn(core_metric)
    inner_disp, inner_vel, inner_acc = turn(inner_disp), turn(inner_vel), turn(inner_acc)
    inner_metric, inner_moduli = turn(inner_metric), turn(inner_moduli)
    ne = (rows - 1) // 4
    ypad = -(-rows // 8) * 8
    tables = {name: jnp.asarray(value) for name, value in constants(rows).items()}
    table = jnp.asarray(exchange_tables(count_x, count_y, rows))
    f32 = jnp.float32
    like = lambda a: jax.ShapeDtypeStruct(a.shape, f32)
    shape = lambda *s: jax.ShapeDtypeStruct(s, f32)
    devices = count_x * count_y
    edge = -(-PAIRS * rows // 8) * 8
    (fields, xa, xb, ya, yb, everyone) = pl.pallas_call(
        functools.partial(force_kernel, rows, count_x, count_y),
        out_shape=[
            shape(FIELDS, ypad, PAD),
            shape(edge, 128),
            shape(edge, 128),
            shape(16, PAD),
            shape(16, PAD),
            shape(devices * BLOCK, 128),
        ],
        scratch_shapes=[
            pltpu.VMEM((4 * ne * 8, WIDTH), f32),
            pltpu.VMEM((13 * ne * 8, PAD), f32),
            pltpu.VMEM((3 * ne * 8, INNER_WIDTH), f32),
            pltpu.VMEM((4 * ne * 8, 3 * PAD), f32),
            pltpu.VMEM((3 * ne * 8, 3 * INNER_PAD), f32),
            pltpu.VMEM((ypad, PAD), f32),
            pltpu.VMEM((2 * ypad, PAIRS * 128), f32),
            pltpu.VMEM((128, PAD), f32),
            pltpu.VMEM((64 + 4 * ypad, 128), f32),
        ]
        + [pltpu.VMEM((PAD // 128, 4 * rows, 128), f32)] * 4
        + [pltpu.VMEM((INNER_PAD // 128, 4 * rows, 128), f32)] * 3
        + [pltpu.VMEM((3 * ne * 8 + 2 * ypad, INNER_WIDTH), f32)]
        + [pltpu.VMEM((ENTRIES, RUN_ROWS * 128), f32)]
        + [pltpu.VMEM((13 * ne * 8, PAD - TILE), f32)]
        + [pltpu.VMEM((rows, WIDTH), f32)],
        name="forces",
    )(
        mantle_disp,
        mantle_vel,
        mantle_acc,
        mantle_metric,
        mantle_moduli,
        mantle_rho,
        core_pot,
        core_rate,
        core_accel,
        core_metric,
        core_kappa,
        core_rho,
        inner_disp,
        inner_vel,
        inner_acc,
        inner_metric,
        inner_moduli,
        inner_rho,
        table,
        tables["table"],
        tables["plain"],
        tables["inner_table"],
        tables["spread"],
        tables["lanes"],
        tables["columns"],
        tables["along_y"],
        tables["pick"],
        tables["polar"],
    )
    everyone = lax.all_to_all(everyone, ("xi", "eta"), 0, 0, tiled=True)
    near = [(i, i ^ 1) for i in range(count_x)]
    far = [(i, (i - 1 if i % 2 == 0 else i + 1) % count_x) for i in range(count_x)]
    xa = lax.ppermute(xa, "xi", near)
    xb = lax.ppermute(xb, "xi", far)
    near = [(j, j ^ 1) for j in range(count_y)]
    far = [(j, (j - 1 if j % 2 == 0 else j + 1) % count_y) for j in range(count_y)]
    ya = lax.ppermute(ya, "eta", near)
    yb = lax.ppermute(yb, "eta", far)
    (mantle_next, core_next, inner_next, vel_half, rate_half, inner_half, fields) = pl.pallas_call(
        window_kernel,
        out_shape=[like(a) for a in (mantle_disp, core_pot, inner_disp) * 2] + [like(fields)],
        compiler_params=pltpu.CompilerParams(vmem_limit_bytes=WINDOW_GRANT),
        name="window",
    )(mantle_disp, mantle_vel, mantle_acc, core_pot, core_rate, core_accel, inner_disp, inner_vel, inner_acc, fields)
    (mantle_vel_next, mantle_acc_next, core_rate_next, core_acc_next, inner_vel_next, inner_acc_next) = pl.pallas_call(
        functools.partial(close_kernel, rows, count_x, count_y),
        out_shape=[
            like(mantle_vel),
            like(mantle_acc),
            like(core_rate),
            like(core_accel),
            like(inner_vel),
            like(inner_acc),
        ],
        scratch_shapes=[
            pltpu.VMEM((FIELDS, ypad, PAD), f32),
            pltpu.VMEM((RADIAL * 32, 128), f32),
            pltpu.VMEM((2 * ypad, 256), f32),
            pltpu.VMEM((PAD // 128, -(-4 * rows // 16) * 16, 128), f32),
            pltpu.VMEM((PAD // 128, 4 * rows, 128), f32),
            pltpu.VMEM((RUNS * devices, RUN_ROWS * 128), f32),
            pltpu.VMEM((ENTRIES, 128), f32),
        ],
        compiler_params=pltpu.CompilerParams(vmem_limit_bytes=(8 << 20) + devices * (48 << 10)),
        name="close",
    )(
        xa,
        xb,
        ya,
        yb,
        everyone,
        fields,
        vel_half,
        rate_half,
        inner_half,
        table,
        tables["pick"],
        tables["polar_back"],
        tables["squeeze"],
    )
    return (
        turn(mantle_next),
        turn(mantle_vel_next),
        turn(mantle_acc_next),
        core_next,
        core_rate_next,
        core_acc_next,
        turn(inner_next),
        turn(inner_vel_next),
        turn(inner_acc_next),
    )


def solution(mesh):
    count_x, count_y = mesh.shape["xi"], mesh.shape["eta"]
    assert count_x % 2 == 0 and count_y % 2 == 0
    assert (count_x * count_y) % 8 == 0
    vector, scalar = P(None, "eta", "xi"), P("eta", "xi")
    placed = (vector,) * 5 + (scalar,) * 4 + (vector,) + (scalar,) * 2 + (vector,) * 5 + (scalar,)
    return jax.shard_map(
        functools.partial(shards, count_x, count_y),
        mesh=mesh,
        in_specs=placed,
        out_specs=(vector,) * 3 + (scalar,) * 3 + (vector,) * 3,
        check_vma=False,
    )
```

```python
import collections
import functools
import math

import jax
import jax.numpy as jnp
import numpy as np
from jax import lax
from jax.experimental import pallas as pl
from jax.experimental.pallas import tpu as pltpu
from jax.sharding import PartitionSpec as P


EX = 1
MANTLE_LAYERS = 2
INNER_LAYERS = 1
GROUPS = 6
ACROSS = 4 * EX + 1
RADIAL = 4 * MANTLE_LAYERS + 1
INNER_RADIAL = 4 * INNER_LAYERS + 1
LINES = ACROSS * GROUPS
WIDTH = LINES * RADIAL
INNER_WIDTH = LINES * INNER_RADIAL
COLUMN = GROUPS * RADIAL
NODES = LINES * 5 * MANTLE_LAYERS
PAD = 384
INNER_PAD = 256
TILE = 256
ENTRIES = 128
BLOCK = 8
RUN_ROWS = 3
RUN_POINTS = 5
RUNS = 2
CLASS = 24
WINDOW_GRANT = 8 << 20
time_step = 0.1

MM, CF, CM, IF, IM, CW, FIELDS = 3, 4, 5, 6, 9, 10, 11
PAIRS = 6
CHANNELS = 10 * INNER_RADIAL + 6 * (RADIAL - INNER_RADIAL) + 2


def channel(r, f):
    if f == CW:
        return {0: CHANNELS - 2, RADIAL - 1: CHANNELS - 1}.get(r)
    if r < INNER_RADIAL:
        return 10 * r + f
    return 10 * INNER_RADIAL + 6 * (r - INNER_RADIAL) + f if f < IF else None


def runs_of(r):
    out = [(0, IF if r >= INNER_RADIAL else CW, channel(r, 0))]
    if channel(r, CW) is not None:
        out.append((CW, FIELDS, channel(r, CW)))
    return out


def gll_tables():
    radical = math.sqrt(3.0 / 7.0)
    points = np.array([-1.0, -radical, 0.0, radical, 1.0])
    weights = np.array([0.1, 49.0 / 90.0, 32.0 / 45.0, 49.0 / 90.0, 0.1])
    products = np.array(
        [np.prod([points[a] - points[c] for c in range(5) if c != a]) for a in range(5)]
    )
    slopes = np.zeros((5, 5))
    for a in range(5):
        for b in range(5):
            if a == b:
                slopes[a, b] = np.sum([1.0 / (points[a] - points[c]) for c in range(5) if c != a])
            else:
                slopes[a, b] = products[a] / (products[b] * (points[a] - points[b]))
    return weights, slopes


def short_slopes():
    slopes = gll_tables()[1]
    round_bf16 = lambda v: float(np.float32(v).astype(jnp.bfloat16))
    high = np.vectorize(round_bf16)(slopes)
    low = np.vectorize(round_bf16)(slopes - high)
    for a in range(5):
        for _ in range(3):
            for b in np.argsort(np.abs(low[a])):
                excess = np.sum(high[a]) + np.sum(low[a])
                low[a, b] = round_bf16(low[a, b] - excess)
    return high + low


def spread_table(count):
    spread = np.zeros((4 * count + 1, 5 * count))
    for element in range(count):
        for node in range(5):
            spread[4 * element + node, 5 * element + node] = 1.0
    return spread


def padded(table, width):
    return np.pad(table, ((0, 0), (0, width - table.shape[1])))


def lane_tables(layers, width):
    weights, slopes = gll_tables()[0], short_slopes()
    spread = spread_table(layers)
    derive = np.kron(np.eye(layers), slopes.T)
    eye_k = np.eye(GROUPS)
    along_x = np.kron(slopes.T, np.kron(eye_k, spread))
    along_r = np.kron(np.eye(ACROSS), np.kron(eye_k, spread @ derive))
    plain = np.kron(np.eye(ACROSS), np.kron(eye_k, spread))
    node = np.kron(weights, np.kron(np.ones(GROUPS), np.tile(weights, layers)))
    lumped_r = spread @ np.tile(weights, layers)
    lumped = np.kron(weights, np.kron(np.ones(GROUPS), lumped_r))
    order = node_order(layers)
    node = node[order]
    table = np.concatenate([padded(t[:, order], width) for t in (along_x, along_r, plain)], axis=1)
    return table.astype(np.float32), node.astype(np.float32), lumped.astype(np.float32)


def node_order(layers):
    radial = [max(0, (r - 1) // 4) for r in range(4 * layers + 1)]
    plain = [line * 5 * layers + 5 * e + r - 4 * e for line in range(LINES) for r, e in enumerate(radial)]
    return plain + [line * 5 * layers + 5 * e for e in range(1, layers) for line in range(LINES)]


def constants(rows_local):
    weights, slopes = gll_tables()
    count_y = (rows_local - 1) // 4
    ypad = -(-rows_local // 8) * 8
    table, node, lumped = lane_tables(MANTLE_LAYERS, PAD)
    inner_table, inner_node, inner_lumped = lane_tables(INNER_LAYERS, INNER_PAD)
    small = np.eye(RADIAL)[:INNER_RADIAL]
    spread = np.kron(np.eye(LINES), small)
    lumped_y = spread_table(count_y) @ np.tile(weights, count_y)
    lanes = np.zeros((8, PAD))
    lanes[0, :NODES] = node
    lanes[1, :WIDTH] = lumped
    lanes[2, :WIDTH] = np.kron(weights, np.ones(COLUMN))
    lanes[3, : INNER_WIDTH] = inner_node
    lanes[4, : INNER_WIDTH] = inner_lumped
    columns = np.zeros((ypad, 8))
    columns[:rows_local, 0] = lumped_y
    columns[:5, 1] = weights
    along_y = np.zeros((16, 8))
    along_y[:5, :5] = slopes
    along_y[8:13, :5] = slopes.T
    pick = np.zeros((RADIAL * 32, PAD))
    for r in range(RADIAL):
        for line in range(LINES):
            pick[r * 32 + line, line * RADIAL + r] = 1.0
    polar = np.zeros((PAIRS * 128, 256))
    for f in range(FIELDS):
        for k in (4, 5):
            for r in range(RADIAL):
                if channel(r, f) is not None:
                    polar[(f // 2) * 128 + (f % 2) * 64 + k * RADIAL + r, (k - 4) * 128 + channel(r, f)] = 1.0
    polar_short = np.zeros((2 * 128, 256))
    for f in range(FIELDS):
        for k in (4, 5):
            for r in range(RADIAL):
                if channel(r, f) is not None:
                    row = (f // 6) * 128 + (f % 2) * 64 + (f // 2 % 3) * 2 * RADIAL + (k - 4) * RADIAL + r
                    polar_short[row, (k - 4) * 128 + channel(r, f)] = 1.0
    as_f32 = lambda t: np.asarray(t, np.float32)
    as_bf16 = lambda t: np.asarray(t, np.float32).astype(bf16)

    def split(t):
        rest = as_f32(t)
        out = []
        for _ in range(2):
            out.append(rest.astype(bf16))
            rest = rest - out[-1].astype(np.float32)
        return np.stack(out)

    return dict(
        table=split(table[:, : 2 * PAD]),
        plain=as_bf16(table[:, 2 * PAD + TILE :] * (np.arange(TILE, PAD) >= WIDTH)),
        inner_table=split(inner_table[:, : 2 * INNER_PAD]),
        spread=as_bf16(padded(spread, PAD)),
        squeeze=as_bf16(np.pad(spread.T, ((0, PAD - WIDTH), (0, 0)))),
        lanes=as_f32(lanes),
        columns=as_f32(columns),
        along_y=as_f32(along_y),
        pick=as_bf16(pick),
        polar=as_bf16(polar_short),
        polar_back=as_bf16(polar.T),
    )


def exchange_tables(count_x, count_y, rows):
    reach_x, reach_y = ACROSS - 1, rows - 1
    side = count_x * reach_x
    ypad = -(-rows // 8) * 8

    def canonical(j, i, y, x, k):
        gy, gx = j * reach_y + y, i * reach_x + x
        if k < 4 and gx == side:
            k, gx = (k + 1) % 4, 0
        if k < 4 and gy == side:
            gx, gy = ((gx, 0), (side, gx), (side - gx, side), (0, side - gx))[k]
            k = 4
        elif k < 4 and gy == 0:
            gx, gy = ((gx, side), (side, side - gx), (side - gx, 0), (0, gx))[k]
            k = 5
        return k, gy, gx

    def swapped(source, target):
        sj, si, sy, sx, sk = source
        j, i, y, x, k = target
        if sj == j and sy == y:
            if (x, sx) == (reach_x, 0):
                if (si, sk) == (i + 1, k):
                    return True
                if i == count_x - 1 and si == 0 and k < 4 and sk == (k + 1) % 4:
                    return True
            if (x, sx) == (0, reach_x):
                if (si, sk) == (i - 1, k):
                    return True
                if i == 0 and si == count_x - 1 and k < 4 and sk == (k - 1) % 4:
                    return True
        if si == i and sx == x:
            if sk == k and (sj, sy, y) in ((j + 1, 0, reach_y), (j - 1, reach_y, 0)):
                return True
            if (j, y, sj, sy) == (0, 0, count_y - 1, reach_y) and (k, sk) in ((4, 0), (0, 5)):
                return True
            if (j, y, sj, sy) == (count_y - 1, reach_y, 0, 0) and (k, sk) in ((0, 4), (5, 0)):
                return True
        return False

    def row_of(y, x, k):
        if y == reach_y:
            return x * GROUPS + k
        if y == 0:
            return 32 + x * GROUPS + k
        return 64 + (k - 4) * 2 * ypad + (ypad if x else 0) + y

    copies = collections.defaultdict(list)
    for j in range(count_y):
        for i in range(count_x):
            for y in range(rows):
                for x in range(ACROSS):
                    if 0 < y < reach_y and 0 < x < reach_x:
                        continue
                    for k in range(GROUPS):
                        copies[canonical(j, i, y, x, k)].append((j, i, y, x, k))
    pairs = collections.defaultdict(list)
    for members in copies.values():
        for target in members:
            for source in members:
                if source != target and not swapped(source, target):
                    key = (source[1] * count_y + source[0], target[1] * count_y + target[0])
                    pairs[key].append((row_of(*source[2:]), row_of(*target[2:])))
    table = np.full((count_x * count_y, 8, ENTRIES), -1.0, np.float32)
    sent = collections.Counter()
    taken = collections.Counter()
    peers = count_x * count_y
    for (source, target), links in sorted(pairs.items()):
        assert len(links) <= RUNS * RUN_POINTS
        for slot, (row_from, row_to) in enumerate(sorted(links)):
            run, place = divmod(slot, RUN_POINTS)
            for device, peer, row, counts, base in (
                (source, target, row_from, sent, 0),
                (target, source, row_to, taken, 2),
            ):
                assert counts[device, place] < CLASS
                entry = place * CLASS + counts[device, place]
                counts[device, place] += 1
                table[device, base, entry] = run * peers + peer
                table[device, base + 1, entry] = row
    return table


bf16 = jnp.bfloat16


def parts_of(x):
    high = x.astype(bf16)
    rest = x - high.astype(jnp.float32)
    middle = rest.astype(bf16)
    return high, middle, (rest - middle.astype(jnp.float32)).astype(bf16)


def product(a, b, back=False):
    dims = (((1,), (1 if back else 0,)), ((), ()))
    return lax.dot_general(a, b, dims, preferred_element_type=jnp.float32)


def pick_right(x, chosen):
    count = x.shape[0]
    out = product(jnp.concatenate(parts_of(x), axis=0), chosen)
    return out[0:count] + out[count : 2 * count] + out[2 * count : 3 * count]


def pick_left(chosen, x):
    width = x.shape[1]
    out = product(chosen, jnp.concatenate(parts_of(x), axis=1))
    return out[:, 0:width] + out[:, width : 2 * width] + out[:, 2 * width : 3 * width]


def times(x, table, lanes, back=False):
    count = x.shape[0]
    high, middle, low = parts_of(x)
    out = product(jnp.concatenate([high, middle, low], axis=0), table[0, :, lanes], back)
    total = out[0:count] + (out[count : 2 * count] + out[2 * count : 3 * count])
    out = product(jnp.concatenate([high, middle], axis=0), table[1, :, lanes], back)
    total = total + (out[0:count] + out[count : 2 * count])
    return total


def turn_lanes(x, shift):
    shift = shift % x.shape[1]
    return pltpu.roll(x, shift, axis=1) if shift else x


def chosen_by(condition):
    return jnp.where(condition, 1.0, 0.0).astype(bf16)


def iota(shape, axis):
    return lax.broadcasted_iota(jnp.int32, shape, axis)


def put(ref, row, block):
    for t in range(ref.shape[0]):
        width = min(128, block.shape[1] - 128 * t)
        ref[t, row : row + block.shape[0], 0:width] = block[:, 128 * t : 128 * t + width]


def take(ref, c, first, count):
    tiles = [ref[t, pl.ds(4 * first + c, count, stride=4), :] for t in range(ref.shape[0])]
    return jnp.concatenate(tiles, axis=1)


def scatter(ref, c, block):
    for t in range(ref.shape[0]):
        ref[t, pl.ds(c, block.shape[0], stride=4), :] = block[:, 128 * t : 128 * t + 128]


def own_table(table_ref, count_y):
    return table_ref[lax.axis_index("xi") * count_y + lax.axis_index("eta")]


def force_kernel(
    rows,
    count_x,
    count_y,
    disp,
    vel,
    acc,
    metric,
    moduli,
    rho,
    pot,
    rate,
    accel,
    core_metric,
    kappa,
    core_rho,
    inner_disp,
    inner_vel,
    inner_acc,
    inner_metric,
    inner_moduli,
    inner_rho,
    table_ref,
    forward,
    plain_lanes,
    inner_forward,
    spread,
    lanes,
    columns,
    along_y,
    pick,
    polar,
    fields,
    send_xa,
    send_xb,
    send_ya,
    send_yb,
    send_all,
    wide,
    narrow,
    inner_rows,
    flux,
    inner_flux,
    wide_u,
    edges,
    rows_t,
    points,
    moved,
    scale,
    lame,
    core_scale,
    inner_moved,
    inner_scale,
    inner_lame,
    stack,
    shifted,
    copies,
    pot_next,
):
    ne = (rows - 1) // 4
    ypad = edges.shape[0] // 2
    half = 0.5 * time_step * time_step
    for y in range(rows):
        block = disp[y] + time_step * vel[y] + half * acc[y]
        put(moved, 4 * y, block)
        put(scale, 4 * y, metric[y])
        put(lame, 4 * y, moduli[y])
        put(core_scale, 4 * y, core_metric[y])
        block = inner_disp[y] + time_step * inner_vel[y] + half * inner_acc[y]
        put(inner_moved, 4 * y, block)
        put(inner_scale, 4 * y, inner_metric[y])
        put(inner_lame, 4 * y, inner_moduli[y])

    def part(ref, c, first=0, count=rows):
        width = WIDTH if ref.shape[0] * 128 == PAD else INNER_WIDTH
        return take(ref, c, first, count)[:, 0:width]

    pot_next[...] = pot[...] + time_step * rate[...] + half * accel[...]

    slope = along_y[0:5, 0:5]
    slope_back = along_y[8:13, 0:5]

    def along(matrix, block):
        total = matrix[:, 0:1] * block[0:1, :]
        for b in range(1, 5):
            total = total + matrix[:, b : b + 1] * block[b : b + 1, :]
        return total

    narrow[:, TILE:PAD] = jnp.zeros((narrow.shape[0], PAD - TILE), jnp.float32)
    for first in (0, INNER_PAD):
        inner_flux[:, first + 128 : first + 256] = jnp.zeros((inner_flux.shape[0], 128), jnp.float32)
    stack[...] = jnp.zeros(stack.shape, jnp.float32)
    fields[...] = jnp.zeros(fields.shape, jnp.float32)

    def slot(f, e):
        return (f * ne + e) * 8

    extras = [(scale, c) for c in range(3)] + [(lame, c) for c in range(2)] + [(core_scale, c) for c in range(3)]
    for e in range(ne):
        for f in range(4):
            block = part(moved, f, 4 * e, 5) if f < 3 else pot_next[4 * e : 4 * e + 5, :]
            wide[slot(f, e) : slot(f, e) + 5, :] = block
            narrow[slot(f, e) : slot(f, e) + 5, 0:WIDTH] = along(slope, block)
        for f, (ref, c) in enumerate(extras):
            narrow[slot(4 + f, e) : slot(4 + f, e) + 5, 0:WIDTH] = part(ref, c, 4 * e, 5)
        narrow[slot(12, e) : slot(12, e) + 5, 0:WIDTH] = core_rho[4 * e : 4 * e + 5, :]
        for f in range(3):
            inner_rows[slot(f, e) : slot(f, e) + 5, :] = part(inner_moved, f, 4 * e, 5)
    whole = slice(None)
    slopes_xr = times(wide[...], forward, whole)
    copies[...] = narrow[:, TILE:PAD] + pick_right(narrow[:, 0:WIDTH], plain_lanes[...])
    inner_xr = times(inner_rows[...], inner_forward, whole)

    def elastic(g, lam, mu, sy, sx, sr, jw):
        scaled = [[sy[i] * g[0], sx[i] * g[1], sr[i] * g[2]] for i in range(3)]
        trace = lam * (scaled[0][0] + scaled[1][1] + scaled[2][2])
        out = [[None] * 3 for _ in range(3)]
        weighted = [jw * g[m] for m in range(3)]
        for i in range(3):
            for m in range(3):
                if i == m:
                    stress = 2.0 * mu * scaled[i][i] + trace
                else:
                    stress = mu * (scaled[i][m] + scaled[m][i])
                out[i][m] = stress * weighted[m]
        return out

    row_weight = columns[0:5, 1:2]
    valid = (iota((5, PAD), 1) < NODES) & (iota((5, PAD), 0) < 5)
    for e in range(ne):
        def plain(f):
            at = slice(slot(f, e), slot(f, e) + 5)
            return jnp.concatenate([narrow[at, 0:TILE], copies[at, :]], axis=1)

        def x_of(f):
            return slopes_xr[slot(f, e) : slot(f, e) + 5, 0:PAD]

        def r_of(f):
            return slopes_xr[slot(f, e) : slot(f, e) + 5, PAD : 2 * PAD]

        node = row_weight * lanes[0:1, :]
        g = [jnp.where(valid, plain(4 + m), 1.0) for m in range(3)]
        q = elastic(
            g,
            plain(7),
            plain(8),
            [plain(f) for f in range(3)],
            [x_of(f) for f in range(3)],
            [r_of(f) for f in range(3)],
            node / (g[0] * g[1] * g[2]),
        )
        g = [jnp.where(valid, plain(9 + m), 1.0) for m in range(3)]
        volume = node / (g[0] * g[1] * g[2] * jnp.where(valid, plain(12), 1.0))
        q.append(
            [
                volume * g[0] * g[0] * plain(3),
                volume * g[1] * g[1] * x_of(3),
                volume * g[2] * g[2] * r_of(3),
            ]
        )
        for f in range(4):
            at = slot(f, e)
            flux[at : at + 5, 0:PAD] = q[f][1]
            flux[at : at + 5, PAD : 2 * PAD] = q[f][2]
            flux[at : at + 5, 2 * PAD : 3 * PAD] = along(slope_back, q[f][0])

        def inner_x(f):
            return inner_xr[slot(f, e) : slot(f, e) + 5, 0:INNER_WIDTH]

        def inner_r(f):
            return inner_xr[slot(f, e) : slot(f, e) + 5, INNER_PAD : INNER_PAD + INNER_WIDTH]

        g = [part(inner_scale, m, 4 * e, 5) for m in range(3)]
        node = row_weight * lanes[3:4, 0:INNER_WIDTH]
        q = elastic(
            g,
            part(inner_lame, 0, 4 * e, 5),
            part(inner_lame, 1, 4 * e, 5),
            [along(slope, inner_rows[slot(f, e) : slot(f, e) + 5, :]) for f in range(3)],
            [inner_x(f) for f in range(3)],
            [inner_r(f) for f in range(3)],
            node / (g[0] * g[1] * g[2]),
        )
        for f in range(3):
            at = slot(f, e)
            inner_flux[at : at + 5, 0:INNER_WIDTH] = q[f][1]
            inner_flux[at : at + 5, INNER_PAD : INNER_PAD + INNER_WIDTH] = q[f][2]
            inner_flux[at : at + 5, 2 * INNER_PAD : 2 * INNER_PAD + INNER_WIDTH] = along(slope_back, q[f][0])

    back = times(flux[:, 0 : 2 * PAD], forward, whole, back=True)
    count = flux.shape[0]
    out = product(
        jnp.concatenate(parts_of(flux[:, 2 * PAD + TILE : 3 * PAD]), axis=0), plain_lanes[...], back=True
    )
    back = back + flux[:, 2 * PAD : 2 * PAD + WIDTH] + (out[0:count] + out[count : 2 * count] + out[2 * count : 3 * count])
    count = 3 * ne * 8
    stack[0:count, :] = (
        times(inner_flux[:, 0 : 2 * INNER_PAD], inner_forward, whole, back=True)
        + inner_flux[:, 2 * INNER_PAD : 2 * INNER_PAD + INNER_WIDTH]
    )
    lumped_y = columns[0:rows, 0:1]
    stack[count : count + rows, :] = inner_rho[...] * (
        lumped_y * lanes[4:5, 0:INNER_WIDTH] / (part(inner_scale, 0) * part(inner_scale, 1) * part(inner_scale, 2))
    )
    stack[count + ypad : count + ypad + rows, :] = part(inner_moved, 2)
    spreads = pick_right(stack[...], spread[...])
    inner_forces = spreads[0:count, 0:WIDTH]
    for e in range(ne):
        here = slice(4 * e, 4 * e + 5)
        for f in range(3):
            fields[f, here, 0:WIDTH] = fields[f, here, 0:WIDTH] - back[slot(f, e) : slot(f, e) + 5, :]
            fields[IF + f, here, 0:WIDTH] = fields[IF + f, here, 0:WIDTH] - inner_forces[slot(f, e) : slot(f, e) + 5, :]
        fields[CF, here, 0:WIDTH] = fields[CF, here, 0:WIDTH] - back[slot(3, e) : slot(3, e) + 5, :]

    lumped = lumped_y * lanes[1:2, 0:WIDTH]
    fields[MM, 0:rows, 0:WIDTH] = rho[...] * (lumped / (part(scale, 0) * part(scale, 1) * part(scale, 2)))
    fields[CM, 0:rows, 0:WIDTH] = lumped / (part(core_scale, 0) * part(core_scale, 1) * part(core_scale, 2)) / kappa[...]
    fields[IM, 0:rows, :] = spreads[count : count + rows]
    radial = lax.rem(iota((rows, WIDTH), 1), RADIAL)
    face = lumped_y * lanes[2:3, 0:WIDTH] / (part(core_scale, 0) * part(core_scale, 1))
    face = jnp.where((radial == 0) | (radial == RADIAL - 1), face, 0.0)
    fields[CW, 0:rows, 0:WIDTH] = face
    wide_u[...] = jnp.zeros(wide_u.shape, jnp.float32)
    wide_u[0:rows, 0:WIDTH] = part(moved, 2)
    above = pltpu.roll(wide_u[...], RADIAL - 1, axis=1)
    below = pltpu.roll(spreads[count + ypad : count + 2 * ypad], PAD - (INNER_RADIAL - 1), axis=1)
    radial = lax.rem(iota((ypad, PAD), 1), RADIAL)
    jump = jnp.where(radial == RADIAL - 1, above, jnp.where(radial == 0, -below, 0.0))
    fields[CF] = fields[CF] + fields[CW] * jump

    low = iota((ypad, 128), 1) < 64
    for p in range(PAIRS):
        left = fields[2 * p]
        right = fields[2 * p + 1] if 2 * p + 1 < FIELDS else jnp.zeros_like(left)
        edges[0:ypad, p * 128 : p * 128 + 128] = jnp.where(low, left[:, 0:128], pltpu.roll(right[:, 0:128], 64, axis=1))
        edges[ypad : 2 * ypad, p * 128 : p * 128 + 128] = jnp.where(
            low,
            pltpu.roll(left, PAD - (WIDTH - COLUMN), axis=1)[:, 0:128],
            pltpu.roll(right, PAD + 64 - (WIDTH - COLUMN), axis=1)[:, 0:128],
        )
    even_x = lax.rem(lax.axis_index("xi"), 2) == 0
    even_y = lax.rem(lax.axis_index("eta"), 2) == 0
    for p in range(PAIRS):
        first = edges[0:rows, p * 128 : p * 128 + 128]
        last = edges[ypad : ypad + rows, p * 128 : p * 128 + 128]
        send_xa[p * rows : (p + 1) * rows, :] = jnp.where(even_x, last, first)
        send_xb[p * rows : (p + 1) * rows, :] = jnp.where(even_x, first, last)
    rows_t[0:16, :] = jnp.zeros((16, PAD), jnp.float32)
    rows_t[64:80, :] = jnp.zeros((16, PAD), jnp.float32)
    for f in range(FIELDS):
        rows_t[f : f + 1, :] = fields[f, rows - 1 : rows, :]
        rows_t[64 + f : 65 + f, :] = fields[f, 0:1, :]
    top = rows_t[0:16, :]
    bottom = rows_t[64:80, :]
    send_ya[...] = jnp.where(even_y, top, bottom)
    send_yb[...] = jnp.where(even_y, bottom, top)

    for at, block in ((0, top), (64, bottom)):
        for n, piece in enumerate(parts_of(block)):
            rows_t[at + 16 * n : at + 16 * n + 16, :] = piece.astype(jnp.float32)
    by_line = product(pick[...], rows_t[...].astype(bf16), back=True)
    by_line = by_line + (pltpu.roll(by_line, 128 - 16, axis=1) + pltpu.roll(by_line, 128 - 32, axis=1))
    lane = iota((32, 128), 1)
    top_points = jnp.zeros((32, 128), jnp.float32)
    bottom_points = jnp.zeros((32, 128), jnp.float32)
    for r in range(RADIAL):
        block = by_line[32 * r : 32 * r + 32, :]
        for first, end, at in runs_of(r):
            upper = jnp.where((lane >= first) & (lane < end), block, 0.0)
            lower = jnp.where((lane >= 64 + first) & (lane < 64 + end), block, 0.0)
            top_points = top_points + turn_lanes(upper, at - first)
            bottom_points = bottom_points + turn_lanes(lower, at - first - 64)
    points[0:32, :] = top_points
    points[32:64, :] = bottom_points
    third = lax.rem(iota((2 * ypad, 128), 1), 64)
    tiles = []
    for t in range(2):
        tile = jnp.zeros((2 * ypad, 128), jnp.float32)
        for j in range(3):
            p = 3 * t + j
            block = turn_lanes(edges[:, p * 128 : p * 128 + 128], 2 * RADIAL * j - 4 * RADIAL)
            tile = jnp.where((third >= 2 * RADIAL * j) & (third < 2 * RADIAL * (j + 1)), block, tile)
        tiles.append(tile)
    caps = pick_right(jnp.concatenate(tiles, axis=1), polar[...])
    points[64 : 64 + 2 * ypad, :] = caps[:, 0:128]
    points[64 + 2 * ypad : 64 + 4 * ypad, :] = caps[:, 128:256]

    own = own_table(table_ref, count_y)
    turned = jnp.transpose(own)
    count = points.shape[0]
    chosen = chosen_by(turned[:, 1:2] == iota((ENTRIES, count), 1).astype(jnp.float32))
    chosen = pick_left(chosen, points[...])
    shifted[...] = jnp.zeros(shifted.shape, jnp.float32)
    lane = iota((CLASS, 128), 1)
    for place in range(RUN_POINTS):
        tile, shift = divmod(place * CHANNELS, 128)
        here = slice(place * CLASS, (place + 1) * CLASS)
        block = turn_lanes(chosen[here], shift)
        shifted[here, tile * 128 : tile * 128 + 128] = jnp.where(lane >= shift, block, 0.0)
        if shift + CHANNELS > 128:
            shifted[here, tile * 128 + 128 : tile * 128 + 256] = jnp.where(lane < shift, block, 0.0)
    peers = count_x * count_y
    number = iota((RUNS * peers, ENTRIES), 0).astype(jnp.float32)
    placed = pick_left(chosen_by(own[0:1, :] == number), shifted[...])
    for row in range(BLOCK):
        run, tile = divmod(row, RUN_ROWS)
        if run < RUNS:
            block = placed[run * peers : (run + 1) * peers, tile * 128 : tile * 128 + 128]
        else:
            block = jnp.zeros((peers, 128), jnp.float32)
        send_all[pl.ds(row, peers, stride=BLOCK), :] = block


def window_kernel(
    disp,
    vel,
    acc,
    pot,
    rate,
    accel,
    inner_disp,
    inner_vel,
    inner_acc,
    fields,
    disp_next,
    pot_next,
    inner_next,
    vel_half,
    rate_half,
    inner_half,
    fields_out,
):
    half = 0.5 * time_step
    for new, between, place, speed, change in (
        (disp_next, vel_half, disp, vel, acc),
        (pot_next, rate_half, pot, rate, accel),
        (inner_next, inner_half, inner_disp, inner_vel, inner_acc),
    ):
        new[...] = place[...] + time_step * speed[...] + half * time_step * change[...]
        between[...] = speed[...] + half * change[...]
    fields_out[...] = fields[...]


def close_kernel(
    rows,
    count_x,
    count_y,
    got_xa,
    got_xb,
    got_ya,
    got_yb,
    got_all,
    fields,
    vel_half,
    rate_half,
    inner_half,
    table_ref,
    pick,
    polar_back,
    squeeze,
    vel_next,
    acc_next,
    rate_next,
    accel_next,
    inner_vel_next,
    inner_acc_next,
    total,
    by_line,
    caps,
    narrow,
    wide,
    runs,
    arrived,
):
    ypad = total.shape[1]
    narrow[...] = jnp.zeros(narrow.shape, jnp.float32)
    own = own_table(table_ref, count_y)
    turned = jnp.transpose(own)
    peers = count_x * count_y
    for run in range(RUNS):
        for tile in range(RUN_ROWS):
            runs[run * peers : (run + 1) * peers, tile * 128 : tile * 128 + 128] = got_all[
                pl.ds(run * RUN_ROWS + tile, peers, stride=BLOCK), :
            ]
    number = iota((ENTRIES, RUNS * peers), 1).astype(jnp.float32)
    shifted = pick_left(chosen_by(turned[:, 2:3] == number), runs[...])
    lane = iota((CLASS, 128), 1)
    arrived[...] = jnp.zeros(arrived.shape, jnp.float32)
    for place in range(RUN_POINTS):
        tile, shift = divmod(place * CHANNELS, 128)
        here = slice(place * CLASS, (place + 1) * CLASS)
        block = shifted[here, tile * 128 : tile * 128 + 128]
        if shift + CHANNELS > 128:
            block = jnp.where(lane >= shift, block, shifted[here, tile * 128 + 128 : tile * 128 + 256])
        arrived[here, :] = jnp.where(lane < CHANNELS, turn_lanes(block, -shift), 0.0)
    count = 64 + 4 * ypad
    points = pick_left(chosen_by(own[3:4, :] == iota((count, ENTRIES), 0).astype(jnp.float32)), arrived[...])
    lane = iota((32, 128), 1)
    upper = points[0:32]
    lower = points[32:64]
    for r in range(RADIAL):
        block = jnp.zeros((32, 128), jnp.float32)
        for first, end, at in runs_of(r):
            high = turn_lanes(upper, first - at)
            low = turn_lanes(lower, 64 + first - at)
            block = jnp.where((lane >= first) & (lane < end), high, block)
            block = jnp.where((lane >= 64 + first) & (lane < 64 + end), low, block)
        high, middle, last = (piece.astype(jnp.float32) for piece in parts_of(block))
        by_line[32 * r : 32 * r + 32, :] = (
            high + pltpu.roll(middle, 16, axis=1) + pltpu.roll(last, 32, axis=1)
        )
    lines = lax.dot_general(
        by_line[...].astype(bf16), pick[...], (((0,), (0,)), ((), ())), preferred_element_type=jnp.float32
    )
    lines_top = lines[0:16] + (lines[16:32] + lines[32:48])
    lines_bottom = lines[64:80] + (lines[80:96] + lines[96:112])
    caps[:, 0:128] = points[64 : 64 + 2 * ypad]
    caps[:, 128:256] = points[64 + 2 * ypad : 64 + 4 * ypad]
    columns = pick_right(caps[...], polar_back[...])

    xi = lax.axis_index("xi")
    eta = lax.axis_index("eta")
    even_x = lax.rem(xi, 2) == 0
    even_y = lax.rem(eta, 2) == 0
    lane = iota((16, PAD), 1)
    group = lax.rem(lane // RADIAL, GROUPS)
    used = lane < WIDTH
    ya = got_ya[...]
    yb = got_yb[...]
    from_above = jnp.where(even_y, ya, yb)
    from_below = jnp.where(even_y, yb, ya)
    four, five = 4 * RADIAL, 5 * RADIAL
    seam_top = jnp.where(
        group == 0,
        pltpu.roll(from_above, PAD - four, axis=1),
        jnp.where(group == 5, pltpu.roll(from_above, five, axis=1), 0.0),
    )
    seam_bottom = jnp.where(
        group == 4,
        pltpu.roll(from_below, four, axis=1),
        jnp.where(group == 0, pltpu.roll(from_below, PAD - five, axis=1), 0.0),
    )
    add_top = jnp.where(eta == count_y - 1, seam_top, from_above) + lines_top
    add_bottom = jnp.where(eta == 0, seam_bottom, from_below) + lines_bottom
    add_top = jnp.where(used, add_top, 0.0)
    add_bottom = jnp.where(used, add_bottom, 0.0)
    total[...] = fields[...]
    lane = iota((rows, 128), 1)
    inside = lax.rem(lane, 64)
    equator = inside < 4 * RADIAL
    keep = inside < COLUMN
    low = lane < 64
    last_x = xi == count_x - 1
    for p in range(PAIRS):
        xa = got_xa[p * rows : (p + 1) * rows, :]
        xb = got_xb[p * rows : (p + 1) * rows, :]
        from_right = jnp.where(even_x, xa, xb)
        from_left = jnp.where(even_x, xb, xa)
        up = jnp.where(
            inside < 3 * RADIAL,
            pltpu.roll(from_right, 128 - RADIAL, axis=1),
            pltpu.roll(from_right, 3 * RADIAL, axis=1),
        )
        down = jnp.where(
            inside < RADIAL,
            pltpu.roll(from_left, 128 - 3 * RADIAL, axis=1),
            pltpu.roll(from_left, RADIAL, axis=1),
        )
        from_right = jnp.where(last_x, jnp.where(equator, up, 0.0), from_right)
        from_left = jnp.where(xi == 0, jnp.where(equator, down, 0.0), from_left)
        at = slice(p * 128, p * 128 + 128)
        from_left = jnp.where(keep, from_left + columns[0:rows, at], 0.0)
        from_right = jnp.where(keep, from_right + columns[ypad : ypad + rows, at], 0.0)
        zero = jnp.zeros((rows, PAD - 128), jnp.float32)
        for h in range(2):
            f = 2 * p + h
            if f >= FIELDS:
                continue
            mine = low if h == 0 else ~low
            left = jnp.where(mine, from_left, 0.0)
            right = jnp.where(mine, from_right, 0.0)
            if h:
                left = pltpu.roll(left, 64, axis=1)
            total[f, 0:rows, 0:128] = total[f, 0:rows, 0:128] + left
            right = jnp.concatenate([right, zero], axis=1)
            right = pltpu.roll(right, WIDTH - COLUMN - 64 * h, axis=1)
            total[f, 0:rows, :] = total[f, 0:rows, :] + right
    for f in range(FIELDS):
        total[f, rows - 1 : rows, :] = total[f, rows - 1 : rows, :] + add_top[f : f + 1, :]
        total[f, 0:1, :] = total[f, 0:1, :] + add_bottom[f : f + 1, :]

    half = 0.5 * time_step
    lane = iota((ypad, PAD), 1)
    radial = lax.rem(lane, RADIAL)
    inside = (lane < WIDTH) & (iota((ypad, PAD), 0) < rows)
    core = total[CF] / jnp.where(inside, total[CM], 1.0)
    accel_next[...] = core[0:rows, 0:WIDTH]
    rate_next[...] = rate_half[...] + half * core[0:rows, 0:WIDTH]
    push = total[CW] * core
    top = jnp.where(radial == 0, pltpu.roll(push, PAD - (RADIAL - 1), axis=1), 0.0)
    bottom = jnp.where(radial == INNER_RADIAL - 1, pltpu.roll(push, INNER_RADIAL - 1, axis=1), 0.0)
    mass = jnp.where(inside, total[MM], 1.0)
    inner_mass = jnp.where(inside & (radial < INNER_RADIAL), total[IM], 1.0)
    for f in range(3):
        force = total[f] + top if f == 2 else total[f]
        result = (force / mass)[0:rows]
        scatter(wide, f, result)
        force = total[IF + f] - bottom if f == 2 else total[IF + f]
        scatter(narrow, f, (force / inner_mass)[0:rows])
    squeezed = pick_right(jnp.concatenate([narrow[t] for t in range(PAD // 128)], axis=1), squeeze[...])
    for y in range(rows):
        result = jnp.concatenate([wide[t, 4 * y : 4 * y + 3, :] for t in range(PAD // 128)], axis=1)[:, 0:WIDTH]
        acc_next[y] = result
        vel_next[y] = vel_half[y] + half * result
        result = squeezed[4 * y : 4 * y + 3, :]
        inner_acc_next[y] = result
        inner_vel_next[y] = inner_half[y] + half * result


def shards(
    count_x,
    count_y,
    mantle_disp,
    mantle_vel,
    mantle_acc,
    mantle_metric,
    mantle_moduli,
    mantle_rho,
    core_pot,
    core_rate,
    core_accel,
    core_metric,
    core_kappa,
    core_rho,
    inner_disp,
    inner_vel,
    inner_acc,
    inner_metric,
    inner_moduli,
    inner_rho,
):
    rows = mantle_disp.shape[1]
    turn = lambda a: jnp.transpose(a, (1, 0, 2))
    mantle_disp, mantle_vel, mantle_acc = turn(mantle_disp), turn(mantle_vel), turn(mantle_acc)
    mantle_metric, mantle_moduli, core_metric = turn(mantle_metric), turn(mantle_moduli), turn(core_metric)
    inner_disp, inner_vel, inner_acc = turn(inner_disp), turn(inner_vel), turn(inner_acc)
    inner_metric, inner_moduli = turn(inner_metric), turn(inner_moduli)
    ne = (rows - 1) // 4
    ypad = -(-rows // 8) * 8
    tables = {name: jnp.asarray(value) for name, value in constants(rows).items()}
    table = jnp.asarray(exchange_tables(count_x, count_y, rows))
    f32 = jnp.float32
    like = lambda a: jax.ShapeDtypeStruct(a.shape, f32)
    shape = lambda *s: jax.ShapeDtypeStruct(s, f32)
    devices = count_x * count_y
    edge = -(-PAIRS * rows // 8) * 8
    (fields, xa, xb, ya, yb, everyone) = pl.pallas_call(
        functools.partial(force_kernel, rows, count_x, count_y),
        out_shape=[
            shape(FIELDS, ypad, PAD),
            shape(edge, 128),
            shape(edge, 128),
            shape(16, PAD),
            shape(16, PAD),
            shape(devices * BLOCK, 128),
        ],
        scratch_shapes=[
            pltpu.VMEM((4 * ne * 8, WIDTH), f32),
            pltpu.VMEM((13 * ne * 8, PAD), f32),
            pltpu.VMEM((3 * ne * 8, INNER_WIDTH), f32),
            pltpu.VMEM((4 * ne * 8, 3 * PAD), f32),
            pltpu.VMEM((3 * ne * 8, 3 * INNER_PAD), f32),
            pltpu.VMEM((ypad, PAD), f32),
            pltpu.VMEM((2 * ypad, PAIRS * 128), f32),
            pltpu.VMEM((128, PAD), f32),
            pltpu.VMEM((64 + 4 * ypad, 128), f32),
        ]
        + [pltpu.VMEM((PAD // 128, 4 * rows, 128), f32)] * 4
        + [pltpu.VMEM((INNER_PAD // 128, 4 * rows, 128), f32)] * 3
        + [pltpu.VMEM((3 * ne * 8 + 2 * ypad, INNER_WIDTH), f32)]
        + [pltpu.VMEM((ENTRIES, RUN_ROWS * 128), f32)]
        + [pltpu.VMEM((13 * ne * 8, PAD - TILE), f32)]
        + [pltpu.VMEM((rows, WIDTH), f32)],
        name="forces",
    )(
        mantle_disp,
        mantle_vel,
        mantle_acc,
        mantle_metric,
        mantle_moduli,
        mantle_rho,
        core_pot,
        core_rate,
        core_accel,
        core_metric,
        core_kappa,
        core_rho,
        inner_disp,
        inner_vel,
        inner_acc,
        inner_metric,
        inner_moduli,
        inner_rho,
        table,
        tables["table"],
        tables["plain"],
        tables["inner_table"],
        tables["spread"],
        tables["lanes"],
        tables["columns"],
        tables["along_y"],
        tables["pick"],
        tables["polar"],
    )
    everyone = lax.all_to_all(everyone, ("xi", "eta"), 0, 0, tiled=True)
    near = [(i, i ^ 1) for i in range(count_x)]
    far = [(i, (i - 1 if i % 2 == 0 else i + 1) % count_x) for i in range(count_x)]
    xa = lax.ppermute(xa, "xi", near)
    xb = lax.ppermute(xb, "xi", far)
    near = [(j, j ^ 1) for j in range(count_y)]
    far = [(j, (j - 1 if j % 2 == 0 else j + 1) % count_y) for j in range(count_y)]
    ya = lax.ppermute(ya, "eta", near)
    yb = lax.ppermute(yb, "eta", far)
    (mantle_next, core_next, inner_next, vel_half, rate_half, inner_half, fields) = pl.pallas_call(
        window_kernel,
        out_shape=[like(a) for a in (mantle_disp, core_pot, inner_disp) * 2] + [like(fields)],
        compiler_params=pltpu.CompilerParams(vmem_limit_bytes=WINDOW_GRANT),
        name="window",
    )(mantle_disp, mantle_vel, mantle_acc, core_pot, core_rate, core_accel, inner_disp, inner_vel, inner_acc, fields)
    (mantle_vel_next, mantle_acc_next, core_rate_next, core_acc_next, inner_vel_next, inner_acc_next) = pl.pallas_call(
        functools.partial(close_kernel, rows, count_x, count_y),
        out_shape=[
            like(mantle_vel),
            like(mantle_acc),
            like(core_rate),
            like(core_accel),
            like(inner_vel),
            like(inner_acc),
        ],
        scratch_shapes=[
            pltpu.VMEM((FIELDS, ypad, PAD), f32),
            pltpu.VMEM((RADIAL * 32, 128), f32),
            pltpu.VMEM((2 * ypad, 256), f32),
            pltpu.VMEM((PAD // 128, -(-4 * rows // 16) * 16, 128), f32),
            pltpu.VMEM((PAD // 128, 4 * rows, 128), f32),
            pltpu.VMEM((RUNS * devices, RUN_ROWS * 128), f32),
            pltpu.VMEM((ENTRIES, 128), f32),
        ],
        compiler_params=pltpu.CompilerParams(vmem_limit_bytes=(8 << 20) + devices * (48 << 10)),
        name="close",
    )(
        xa,
        xb,
        ya,
        yb,
        everyone,
        fields,
        vel_half,
        rate_half,
        inner_half,
        table,
        tables["pick"],
        tables["polar_back"],
        tables["squeeze"],
    )
    return (
        turn(mantle_next),
        turn(mantle_vel_next),
        turn(mantle_acc_next),
        core_next,
        core_rate_next,
        core_acc_next,
        turn(inner_next),
        turn(inner_vel_next),
        turn(inner_acc_next),
    )


def solution(mesh):
    count_x, count_y = mesh.shape["xi"], mesh.shape["eta"]
    assert count_x % 2 == 0 and count_y % 2 == 0
    assert (count_x * count_y) % 8 == 0
    vector, scalar = P(None, "eta", "xi"), P("eta", "xi")
    placed = (vector,) * 5 + (scalar,) * 4 + (vector,) + (scalar,) * 2 + (vector,) * 5 + (scalar,)
    return jax.shard_map(
        functools.partial(shards, count_x, count_y),
        mesh=mesh,
        in_specs=placed,
        out_specs=(vector,) * 3 + (scalar,) * 3 + (vector,) * 3,
        check_vma=False,
    )
```

```python
import collections
import functools
import math

import jax
import jax.numpy as jnp
import numpy as np
from jax import lax
from jax.experimental import pallas as pl
from jax.experimental.pallas import tpu as pltpu
from jax.sharding import PartitionSpec as P


EX = 1
MANTLE_LAYERS = 2
INNER_LAYERS = 1
GROUPS = 6
ACROSS = 4 * EX + 1
RADIAL = 4 * MANTLE_LAYERS + 1
INNER_RADIAL = 4 * INNER_LAYERS + 1
LINES = ACROSS * GROUPS
WIDTH = LINES * RADIAL
INNER_WIDTH = LINES * INNER_RADIAL
COLUMN = GROUPS * RADIAL
NODES = LINES * 5 * MANTLE_LAYERS
PAD = 384
INNER_PAD = 256
TILE = 256
TAIL = 64
SLOPES = 2 * TILE + 2 * TAIL
INNER_SLOPES = 2 * 128 + 2 * TAIL
ENTRIES = 128
BLOCK = 8
RUN_ROWS = 3
RUN_POINTS = 5
RUNS = 2
CLASS = 24
WINDOW_GRANT = 8 << 20
time_step = 0.1

MM, CF, CM, IF, IM, CW, FIELDS = 3, 4, 5, 6, 9, 10, 11
PAIRS = 6
CHANNELS = 10 * INNER_RADIAL + 6 * (RADIAL - INNER_RADIAL) + 2


def channel(r, f):
    if f == CW:
        return {0: CHANNELS - 2, RADIAL - 1: CHANNELS - 1}.get(r)
    if r < INNER_RADIAL:
        return 10 * r + f
    return 10 * INNER_RADIAL + 6 * (r - INNER_RADIAL) + f if f < IF else None


def runs_of(r):
    out = [(0, IF if r >= INNER_RADIAL else CW, channel(r, 0))]
    if channel(r, CW) is not None:
        out.append((CW, FIELDS, channel(r, CW)))
    return out


def gll_tables():
    radical = math.sqrt(3.0 / 7.0)
    points = np.array([-1.0, -radical, 0.0, radical, 1.0])
    weights = np.array([0.1, 49.0 / 90.0, 32.0 / 45.0, 49.0 / 90.0, 0.1])
    products = np.array(
        [np.prod([points[a] - points[c] for c in range(5) if c != a]) for a in range(5)]
    )
    slopes = np.zeros((5, 5))
    for a in range(5):
        for b in range(5):
            if a == b:
                slopes[a, b] = np.sum([1.0 / (points[a] - points[c]) for c in range(5) if c != a])
            else:
                slopes[a, b] = products[a] / (products[b] * (points[a] - points[b]))
    return weights, slopes


def short_slopes():
    slopes = gll_tables()[1]
    round_bf16 = lambda v: float(np.float32(v).astype(jnp.bfloat16))
    high = np.vectorize(round_bf16)(slopes)
    low = np.vectorize(round_bf16)(slopes - high)
    for a in range(5):
        for _ in range(3):
            for b in np.argsort(np.abs(low[a])):
                excess = np.sum(high[a]) + np.sum(low[a])
                low[a, b] = round_bf16(low[a, b] - excess)
    return high + low


def spread_table(count):
    spread = np.zeros((4 * count + 1, 5 * count))
    for element in range(count):
        for node in range(5):
            spread[4 * element + node, 5 * element + node] = 1.0
    return spread


def padded(table, width):
    return np.pad(table, ((0, 0), (0, width - table.shape[1])))


def lane_tables(layers, width):
    weights, slopes = gll_tables()[0], short_slopes()
    spread = spread_table(layers)
    derive = np.kron(np.eye(layers), slopes.T)
    eye_k = np.eye(GROUPS)
    along_x = np.kron(slopes.T, np.kron(eye_k, spread))
    along_r = np.kron(np.eye(ACROSS), np.kron(eye_k, spread @ derive))
    plain = np.kron(np.eye(ACROSS), np.kron(eye_k, spread))
    node = np.kron(weights, np.kron(np.ones(GROUPS), np.tile(weights, layers)))
    lumped_r = spread @ np.tile(weights, layers)
    lumped = np.kron(weights, np.kron(np.ones(GROUPS), lumped_r))
    order = node_order(layers)
    node = node[order]
    table = np.concatenate([padded(t[:, order], width) for t in (along_x, along_r, plain)], axis=1)
    return table.astype(np.float32), node.astype(np.float32), lumped.astype(np.float32)


def node_order(layers):
    radial = [max(0, (r - 1) // 4) for r in range(4 * layers + 1)]
    plain = [line * 5 * layers + 5 * e + r - 4 * e for line in range(LINES) for r, e in enumerate(radial)]
    return plain + [line * 5 * layers + 5 * e for e in range(1, layers) for line in range(LINES)]


def constants(rows_local):
    weights, slopes = gll_tables()
    count_y = (rows_local - 1) // 4
    ypad = -(-rows_local // 8) * 8
    table, node, lumped = lane_tables(MANTLE_LAYERS, PAD)
    inner_table, inner_node, inner_lumped = lane_tables(INNER_LAYERS, INNER_PAD)
    small = np.eye(RADIAL)[:INNER_RADIAL]
    spread = np.kron(np.eye(LINES), small)
    lumped_y = spread_table(count_y) @ np.tile(weights, count_y)
    lanes = np.zeros((8, PAD))
    lanes[0, :NODES] = node
    lanes[1, :WIDTH] = lumped
    lanes[2, :WIDTH] = np.kron(weights, np.ones(COLUMN))
    lanes[3, : INNER_WIDTH] = inner_node
    lanes[4, : INNER_WIDTH] = inner_lumped
    columns = np.zeros((ypad, 8))
    columns[:rows_local, 0] = lumped_y
    columns[:5, 1] = weights
    along_y = np.zeros((16, 8))
    along_y[:5, :5] = slopes
    along_y[8:13, :5] = slopes.T
    pick = np.zeros((RADIAL * 32, PAD))
    for r in range(RADIAL):
        for line in range(LINES):
            pick[r * 32 + line, line * RADIAL + r] = 1.0
    polar = np.zeros((PAIRS * 128, 256))
    for f in range(FIELDS):
        for k in (4, 5):
            for r in range(RADIAL):
                if channel(r, f) is not None:
                    polar[(f // 2) * 128 + (f % 2) * 64 + k * RADIAL + r, (k - 4) * 128 + channel(r, f)] = 1.0
    polar_short = np.zeros((2 * 128, 256))
    for f in range(FIELDS):
        for k in (4, 5):
            for r in range(RADIAL):
                if channel(r, f) is not None:
                    row = (f // 6) * 128 + (f % 2) * 64 + (f // 2 % 3) * 2 * RADIAL + (k - 4) * RADIAL + r
                    polar_short[row, (k - 4) * 128 + channel(r, f)] = 1.0
    as_f32 = lambda t: np.asarray(t, np.float32)
    as_bf16 = lambda t: np.asarray(t, np.float32).astype(bf16)

    def split(t):
        rest = as_f32(t)
        out = []
        for _ in range(2):
            out.append(rest.astype(bf16))
            rest = rest - out[-1].astype(np.float32)
        return np.stack(out)

    return dict(
        table=split(
            np.concatenate([table[:, a : a + n] for a, n in ((0, TILE), (PAD, TILE), (TILE, TAIL), (PAD + TILE, TAIL))], axis=1)
        ),
        plain=as_bf16(table[:, 2 * PAD + TILE :] * (np.arange(TILE, PAD) >= WIDTH)),
        inner_table=split(
            np.concatenate(
                [inner_table[:, a : a + n] for a, n in ((0, 128), (INNER_PAD, 128), (128, TAIL), (INNER_PAD + 128, TAIL))],
                axis=1,
            )
        ),
        spread=as_bf16(padded(spread, PAD)),
        squeeze=as_bf16(np.pad(spread.T, ((0, PAD - WIDTH), (0, 0)))),
        lanes=as_f32(lanes),
        columns=as_f32(columns),
        along_y=as_f32(along_y),
        pick=as_bf16(pick),
        polar=as_bf16(polar_short),
        polar_back=as_bf16(polar.T),
    )


def exchange_tables(count_x, count_y, rows):
    reach_x, reach_y = ACROSS - 1, rows - 1
    side = count_x * reach_x
    ypad = -(-rows // 8) * 8

    def canonical(j, i, y, x, k):
        gy, gx = j * reach_y + y, i * reach_x + x
        if k < 4 and gx == side:
            k, gx = (k + 1) % 4, 0
        if k < 4 and gy == side:
            gx, gy = ((gx, 0), (side, gx), (side - gx, side), (0, side - gx))[k]
            k = 4
        elif k < 4 and gy == 0:
            gx, gy = ((gx, side), (side, side - gx), (side - gx, 0), (0, gx))[k]
            k = 5
        return k, gy, gx

    def swapped(source, target):
        sj, si, sy, sx, sk = source
        j, i, y, x, k = target
        if sj == j and sy == y:
            if (x, sx) == (reach_x, 0):
                if (si, sk) == (i + 1, k):
                    return True
                if i == count_x - 1 and si == 0 and k < 4 and sk == (k + 1) % 4:
                    return True
            if (x, sx) == (0, reach_x):
                if (si, sk) == (i - 1, k):
                    return True
                if i == 0 and si == count_x - 1 and k < 4 and sk == (k - 1) % 4:
                    return True
        if si == i and sx == x:
            if sk == k and (sj, sy, y) in ((j + 1, 0, reach_y), (j - 1, reach_y, 0)):
                return True
            if (j, y, sj, sy) == (0, 0, count_y - 1, reach_y) and (k, sk) in ((4, 0), (0, 5)):
                return True
            if (j, y, sj, sy) == (count_y - 1, reach_y, 0, 0) and (k, sk) in ((0, 4), (5, 0)):
                return True
        return False

    def row_of(y, x, k):
        if y == reach_y:
            return x * GROUPS + k
        if y == 0:
            return 32 + x * GROUPS + k
        return 64 + (k - 4) * 2 * ypad + (ypad if x else 0) + y

    copies = collections.defaultdict(list)
    for j in range(count_y):
        for i in range(count_x):
            for y in range(rows):
                for x in range(ACROSS):
                    if 0 < y < reach_y and 0 < x < reach_x:
                        continue
                    for k in range(GROUPS):
                        copies[canonical(j, i, y, x, k)].append((j, i, y, x, k))
    pairs = collections.defaultdict(list)
    for members in copies.values():
        for target in members:
            for source in members:
                if source != target and not swapped(source, target):
                    key = (source[1] * count_y + source[0], target[1] * count_y + target[0])
                    pairs[key].append((row_of(*source[2:]), row_of(*target[2:])))
    table = np.full((count_x * count_y, 8, ENTRIES), -1.0, np.float32)
    sent = collections.Counter()
    taken = collections.Counter()
    peers = count_x * count_y
    for (source, target), links in sorted(pairs.items()):
        assert len(links) <= RUNS * RUN_POINTS
        for slot, (row_from, row_to) in enumerate(sorted(links)):
            run, place = divmod(slot, RUN_POINTS)
            for device, peer, row, counts, base in (
                (source, target, row_from, sent, 0),
                (target, source, row_to, taken, 2),
            ):
                assert counts[device, place] < CLASS
                entry = place * CLASS + counts[device, place]
                counts[device, place] += 1
                table[device, base, entry] = run * peers + peer
                table[device, base + 1, entry] = row
    return table


bf16 = jnp.bfloat16


def parts_of(x):
    high = x.astype(bf16)
    rest = x - high.astype(jnp.float32)
    middle = rest.astype(bf16)
    return high, middle, (rest - middle.astype(jnp.float32)).astype(bf16)


def product(a, b, back=False):
    dims = (((1,), (1 if back else 0,)), ((), ()))
    return lax.dot_general(a, b, dims, preferred_element_type=jnp.float32)


def pick_right(x, chosen):
    count = x.shape[0]
    out = product(jnp.concatenate(parts_of(x), axis=0), chosen)
    return out[0:count] + out[count : 2 * count] + out[2 * count : 3 * count]


def pick_left(chosen, x):
    width = x.shape[1]
    out = product(chosen, jnp.concatenate(parts_of(x), axis=1))
    return out[:, 0:width] + out[:, width : 2 * width] + out[:, 2 * width : 3 * width]


def times(x, table, lanes, back=False):
    count = x.shape[0]
    high, middle, low = parts_of(x)
    out = product(jnp.concatenate([high, middle, low], axis=0), table[0, :, lanes], back)
    total = out[0:count] + (out[count : 2 * count] + out[2 * count : 3 * count])
    out = product(jnp.concatenate([high, middle], axis=0), table[1, :, lanes], back)
    total = total + (out[0:count] + out[count : 2 * count])
    return total


def turn_lanes(x, shift):
    shift = shift % x.shape[1]
    return pltpu.roll(x, shift, axis=1) if shift else x


def chosen_by(condition):
    return jnp.where(condition, 1.0, 0.0).astype(bf16)


def iota(shape, axis):
    return lax.broadcasted_iota(jnp.int32, shape, axis)


def put(ref, row, block):
    for t in range(ref.shape[0]):
        width = min(128, block.shape[1] - 128 * t)
        ref[t, row : row + block.shape[0], 0:width] = block[:, 128 * t : 128 * t + width]


def take(ref, c, first, count):
    tiles = [ref[t, pl.ds(4 * first + c, count, stride=4), :] for t in range(ref.shape[0])]
    return jnp.concatenate(tiles, axis=1)


def scatter(ref, c, block):
    for t in range(ref.shape[0]):
        ref[t, pl.ds(c, block.shape[0], stride=4), :] = block[:, 128 * t : 128 * t + 128]


def own_table(table_ref, count_y):
    return table_ref[lax.axis_index("xi") * count_y + lax.axis_index("eta")]


def force_kernel(
    rows,
    count_x,
    count_y,
    disp,
    vel,
    acc,
    metric,
    moduli,
    rho,
    pot,
    rate,
    accel,
    core_metric,
    kappa,
    core_rho,
    inner_disp,
    inner_vel,
    inner_acc,
    inner_metric,
    inner_moduli,
    inner_rho,
    table_ref,
    forward,
    plain_lanes,
    inner_forward,
    spread,
    lanes,
    columns,
    along_y,
    pick,
    polar,
    fields,
    send_xa,
    send_xb,
    send_ya,
    send_yb,
    send_all,
    wide,
    narrow,
    inner_rows,
    flux,
    inner_flux,
    wide_u,
    edges,
    rows_t,
    points,
    moved,
    scale,
    lame,
    core_scale,
    inner_moved,
    inner_scale,
    inner_lame,
    stack,
    shifted,
    copies,
    pot_next,
):
    ne = (rows - 1) // 4
    ypad = edges.shape[0] // 2
    half = 0.5 * time_step * time_step
    for y in range(rows):
        block = disp[y] + time_step * vel[y] + half * acc[y]
        put(moved, 4 * y, block)
        put(scale, 4 * y, metric[y])
        put(lame, 4 * y, moduli[y])
        put(core_scale, 4 * y, core_metric[y])
        block = inner_disp[y] + time_step * inner_vel[y] + half * inner_acc[y]
        put(inner_moved, 4 * y, block)
        put(inner_scale, 4 * y, inner_metric[y])
        put(inner_lame, 4 * y, inner_moduli[y])

    def part(ref, c, first=0, count=rows):
        width = WIDTH if ref.shape[0] * 128 == PAD else INNER_WIDTH
        return take(ref, c, first, count)[:, 0:width]

    pot_next[...] = pot[...] + time_step * rate[...] + half * accel[...]

    slope = along_y[0:5, 0:5]
    slope_back = along_y[8:13, 0:5]

    def along(matrix, block):
        total = matrix[:, 0:1] * block[0:1, :]
        for b in range(1, 5):
            total = total + matrix[:, b : b + 1] * block[b : b + 1, :]
        return total

    narrow[:, TILE:PAD] = jnp.zeros((narrow.shape[0], PAD - TILE), jnp.float32)
    inner_flux[:, 256:INNER_SLOPES] = jnp.zeros((inner_flux.shape[0], 2 * TAIL), jnp.float32)
    stack[...] = jnp.zeros(stack.shape, jnp.float32)
    fields[...] = jnp.zeros(fields.shape, jnp.float32)

    def slot(f, e):
        return (f * ne + e) * 8

    extras = [(scale, c) for c in range(3)] + [(lame, c) for c in range(2)] + [(core_scale, c) for c in range(3)]
    for e in range(ne):
        for f in range(4):
            block = part(moved, f, 4 * e, 5) if f < 3 else pot_next[4 * e : 4 * e + 5, :]
            wide[slot(f, e) : slot(f, e) + 5, :] = block
            narrow[slot(f, e) : slot(f, e) + 5, 0:WIDTH] = along(slope, block)
        for f, (ref, c) in enumerate(extras):
            narrow[slot(4 + f, e) : slot(4 + f, e) + 5, 0:WIDTH] = part(ref, c, 4 * e, 5)
        narrow[slot(12, e) : slot(12, e) + 5, 0:WIDTH] = core_rho[4 * e : 4 * e + 5, :]
        for f in range(3):
            inner_rows[slot(f, e) : slot(f, e) + 5, :] = part(inner_moved, f, 4 * e, 5)
    whole = slice(None)
    slopes_xr = times(wide[...], forward, whole)
    tail_x = slopes_xr[:, 2 * TILE : SLOPES]
    tail_r = pltpu.roll(tail_x, TAIL, axis=1)
    copies[...] = narrow[:, TILE:PAD] + pick_right(narrow[:, 0:WIDTH], plain_lanes[...])
    inner_xr = times(inner_rows[...], inner_forward, whole)
    inner_tail_x = inner_xr[:, 256:INNER_SLOPES]
    inner_tail_r = pltpu.roll(inner_tail_x, TAIL, axis=1)
    rest = INNER_WIDTH - 128

    def elastic(g, lam, mu, sy, sx, sr, jw):
        scaled = [[sy[i] * g[0], sx[i] * g[1], sr[i] * g[2]] for i in range(3)]
        trace = lam * (scaled[0][0] + scaled[1][1] + scaled[2][2])
        out = [[None] * 3 for _ in range(3)]
        weighted = [jw * g[m] for m in range(3)]
        for i in range(3):
            for m in range(3):
                if i == m:
                    stress = 2.0 * mu * scaled[i][i] + trace
                else:
                    stress = mu * (scaled[i][m] + scaled[m][i])
                out[i][m] = stress * weighted[m]
        return out

    row_weight = columns[0:5, 1:2]
    valid = (iota((5, PAD), 1) < NODES) & (iota((5, PAD), 0) < 5)
    for e in range(ne):
        def plain(f):
            at = slice(slot(f, e), slot(f, e) + 5)
            return jnp.concatenate([narrow[at, 0:TILE], copies[at, :]], axis=1)

        def x_of(f):
            at = slice(slot(f, e), slot(f, e) + 5)
            return jnp.concatenate([slopes_xr[at, 0:TILE], tail_x[at]], axis=1)

        def r_of(f):
            at = slice(slot(f, e), slot(f, e) + 5)
            return jnp.concatenate([slopes_xr[at, TILE : 2 * TILE], tail_r[at]], axis=1)

        node = row_weight * lanes[0:1, :]
        g = [jnp.where(valid, plain(4 + m), 1.0) for m in range(3)]
        q = elastic(
            g,
            plain(7),
            plain(8),
            [plain(f) for f in range(3)],
            [x_of(f) for f in range(3)],
            [r_of(f) for f in range(3)],
            node / (g[0] * g[1] * g[2]),
        )
        g = [jnp.where(valid, plain(9 + m), 1.0) for m in range(3)]
        volume = node / (g[0] * g[1] * g[2] * jnp.where(valid, plain(12), 1.0))
        q.append(
            [
                volume * g[0] * g[0] * plain(3),
                volume * g[1] * g[1] * x_of(3),
                volume * g[2] * g[2] * r_of(3),
            ]
        )
        for f in range(4):
            at = slot(f, e)
            flux[at : at + 5, 0:TILE] = q[f][1][:, 0:TILE]
            flux[at : at + 5, TILE : 2 * TILE] = q[f][2][:, 0:TILE]
            flux[at : at + 5, 2 * TILE : SLOPES] = jnp.where(
                iota((5, 2 * TAIL), 1) < TAIL, q[f][1][:, TILE:PAD], pltpu.roll(q[f][2][:, TILE:PAD], TAIL, axis=1)
            )
            flux[at : at + 5, SLOPES : SLOPES + PAD] = along(slope_back, q[f][0])

        def inner_x(f):
            at = slice(slot(f, e), slot(f, e) + 5)
            return jnp.concatenate([inner_xr[at, 0:128], inner_tail_x[at, 0:rest]], axis=1)

        def inner_r(f):
            at = slice(slot(f, e), slot(f, e) + 5)
            return jnp.concatenate([inner_xr[at, 128:256], inner_tail_r[at, 0:rest]], axis=1)

        g = [part(inner_scale, m, 4 * e, 5) for m in range(3)]
        node = row_weight * lanes[3:4, 0:INNER_WIDTH]
        q = elastic(
            g,
            part(inner_lame, 0, 4 * e, 5),
            part(inner_lame, 1, 4 * e, 5),
            [along(slope, inner_rows[slot(f, e) : slot(f, e) + 5, :]) for f in range(3)],
            [inner_x(f) for f in range(3)],
            [inner_r(f) for f in range(3)],
            node / (g[0] * g[1] * g[2]),
        )
        for f in range(3):
            at = slot(f, e)
            for m, first in ((1, 0), (2, 128)):
                inner_flux[at : at + 5, first : first + 128] = q[f][m][:, 0:128]
                tail = 256 + TAIL * (m - 1)
                inner_flux[at : at + 5, tail : tail + rest] = q[f][m][:, 128:INNER_WIDTH]
            inner_flux[at : at + 5, INNER_SLOPES : INNER_SLOPES + INNER_WIDTH] = along(slope_back, q[f][0])

    back = times(flux[:, 0:SLOPES], forward, whole, back=True)
    count = flux.shape[0]
    out = product(
        jnp.concatenate(parts_of(flux[:, SLOPES + TILE : SLOPES + PAD]), axis=0), plain_lanes[...], back=True
    )
    back = back + flux[:, SLOPES : SLOPES + WIDTH] + (out[0:count] + out[count : 2 * count] + out[2 * count : 3 * count])
    count = 3 * ne * 8
    stack[0:count, :] = (
        times(inner_flux[:, 0:INNER_SLOPES], inner_forward, whole, back=True)
        + inner_flux[:, INNER_SLOPES : INNER_SLOPES + INNER_WIDTH]
    )
    lumped_y = columns[0:rows, 0:1]
    stack[count : count + rows, :] = inner_rho[...] * (
        lumped_y * lanes[4:5, 0:INNER_WIDTH] / (part(inner_scale, 0) * part(inner_scale, 1) * part(inner_scale, 2))
    )
    stack[count + ypad : count + ypad + rows, :] = part(inner_moved, 2)
    spreads = pick_right(stack[...], spread[...])
    inner_forces = spreads[0:count, 0:WIDTH]
    for e in range(ne):
        here = slice(4 * e, 4 * e + 5)
        for f in range(3):
            fields[f, here, 0:WIDTH] = fields[f, here, 0:WIDTH] - back[slot(f, e) : slot(f, e) + 5, :]
            fields[IF + f, here, 0:WIDTH] = fields[IF + f, here, 0:WIDTH] - inner_forces[slot(f, e) : slot(f, e) + 5, :]
        fields[CF, here, 0:WIDTH] = fields[CF, here, 0:WIDTH] - back[slot(3, e) : slot(3, e) + 5, :]

    lumped = lumped_y * lanes[1:2, 0:WIDTH]
    fields[MM, 0:rows, 0:WIDTH] = rho[...] * (lumped / (part(scale, 0) * part(scale, 1) * part(scale, 2)))
    fields[CM, 0:rows, 0:WIDTH] = lumped / (part(core_scale, 0) * part(core_scale, 1) * part(core_scale, 2)) / kappa[...]
    fields[IM, 0:rows, :] = spreads[count : count + rows]
    radial = lax.rem(iota((rows, WIDTH), 1), RADIAL)
    face = lumped_y * lanes[2:3, 0:WIDTH] / (part(core_scale, 0) * part(core_scale, 1))
    face = jnp.where((radial == 0) | (radial == RADIAL - 1), face, 0.0)
    fields[CW, 0:rows, 0:WIDTH] = face
    wide_u[...] = jnp.zeros(wide_u.shape, jnp.float32)
    wide_u[0:rows, 0:WIDTH] = part(moved, 2)
    above = pltpu.roll(wide_u[...], RADIAL - 1, axis=1)
    below = pltpu.roll(spreads[count + ypad : count + 2 * ypad], PAD - (INNER_RADIAL - 1), axis=1)
    radial = lax.rem(iota((ypad, PAD), 1), RADIAL)
    jump = jnp.where(radial == RADIAL - 1, above, jnp.where(radial == 0, -below, 0.0))
    fields[CF] = fields[CF] + fields[CW] * jump

    low = iota((ypad, 128), 1) < 64
    for p in range(PAIRS):
        left = fields[2 * p]
        right = fields[2 * p + 1] if 2 * p + 1 < FIELDS else jnp.zeros_like(left)
        edges[0:ypad, p * 128 : p * 128 + 128] = jnp.where(low, left[:, 0:128], pltpu.roll(right[:, 0:128], 64, axis=1))
        edges[ypad : 2 * ypad, p * 128 : p * 128 + 128] = jnp.where(
            low,
            pltpu.roll(left, PAD - (WIDTH - COLUMN), axis=1)[:, 0:128],
            pltpu.roll(right, PAD + 64 - (WIDTH - COLUMN), axis=1)[:, 0:128],
        )
    even_x = lax.rem(lax.axis_index("xi"), 2) == 0
    even_y = lax.rem(lax.axis_index("eta"), 2) == 0
    for p in range(PAIRS):
        first = edges[0:rows, p * 128 : p * 128 + 128]
        last = edges[ypad : ypad + rows, p * 128 : p * 128 + 128]
        send_xa[p * rows : (p + 1) * rows, :] = jnp.where(even_x, last, first)
        send_xb[p * rows : (p + 1) * rows, :] = jnp.where(even_x, first, last)
    rows_t[0:16, :] = jnp.zeros((16, PAD), jnp.float32)
    rows_t[64:80, :] = jnp.zeros((16, PAD), jnp.float32)
    for f in range(FIELDS):
        rows_t[f : f + 1, :] = fields[f, rows - 1 : rows, :]
        rows_t[64 + f : 65 + f, :] = fields[f, 0:1, :]
    top = rows_t[0:16, :]
    bottom = rows_t[64:80, :]
    send_ya[...] = jnp.where(even_y, top, bottom)
    send_yb[...] = jnp.where(even_y, bottom, top)

    for at, block in ((0, top), (64, bottom)):
        for n, piece in enumerate(parts_of(block)):
            rows_t[at + 16 * n : at + 16 * n + 16, :] = piece.astype(jnp.float32)
    by_line = product(pick[...], rows_t[...].astype(bf16), back=True)
    by_line = by_line + (pltpu.roll(by_line, 128 - 16, axis=1) + pltpu.roll(by_line, 128 - 32, axis=1))
    lane = iota((32, 128), 1)
    top_points = jnp.zeros((32, 128), jnp.float32)
    bottom_points = jnp.zeros((32, 128), jnp.float32)
    for r in range(RADIAL):
        block = by_line[32 * r : 32 * r + 32, :]
        for first, end, at in runs_of(r):
            upper = jnp.where((lane >= first) & (lane < end), block, 0.0)
            lower = jnp.where((lane >= 64 + first) & (lane < 64 + end), block, 0.0)
            top_points = top_points + turn_lanes(upper, at - first)
            bottom_points = bottom_points + turn_lanes(lower, at - first - 64)
    points[0:32, :] = top_points
    points[32:64, :] = bottom_points
    third = lax.rem(iota((2 * ypad, 128), 1), 64)
    tiles = []
    for t in range(2):
        tile = jnp.zeros((2 * ypad, 128), jnp.float32)
        for j in range(3):
            p = 3 * t + j
            block = turn_lanes(edges[:, p * 128 : p * 128 + 128], 2 * RADIAL * j - 4 * RADIAL)
            tile = jnp.where((third >= 2 * RADIAL * j) & (third < 2 * RADIAL * (j + 1)), block, tile)
        tiles.append(tile)
    caps = pick_right(jnp.concatenate(tiles, axis=1), polar[...])
    points[64 : 64 + 2 * ypad, :] = caps[:, 0:128]
    points[64 + 2 * ypad : 64 + 4 * ypad, :] = caps[:, 128:256]

    own = own_table(table_ref, count_y)
    turned = jnp.transpose(own)
    count = points.shape[0]
    chosen = chosen_by(turned[:, 1:2] == iota((ENTRIES, count), 1).astype(jnp.float32))
    chosen = pick_left(chosen, points[...])
    shifted[...] = jnp.zeros(shifted.shape, jnp.float32)
    lane = iota((CLASS, 128), 1)
    for place in range(RUN_POINTS):
        tile, shift = divmod(place * CHANNELS, 128)
        here = slice(place * CLASS, (place + 1) * CLASS)
        block = turn_lanes(chosen[here], shift)
        shifted[here, tile * 128 : tile * 128 + 128] = jnp.where(lane >= shift, block, 0.0)
        if shift + CHANNELS > 128:
            shifted[here, tile * 128 + 128 : tile * 128 + 256] = jnp.where(lane < shift, block, 0.0)
    peers = count_x * count_y
    number = iota((RUNS * peers, ENTRIES), 0).astype(jnp.float32)
    placed = pick_left(chosen_by(own[0:1, :] == number), shifted[...])
    for row in range(BLOCK):
        run, tile = divmod(row, RUN_ROWS)
        if run < RUNS:
            block = placed[run * peers : (run + 1) * peers, tile * 128 : tile * 128 + 128]
        else:
            block = jnp.zeros((peers, 128), jnp.float32)
        send_all[pl.ds(row, peers, stride=BLOCK), :] = block


def window_kernel(
    disp,
    vel,
    acc,
    pot,
    rate,
    accel,
    inner_disp,
    inner_vel,
    inner_acc,
    fields,
    disp_next,
    pot_next,
    inner_next,
    vel_half,
    rate_half,
    inner_half,
    fields_out,
):
    half = 0.5 * time_step
    for new, between, place, speed, change in (
        (disp_next, vel_half, disp, vel, acc),
        (pot_next, rate_half, pot, rate, accel),
        (inner_next, inner_half, inner_disp, inner_vel, inner_acc),
    ):
        new[...] = place[...] + time_step * speed[...] + half * time_step * change[...]
        between[...] = speed[...] + half * change[...]
    fields_out[...] = fields[...]


def close_kernel(
    rows,
    count_x,
    count_y,
    got_xa,
    got_xb,
    got_ya,
    got_yb,
    got_all,
    fields,
    vel_half,
    rate_half,
    inner_half,
    table_ref,
    pick,
    polar_back,
    squeeze,
    vel_next,
    acc_next,
    rate_next,
    accel_next,
    inner_vel_next,
    inner_acc_next,
    total,
    by_line,
    caps,
    narrow,
    wide,
    runs,
    arrived,
):
    ypad = total.shape[1]
    narrow[...] = jnp.zeros(narrow.shape, jnp.float32)
    own = own_table(table_ref, count_y)
    turned = jnp.transpose(own)
    peers = count_x * count_y
    for run in range(RUNS):
        for tile in range(RUN_ROWS):
            runs[run * peers : (run + 1) * peers, tile * 128 : tile * 128 + 128] = got_all[
                pl.ds(run * RUN_ROWS + tile, peers, stride=BLOCK), :
            ]
    number = iota((ENTRIES, RUNS * peers), 1).astype(jnp.float32)
    shifted = pick_left(chosen_by(turned[:, 2:3] == number), runs[...])
    lane = iota((CLASS, 128), 1)
    arrived[...] = jnp.zeros(arrived.shape, jnp.float32)
    for place in range(RUN_POINTS):
        tile, shift = divmod(place * CHANNELS, 128)
        here = slice(place * CLASS, (place + 1) * CLASS)
        block = shifted[here, tile * 128 : tile * 128 + 128]
        if shift + CHANNELS > 128:
            block = jnp.where(lane >= shift, block, shifted[here, tile * 128 + 128 : tile * 128 + 256])
        arrived[here, :] = jnp.where(lane < CHANNELS, turn_lanes(block, -shift), 0.0)
    count = 64 + 4 * ypad
    points = pick_left(chosen_by(own[3:4, :] == iota((count, ENTRIES), 0).astype(jnp.float32)), arrived[...])
    lane = iota((32, 128), 1)
    upper = points[0:32]
    lower = points[32:64]
    for r in range(RADIAL):
        block = jnp.zeros((32, 128), jnp.float32)
        for first, end, at in runs_of(r):
            high = turn_lanes(upper, first - at)
            low = turn_lanes(lower, 64 + first - at)
            block = jnp.where((lane >= first) & (lane < end), high, block)
            block = jnp.where((lane >= 64 + first) & (lane < 64 + end), low, block)
        high, middle, last = (piece.astype(jnp.float32) for piece in parts_of(block))
        by_line[32 * r : 32 * r + 32, :] = (
            high + pltpu.roll(middle, 16, axis=1) + pltpu.roll(last, 32, axis=1)
        )
    lines = lax.dot_general(
        by_line[...].astype(bf16), pick[...], (((0,), (0,)), ((), ())), preferred_element_type=jnp.float32
    )
    lines_top = lines[0:16] + (lines[16:32] + lines[32:48])
    lines_bottom = lines[64:80] + (lines[80:96] + lines[96:112])
    caps[:, 0:128] = points[64 : 64 + 2 * ypad]
    caps[:, 128:256] = points[64 + 2 * ypad : 64 + 4 * ypad]
    columns = pick_right(caps[...], polar_back[...])

    xi = lax.axis_index("xi")
    eta = lax.axis_index("eta")
    even_x = lax.rem(xi, 2) == 0
    even_y = lax.rem(eta, 2) == 0
    lane = iota((16, PAD), 1)
    group = lax.rem(lane // RADIAL, GROUPS)
    used = lane < WIDTH
    ya = got_ya[...]
    yb = got_yb[...]
    from_above = jnp.where(even_y, ya, yb)
    from_below = jnp.where(even_y, yb, ya)
    four, five = 4 * RADIAL, 5 * RADIAL
    seam_top = jnp.where(
        group == 0,
        pltpu.roll(from_above, PAD - four, axis=1),
        jnp.where(group == 5, pltpu.roll(from_above, five, axis=1), 0.0),
    )
    seam_bottom = jnp.where(
        group == 4,
        pltpu.roll(from_below, four, axis=1),
        jnp.where(group == 0, pltpu.roll(from_below, PAD - five, axis=1), 0.0),
    )
    add_top = jnp.where(eta == count_y - 1, seam_top, from_above) + lines_top
    add_bottom = jnp.where(eta == 0, seam_bottom, from_below) + lines_bottom
    add_top = jnp.where(used, add_top, 0.0)
    add_bottom = jnp.where(used, add_bottom, 0.0)
    total[...] = fields[...]
    lane = iota((rows, 128), 1)
    inside = lax.rem(lane, 64)
    equator = inside < 4 * RADIAL
    keep = inside < COLUMN
    low = lane < 64
    last_x = xi == count_x - 1
    for p in range(PAIRS):
        xa = got_xa[p * rows : (p + 1) * rows, :]
        xb = got_xb[p * rows : (p + 1) * rows, :]
        from_right = jnp.where(even_x, xa, xb)
        from_left = jnp.where(even_x, xb, xa)
        up = jnp.where(
            inside < 3 * RADIAL,
            pltpu.roll(from_right, 128 - RADIAL, axis=1),
            pltpu.roll(from_right, 3 * RADIAL, axis=1),
        )
        down = jnp.where(
            inside < RADIAL,
            pltpu.roll(from_left, 128 - 3 * RADIAL, axis=1),
            pltpu.roll(from_left, RADIAL, axis=1),
        )
        from_right = jnp.where(last_x, jnp.where(equator, up, 0.0), from_right)
        from_left = jnp.where(xi == 0, jnp.where(equator, down, 0.0), from_left)
        at = slice(p * 128, p * 128 + 128)
        from_left = jnp.where(keep, from_left + columns[0:rows, at], 0.0)
        from_right = jnp.where(keep, from_right + columns[ypad : ypad + rows, at], 0.0)
        zero = jnp.zeros((rows, PAD - 128), jnp.float32)
        for h in range(2):
            f = 2 * p + h
            if f >= FIELDS:
                continue
            mine = low if h == 0 else ~low
            left = jnp.where(mine, from_left, 0.0)
            right = jnp.where(mine, from_right, 0.0)
            if h:
                left = pltpu.roll(left, 64, axis=1)
            total[f, 0:rows, 0:128] = total[f, 0:rows, 0:128] + left
            right = jnp.concatenate([right, zero], axis=1)
            right = pltpu.roll(right, WIDTH - COLUMN - 64 * h, axis=1)
            total[f, 0:rows, :] = total[f, 0:rows, :] + right
    for f in range(FIELDS):
        total[f, rows - 1 : rows, :] = total[f, rows - 1 : rows, :] + add_top[f : f + 1, :]
        total[f, 0:1, :] = total[f, 0:1, :] + add_bottom[f : f + 1, :]

    half = 0.5 * time_step
    lane = iota((ypad, PAD), 1)
    radial = lax.rem(lane, RADIAL)
    inside = (lane < WIDTH) & (iota((ypad, PAD), 0) < rows)
    core = total[CF] / jnp.where(inside, total[CM], 1.0)
    accel_next[...] = core[0:rows, 0:WIDTH]
    rate_next[...] = rate_half[...] + half * core[0:rows, 0:WIDTH]
    push = total[CW] * core
    top = jnp.where(radial == 0, pltpu.roll(push, PAD - (RADIAL - 1), axis=1), 0.0)
    bottom = jnp.where(radial == INNER_RADIAL - 1, pltpu.roll(push, INNER_RADIAL - 1, axis=1), 0.0)
    mass = jnp.where(inside, total[MM], 1.0)
    inner_mass = jnp.where(inside & (radial < INNER_RADIAL), total[IM], 1.0)
    for f in range(3):
        force = total[f] + top if f == 2 else total[f]
        result = (force / mass)[0:rows]
        scatter(wide, f, result)
        force = total[IF + f] - bottom if f == 2 else total[IF + f]
        scatter(narrow, f, (force / inner_mass)[0:rows])
    squeezed = pick_right(jnp.concatenate([narrow[t] for t in range(PAD // 128)], axis=1), squeeze[...])
    for y in range(rows):
        result = jnp.concatenate([wide[t, 4 * y : 4 * y + 3, :] for t in range(PAD // 128)], axis=1)[:, 0:WIDTH]
        acc_next[y] = result
        vel_next[y] = vel_half[y] + half * result
        result = squeezed[4 * y : 4 * y + 3, :]
        inner_acc_next[y] = result
        inner_vel_next[y] = inner_half[y] + half * result


def shards(
    count_x,
    count_y,
    mantle_disp,
    mantle_vel,
    mantle_acc,
    mantle_metric,
    mantle_moduli,
    mantle_rho,
    core_pot,
    core_rate,
    core_accel,
    core_metric,
    core_kappa,
    core_rho,
    inner_disp,
    inner_vel,
    inner_acc,
    inner_metric,
    inner_moduli,
    inner_rho,
):
    rows = mantle_disp.shape[1]
    turn = lambda a: jnp.transpose(a, (1, 0, 2))
    mantle_disp, mantle_vel, mantle_acc = turn(mantle_disp), turn(mantle_vel), turn(mantle_acc)
    mantle_metric, mantle_moduli, core_metric = turn(mantle_metric), turn(mantle_moduli), turn(core_metric)
    inner_disp, inner_vel, inner_acc = turn(inner_disp), turn(inner_vel), turn(inner_acc)
    inner_metric, inner_moduli = turn(inner_metric), turn(inner_moduli)
    ne = (rows - 1) // 4
    ypad = -(-rows // 8) * 8
    tables = {name: jnp.asarray(value) for name, value in constants(rows).items()}
    table = jnp.asarray(exchange_tables(count_x, count_y, rows))
    f32 = jnp.float32
    like = lambda a: jax.ShapeDtypeStruct(a.shape, f32)
    shape = lambda *s: jax.ShapeDtypeStruct(s, f32)
    devices = count_x * count_y
    edge = -(-PAIRS * rows // 8) * 8
    (fields, xa, xb, ya, yb, everyone) = pl.pallas_call(
        functools.partial(force_kernel, rows, count_x, count_y),
        out_shape=[
            shape(FIELDS, ypad, PAD),
            shape(edge, 128),
            shape(edge, 128),
            shape(16, PAD),
            shape(16, PAD),
            shape(devices * BLOCK, 128),
        ],
        scratch_shapes=[
            pltpu.VMEM((4 * ne * 8, WIDTH), f32),
            pltpu.VMEM((13 * ne * 8, PAD), f32),
            pltpu.VMEM((3 * ne * 8, INNER_WIDTH), f32),
            pltpu.VMEM((4 * ne * 8, SLOPES + PAD), f32),
            pltpu.VMEM((3 * ne * 8, INNER_SLOPES + INNER_PAD), f32),
            pltpu.VMEM((ypad, PAD), f32),
            pltpu.VMEM((2 * ypad, PAIRS * 128), f32),
            pltpu.VMEM((128, PAD), f32),
            pltpu.VMEM((64 + 4 * ypad, 128), f32),
        ]
        + [pltpu.VMEM((PAD // 128, 4 * rows, 128), f32)] * 4
        + [pltpu.VMEM((INNER_PAD // 128, 4 * rows, 128), f32)] * 3
        + [pltpu.VMEM((3 * ne * 8 + 2 * ypad, INNER_WIDTH), f32)]
        + [pltpu.VMEM((ENTRIES, RUN_ROWS * 128), f32)]
        + [pltpu.VMEM((13 * ne * 8, PAD - TILE), f32)]
        + [pltpu.VMEM((rows, WIDTH), f32)],
        name="forces",
    )(
        mantle_disp,
        mantle_vel,
        mantle_acc,
        mantle_metric,
        mantle_moduli,
        mantle_rho,
        core_pot,
        core_rate,
        core_accel,
        core_metric,
        core_kappa,
        core_rho,
        inner_disp,
        inner_vel,
        inner_acc,
        inner_metric,
        inner_moduli,
        inner_rho,
        table,
        tables["table"],
        tables["plain"],
        tables["inner_table"],
        tables["spread"],
        tables["lanes"],
        tables["columns"],
        tables["along_y"],
        tables["pick"],
        tables["polar"],
    )
    everyone = lax.all_to_all(everyone, ("xi", "eta"), 0, 0, tiled=True)
    near = [(i, i ^ 1) for i in range(count_x)]
    far = [(i, (i - 1 if i % 2 == 0 else i + 1) % count_x) for i in range(count_x)]
    xa = lax.ppermute(xa, "xi", near)
    xb = lax.ppermute(xb, "xi", far)
    near = [(j, j ^ 1) for j in range(count_y)]
    far = [(j, (j - 1 if j % 2 == 0 else j + 1) % count_y) for j in range(count_y)]
    ya = lax.ppermute(ya, "eta", near)
    yb = lax.ppermute(yb, "eta", far)
    (mantle_next, core_next, inner_next, vel_half, rate_half, inner_half, fields) = pl.pallas_call(
        window_kernel,
        out_shape=[like(a) for a in (mantle_disp, core_pot, inner_disp) * 2] + [like(fields)],
        compiler_params=pltpu.CompilerParams(vmem_limit_bytes=WINDOW_GRANT),
        name="window",
    )(mantle_disp, mantle_vel, mantle_acc, core_pot, core_rate, core_accel, inner_disp, inner_vel, inner_acc, fields)
    (mantle_vel_next, mantle_acc_next, core_rate_next, core_acc_next, inner_vel_next, inner_acc_next) = pl.pallas_call(
        functools.partial(close_kernel, rows, count_x, count_y),
        out_shape=[
            like(mantle_vel),
            like(mantle_acc),
            like(core_rate),
            like(core_accel),
            like(inner_vel),
            like(inner_acc),
        ],
        scratch_shapes=[
            pltpu.VMEM((FIELDS, ypad, PAD), f32),
            pltpu.VMEM((RADIAL * 32, 128), f32),
            pltpu.VMEM((2 * ypad, 256), f32),
            pltpu.VMEM((PAD // 128, -(-4 * rows // 16) * 16, 128), f32),
            pltpu.VMEM((PAD // 128, 4 * rows, 128), f32),
            pltpu.VMEM((RUNS * devices, RUN_ROWS * 128), f32),
            pltpu.VMEM((ENTRIES, 128), f32),
        ],
        compiler_params=pltpu.CompilerParams(vmem_limit_bytes=(8 << 20) + devices * (48 << 10)),
        name="close",
    )(
        xa,
        xb,
        ya,
        yb,
        everyone,
        fields,
        vel_half,
        rate_half,
        inner_half,
        table,
        tables["pick"],
        tables["polar_back"],
        tables["squeeze"],
    )
    return (
        turn(mantle_next),
        turn(mantle_vel_next),
        turn(mantle_acc_next),
        core_next,
        core_rate_next,
        core_acc_next,
        turn(inner_next),
        turn(inner_vel_next),
        turn(inner_acc_next),
    )


def solution(mesh):
    count_x, count_y = mesh.shape["xi"], mesh.shape["eta"]
    assert count_x % 2 == 0 and count_y % 2 == 0
    assert (count_x * count_y) % 8 == 0
    vector, scalar = P(None, "eta", "xi"), P("eta", "xi")
    placed = (vector,) * 5 + (scalar,) * 4 + (vector,) + (scalar,) * 2 + (vector,) * 5 + (scalar,)
    return jax.shard_map(
        functools.partial(shards, count_x, count_y),
        mesh=mesh,
        in_specs=placed,
        out_specs=(vector,) * 3 + (scalar,) * 3 + (vector,) * 3,
        check_vma=False,
    )
```
